128 devices in a mesh: slab: 32 (over y, z_hi, x), coil: 4 (over z_lo, core).
Axes of the slice: x: 4, y: 4, z: 4 (z_hi: 2, z_lo: 2; z = z_hi * 2 + z_lo), core: 2. Of those that a mesh axis runs over, the one named last changes fastest.
Arguments:
- image: float32 [256, 2, 32, 384], P(('slab', 'coil')), may hold values from -6 to 6
- noise: float32 [256, 2, 32, 384], P(('slab', 'coil')), may hold values from -1.2 to 1.2
- sens: bfloat16 [16, 2, 32, 384, 256], P('coil', None, 'slab'), may hold values from -1 to 1
- measured: bfloat16 [16, 2, 32, 384, 256], P('coil', None, 'slab'), may hold values from -3 to 3
- mask: int32 [384, 256], replicated, may hold values 0 or 1
- w_first: bfloat16 [3, 3, 10, 128], replicated, may hold values from -0.625 to 0.625
- b_first: float32 [128], replicated, may hold values from -3 to 3
- w_second: bfloat16 [128, 128], replicated, may hold values from -0.5 to 0.5
- b_second: float32 [128], replicated, may hold values from -3 to 3
- w_third: bfloat16 [128, 128], replicated, may hold values from -0.5 to 0.5
- b_third: float32 [128], replicated, may hold values from -3 to 3
- w_last: bfloat16 [3, 3, 2, 128], replicated, may hold values from -0.1875 to 0.1875
Outputs:
- updated: float32 [256, 2, 32, 384], P(('slab', 'coil'))
The draws below stay inside these ranges and needn't reach their ends.
Inputs may be any that keep to these rules, and one draw needn't show every extreme that they name: `mask`: 1 where the (ky, kz) line was measured, else 0.
All inputs are finite; a program needn't handle non-finite values.
Results may differ from the reference program's by a relative error of at most 0.0035.
Values may be sent and summed in bfloat16 or wider, within the bound.
A program may use at most 256 MiB of HBM per device.

```python
import jax
import jax.numpy as jnp
from jax import lax

NY = 384
COILS = 16
WIDTH = 128
XW = 32
NZ = 256


def place_ends(entries, rng, low, high):
    longest = entries.shape.index(max(entries.shape))
    spots = []
    for shift in (0, 1):
        where = [jax.random.randint(jax.random.fold_in(rng, axis), (), 0, length) for axis, length in enumerate(entries.shape)]
        where[longest] = (where[longest] + shift) % entries.shape[longest]
        spots.append(tuple(where))
    return entries.at[spots[0]].set(low).at[spots[1]].set(high)


def steps_of(stream_key, extent, pieces, low, high):
    def one(axis_at, shards_of):
        draws = jax.random.uniform(jax.random.fold_in(jax.random.fold_in(stream_key, 6), axis_at), (shards_of,), jnp.float32, low / len(pieces), high / len(pieces))
        return jnp.repeat(jnp.exp(draws), extent[axis_at] // shards_of).reshape((-1,) + (1,) * (len(extent) - axis_at - 1))

    factor_of = one(*pieces[0])
    for cut in pieces[1:]:
        factor_of = factor_of * one(*cut)
    return factor_of


def scatter_about(own_key, extent, spread, bound, cuts=(), held_as=jnp.bfloat16):
    loudness = steps_of(own_key, extent, cuts, -0.22, 0.18) if cuts else 1.0
    values = jax.random.normal(own_key, extent, jnp.float32) * spread * loudness
    return jnp.minimum(jnp.maximum(values, -bound), bound).astype(held_as)


def setup_inputs(seed: int = 0) -> dict:
    streams_of = jax.random.split(jax.random.key(seed), 13)
    image = scatter_about(streams_of[0], (NZ, 2, XW, NY), 1.0, 6.0, ((0, 128),), jnp.float32)
    noise = scatter_about(streams_of[1], (NZ, 2, XW, NY), 0.2, 1.2, ((0, 128),), jnp.float32)
    sens = scatter_about(streams_of[2], (COILS, 2, XW, NY, NZ), 0.18, 1.0, ((0, 4), (2, 32)))
    measured = scatter_about(streams_of[3], (COILS, 2, XW, NY, NZ), 0.5, 3.0, ((0, 4), (2, 32)))
    mask = place_ends((jax.random.randint(streams_of[4], (NY, NZ), 0, 3) < 1).astype(jnp.int32), jax.random.fold_in(streams_of[4], 1), 0, 1)
    w_first = scatter_about(streams_of[5], (3, 3, 10, WIDTH), 90 ** -0.5, 0.625)
    b_first = scatter_about(streams_of[6], (WIDTH,), 0.5, 3.0, (), jnp.float32)
    w_second = scatter_about(streams_of[7], (WIDTH, WIDTH), WIDTH ** -0.5, 0.5)
    b_second = scatter_about(streams_of[8], (WIDTH,), 0.5, 3.0, (), jnp.float32)
    w_third = scatter_about(streams_of[9], (WIDTH, WIDTH), WIDTH ** -0.5, 0.5)
    b_third = scatter_about(streams_of[10], (WIDTH,), 0.5, 3.0, (), jnp.float32)
    w_last = scatter_about(streams_of[11], (3, 3, 2, WIDTH), (9 * WIDTH) ** -0.5, 0.1875)
    return dict(image=image, noise=noise, sens=sens, measured=measured, mask=mask, w_first=w_first, b_first=b_first, w_second=w_second, b_second=b_second, w_third=w_third, b_third=b_third, w_last=w_last)


STEP_SIZE = 0.5
HIGHEST_MODE = lax.Precision.HIGHEST

def dft_tables(length):
    line_index = jnp.arange(length, dtype=jnp.int32)
    phase_turns = line_index[:, None] * line_index[None, :] % length
    phase_angle = phase_turns.astype(jnp.float32) * (2.0 * jnp.pi / length)
    norm_scale = 1.0 / jnp.sqrt(jnp.float32(length))
    return ((jnp.cos(phase_angle) * norm_scale).astype(jnp.bfloat16), (jnp.sin(phase_angle) * norm_scale).astype(jnp.bfloat16))

def widen(values):
    return lax.optimization_barrier(values).astype(jnp.float32)

def along_y(values, table):
    return jnp.einsum('...yz,yk->...kz', widen(values), widen(table), precision=HIGHEST_MODE)

def along_z(values, table):
    return jnp.einsum('...z,zk->...k', widen(values), widen(table), precision=HIGHEST_MODE)

def spectrum(real_part, imag_part, cos_y, sin_y, cos_z, sin_z, forward):
    sign = 1.0 if forward else -1.0
    out_real = (along_y(real_part, cos_y) + sign * along_y(imag_part, sin_y)).astype(jnp.bfloat16)
    out_imag = (along_y(imag_part, cos_y) - sign * along_y(real_part, sin_y)).astype(jnp.bfloat16)
    last_real = along_z(out_real, cos_z) + sign * along_z(out_imag, sin_z)
    last_imag = along_z(out_imag, cos_z) - sign * along_z(out_real, sin_z)
    return (last_real, last_imag)

def coil_adjoint(planes, coil_sens, coil_data, sampled, tables_all):
    cos_y, sin_y, cos_z, sin_z = tables_all
    sens_real = coil_sens[..., 0, :, :, :].astype(jnp.float32)
    sens_imag = coil_sens[..., 1, :, :, :].astype(jnp.float32)
    image_real = planes[0]
    image_imag = planes[1]
    coil_real = (sens_real * image_real - sens_imag * image_imag).astype(jnp.bfloat16)
    coil_imag = (sens_real * image_imag + sens_imag * image_real).astype(jnp.bfloat16)
    spec_real, spec_imag = spectrum(coil_real, coil_imag, cos_y, sin_y, cos_z, sin_z, True)
    miss_real = (sampled * (spec_real - coil_data[..., 0, :, :, :].astype(jnp.float32))).astype(jnp.bfloat16)
    miss_imag = (sampled * (spec_imag - coil_data[..., 1, :, :, :].astype(jnp.float32))).astype(jnp.bfloat16)
    back_real, back_imag = spectrum(miss_real, miss_imag, cos_y, sin_y, cos_z, sin_z, False)
    return (sens_real * back_real + sens_imag * back_imag, sens_real * back_imag - sens_imag * back_real)

def score_net(window, w_first, b_first, w_second, b_second, w_third, b_third, w_last):
    slice_count = window.shape[0] - 4
    row_count = window.shape[2]
    col_count = window.shape[3]
    stacked = jnp.concatenate([window[offset:offset + slice_count] for offset in range(5)], axis=1)
    framed = jnp.pad(stacked, ((0, 0), (0, 0), (1, 1), (1, 1))).astype(jnp.float32)
    first_sum = jnp.zeros((slice_count, row_count, col_count, w_first.shape[-1]), jnp.float32)
    for shift_x in range(3):
        for shift_y in range(3):
            first_sum = first_sum + jnp.einsum('zcxy,ck->zxyk', framed[:, :, shift_x:shift_x + row_count, shift_y:shift_y + col_count], w_first[shift_x, shift_y].astype(jnp.float32))
    hidden = jax.nn.silu(first_sum + b_first).astype(jnp.bfloat16)
    hidden = jax.nn.silu(jnp.einsum('zxyk,kj->zxyj', hidden.astype(jnp.float32), w_second.astype(jnp.float32)) + b_second).astype(jnp.bfloat16)
    hidden = jax.nn.silu(jnp.einsum('zxyk,kj->zxyj', hidden.astype(jnp.float32), w_third.astype(jnp.float32)) + b_third).astype(jnp.bfloat16)
    framed = jnp.pad(hidden, ((0, 0), (1, 1), (1, 1), (0, 0))).astype(jnp.float32)
    score_field = jnp.zeros((slice_count, 2, row_count, col_count), jnp.float32)
    for shift_x in range(3):
        for shift_y in range(3):
            score_field = score_field + jnp.einsum('zxyk,ok->zoxy', framed[:, shift_x:shift_x + row_count, shift_y:shift_y + col_count], w_last[shift_x, shift_y].astype(jnp.float32))
    return score_field

def reference(image, noise, sens, measured, mask, w_first, b_first, w_second, b_second, w_third, b_third, w_last):
    padded = jnp.pad(image.astype(jnp.bfloat16), ((2, 2), (0, 0), (0, 0), (0, 0)))

    def one_slice(slice_index):
        window = lax.dynamic_slice_in_dim(padded, slice_index, 5, 0)
        return score_net(window, w_first, b_first, w_second, b_second, w_third, b_third, w_last)[0]
    score_field = lax.map(one_slice, jnp.arange(NZ, dtype=jnp.int32))
    planes = jnp.transpose(image, (1, 2, 3, 0))
    cos_y, sin_y = dft_tables(NY)
    cos_z, sin_z = dft_tables(NZ)
    sampled = mask.astype(jnp.float32)

    def add_coil(running_sum, pair):
        part_real, part_imag = coil_adjoint(planes, pair[0], pair[1], sampled, (cos_y, sin_y, cos_z, sin_z))
        return (running_sum + jnp.stack([part_real, part_imag]), None)
    start_sum = jnp.zeros(planes.shape, jnp.float32)
    gradient, _ = lax.scan(add_coil, start_sum, (sens, measured))
    gradient = jnp.transpose(gradient, (3, 0, 1, 2))
    return image + STEP_SIZE * (score_field - gradient) + noise
```

```python
import jax
import jax.numpy as jnp
from jax import lax
from jax.sharding import PartitionSpec as P
from jax.experimental import pallas as pl
from jax.experimental.pallas import tpu as pltpu

STEP_SIZE = 0.5


def with_halo(shard, sides, width):
    for axis, dim in sides:
        devices, length = (lax.axis_size(axis), shard.shape[dim])
        up = [(i, (i + 1) % devices) for i in range(devices - 1)]
        down = [(j, i) for i, j in up]
        last = lax.slice_in_dim(shard, length - width, length, axis=dim)
        first = lax.slice_in_dim(shard, 0, width, axis=dim)
        before = lax.ppermute(last, axis, up)
        after = lax.ppermute(first, axis, down)
        shard = jnp.concatenate([before, shard, after], axis=dim)
    return shard


def dft_tables(length):
    line_index = jnp.arange(length, dtype=jnp.int32)
    phase_turns = line_index[:, None] * line_index[None, :] % length
    phase_angle = phase_turns.astype(jnp.float32) * (2.0 * jnp.pi / length)
    norm_scale = 1.0 / jnp.sqrt(jnp.float32(length))
    return (
        (jnp.cos(phase_angle) * norm_scale).astype(jnp.bfloat16),
        (jnp.sin(phase_angle) * norm_scale).astype(jnp.bfloat16),
    )


def along_y(values, table):
    return jnp.einsum("...yz,yk->...kz", values, table, preferred_element_type=jnp.float32)


def along_z(values, table):
    return jnp.einsum("...z,zk->...k", values, table, preferred_element_type=jnp.float32)


def spectrum(real_part, imag_part, cos_y, sin_y, cos_z, sin_z, forward):
    sign = 1.0 if forward else -1.0
    out_real = (along_y(real_part, cos_y) + sign * along_y(imag_part, sin_y)).astype(jnp.bfloat16)
    out_imag = (along_y(imag_part, cos_y) - sign * along_y(real_part, sin_y)).astype(jnp.bfloat16)
    last_real = along_z(out_real, cos_z) + sign * along_z(out_imag, sin_z)
    last_imag = along_z(out_imag, cos_z) - sign * along_z(out_real, sin_z)
    return (last_real, last_imag)


def coil_adjoint(planes, sens, measured, mask):
    cos_y, sin_y = dft_tables(planes.shape[2])
    cos_z, sin_z = dft_tables(planes.shape[3])
    sampled = mask.astype(jnp.float32)
    sens_real = sens[:, 0].astype(jnp.float32)
    sens_imag = sens[:, 1].astype(jnp.float32)
    image_real = planes[0]
    image_imag = planes[1]
    coil_real = (sens_real * image_real - sens_imag * image_imag).astype(jnp.bfloat16)
    coil_imag = (sens_real * image_imag + sens_imag * image_real).astype(jnp.bfloat16)
    spec_real, spec_imag = spectrum(coil_real, coil_imag, cos_y, sin_y, cos_z, sin_z, True)
    miss_real = (sampled * (spec_real - measured[:, 0].astype(jnp.float32))).astype(jnp.bfloat16)
    miss_imag = (sampled * (spec_imag - measured[:, 1].astype(jnp.float32))).astype(jnp.bfloat16)
    back_real, back_imag = spectrum(miss_real, miss_imag, cos_y, sin_y, cos_z, sin_z, False)
    total_real = jnp.sum(sens_real * back_real + sens_imag * back_imag, axis=0)
    total_imag = jnp.sum(sens_real * back_imag - sens_imag * back_real, axis=0)
    return jnp.stack([total_real, total_imag])


def net_kernel(x_ref, w1_ref, b1_ref, w2_ref, b2_ref, w3_ref, b3_ref, wl_ref, q_ref):
    h = jnp.dot(w1_ref[...], x_ref[0], preferred_element_type=jnp.float32) + b1_ref[...]
    h = jax.nn.silu(h).astype(jnp.bfloat16)
    h = jnp.dot(w2_ref[...], h, preferred_element_type=jnp.float32) + b2_ref[...]
    h = jax.nn.silu(h).astype(jnp.bfloat16)
    h = jnp.dot(w3_ref[...], h, preferred_element_type=jnp.float32) + b3_ref[...]
    h = jax.nn.silu(h).astype(jnp.bfloat16)
    q = jnp.dot(wl_ref[...], h, preferred_element_type=jnp.float32)
    cols = q_ref.shape[3]
    for row in range(q_ref.shape[1]):
        q_ref[0, row] = q[:, row * cols : (row + 1) * cols]


def score_net(window, w_first, b_first, w_second, b_second, w_third, b_third, w_last):
    slice_count = window.shape[0] - 4
    row_count = window.shape[2]
    col_count = window.shape[3]
    width = w_first.shape[-1]
    pixels = row_count * col_count
    stacked = jnp.concatenate(
        [window[offset : offset + slice_count] for offset in range(5)], axis=1
    )
    framed = jnp.pad(stacked, ((0, 0), (0, 0), (1, 1), (1, 1)))
    columns = jnp.concatenate(
        [
            framed[:, :, shift_x : shift_x + row_count, shift_y : shift_y + col_count]
            for shift_x in range(3)
            for shift_y in range(3)
        ],
        axis=1,
    ).reshape(slice_count, -1, pixels)
    taps_in = columns.shape[1]
    w1 = w_first.reshape(taps_in, width).T
    wl = w_last.reshape(-1, width)
    outs = wl.shape[0]
    chunk = 1536
    full = lambda z, n: (0, 0)
    q = pl.pallas_call(
        net_kernel,
        grid=(slice_count, pixels // chunk),
        in_specs=[
            pl.BlockSpec((1, taps_in, chunk), lambda z, n: (z, 0, n)),
            pl.BlockSpec((width, taps_in), full),
            pl.BlockSpec((width, 1), full),
            pl.BlockSpec((width, width), full),
            pl.BlockSpec((width, 1), full),
            pl.BlockSpec((width, width), full),
            pl.BlockSpec((width, 1), full),
            pl.BlockSpec((outs, width), full),
        ],
        out_specs=pl.BlockSpec((1, chunk // col_count, outs, col_count), lambda z, n: (z, n, 0, 0)),
        out_shape=jax.ShapeDtypeStruct((slice_count, row_count, outs, col_count), jnp.float32),
    )(
        columns,
        w1,
        b_first.reshape(width, 1),
        w_second.T,
        b_second.reshape(width, 1),
        w_third.T,
        b_third.reshape(width, 1),
        wl,
    )
    q = jnp.pad(q, ((0, 0), (1, 1), (0, 0), (1, 1)))
    score_field = jnp.zeros((slice_count, row_count, 2, col_count), jnp.float32)
    for shift_x in range(3):
        for shift_y in range(3):
            tap = (shift_x * 3 + shift_y) * 2
            score_field = score_field + q[
                :, shift_x : shift_x + row_count, tap : tap + 2, shift_y : shift_y + col_count
            ]
    score_field = jnp.transpose(score_field, (0, 2, 1, 3))
    return score_field


def slab_slices(image):
    return lax.all_gather(image, "coil", axis=0, tiled=True)


def on_device(
    image,
    noise,
    sens,
    measured,
    mask,
    w_first,
    b_first,
    w_second,
    b_second,
    w_third,
    b_third,
    w_last,
):
    window = with_halo(image.astype(jnp.bfloat16), ((("slab", "coil"), 0),), 2)
    score_field = score_net(window, w_first, b_first, w_second, b_second, w_third, b_third, w_last)
    planes_in = lax.all_to_all(slab_slices(image), "slab", split_axis=2, concat_axis=0, tiled=True)
    planes = jnp.transpose(planes_in, (1, 2, 3, 0))
    partial_sum = coil_adjoint(planes, sens, measured, mask)
    by_depth = jnp.transpose(partial_sum, (3, 0, 1, 2))
    slab_part = lax.all_to_all(
        by_depth.astype(jnp.bfloat16), "slab", split_axis=0, concat_axis=2, tiled=True
    ).astype(by_depth.dtype)
    gradient = lax.psum_scatter(
        slab_part.astype(jnp.bfloat16), "coil", scatter_dimension=0, tiled=True
    ).astype(jnp.float32)
    return image + STEP_SIZE * (score_field - gradient) + noise


def solution(mesh):
    in_specs = (
        P(("slab", "coil"), None, None, None),
        P(("slab", "coil"), None, None, None),
        P("coil", None, "slab", None, None),
        P("coil", None, "slab", None, None),
        P(),
        P(),
        P(),
        P(),
        P(),
        P(),
        P(),
        P(),
    )
    out_specs = P(("slab", "coil"), None, None, None)
    return jax.shard_map(
        on_device, mesh=mesh, in_specs=in_specs, out_specs=out_specs, check_vma=False
    )
```

```python
import jax
import jax.numpy as jnp
from jax import lax
from jax.sharding import PartitionSpec as P
from jax.experimental import pallas as pl
from jax.experimental.pallas import tpu as pltpu

STEP_SIZE = 0.5


def with_halo(shard, sides, width):
    for axis, dim in sides:
        devices, length = (lax.axis_size(axis), shard.shape[dim])
        up = [(i, (i + 1) % devices) for i in range(devices - 1)]
        down = [(j, i) for i, j in up]
        last = lax.slice_in_dim(shard, length - width, length, axis=dim)
        first = lax.slice_in_dim(shard, 0, width, axis=dim)
        before = lax.ppermute(last, axis, up)
        after = lax.ppermute(first, axis, down)
        shard = jnp.concatenate([before, shard, after], axis=dim)
    return shard


def dft_tables(length):
    line_index = jnp.arange(length, dtype=jnp.int32)
    phase_turns = line_index[:, None] * line_index[None, :] % length
    phase_angle = phase_turns.astype(jnp.float32) * (2.0 * jnp.pi / length)
    norm_scale = 1.0 / jnp.sqrt(jnp.float32(length))
    return (
        (jnp.cos(phase_angle) * norm_scale).astype(jnp.bfloat16),
        (jnp.sin(phase_angle) * norm_scale).astype(jnp.bfloat16),
    )


def along_y(values, table):
    return jnp.einsum("...yz,yk->...kz", values, table, preferred_element_type=jnp.float32)


def along_z(values, table):
    return jnp.einsum("...z,zk->...k", values, table, preferred_element_type=jnp.float32)


def spectrum(real_part, imag_part, cos_y, sin_y, cos_z, sin_z, forward):
    sign = 1.0 if forward else -1.0
    out_real = (along_y(real_part, cos_y) + sign * along_y(imag_part, sin_y)).astype(jnp.bfloat16)
    out_imag = (along_y(imag_part, cos_y) - sign * along_y(real_part, sin_y)).astype(jnp.bfloat16)
    last_real = along_z(out_real, cos_z) + sign * along_z(out_imag, sin_z)
    last_imag = along_z(out_imag, cos_z) - sign * along_z(out_real, sin_z)
    return (last_real, last_imag)


def adjoint_kernel(planes_ref, sens_ref, meas_ref, mask_ref, ty_ref, tz_ref, out_ref):
    ny = planes_ref.shape[1]
    nz = planes_ref.shape[2]

    @pl.when(pl.program_id(0) == 0)
    def _():
        out_ref[...] = jnp.zeros_like(out_ref)

    ty = ty_ref[...]
    tz = tz_ref[...]
    sens_real = sens_ref[0].astype(jnp.float32)
    sens_imag = sens_ref[1].astype(jnp.float32)
    image_real = planes_ref[0]
    image_imag = planes_ref[1]
    coil_real = (sens_real * image_real - sens_imag * image_imag).astype(jnp.bfloat16)
    coil_imag = (sens_real * image_imag + sens_imag * image_real).astype(jnp.bfloat16)
    half = jnp.dot(ty, jnp.concatenate([coil_real, coil_imag], axis=1), preferred_element_type=jnp.float32)
    half_real = (half[:ny, :nz] + half[ny:, nz:]).astype(jnp.bfloat16)
    half_imag = (half[:ny, nz:] - half[ny:, :nz]).astype(jnp.bfloat16)
    full = jnp.dot(jnp.concatenate([half_real, half_imag], axis=0), tz, preferred_element_type=jnp.float32)
    spec_real = full[:ny, :nz] + full[ny:, nz:]
    spec_imag = full[ny:, :nz] - full[:ny, nz:]
    sampled = mask_ref[...].astype(jnp.float32)
    miss_real = (sampled * (spec_real - meas_ref[0].astype(jnp.float32))).astype(jnp.bfloat16)
    miss_imag = (sampled * (spec_imag - meas_ref[1].astype(jnp.float32))).astype(jnp.bfloat16)
    half = jnp.dot(ty, jnp.concatenate([miss_real, miss_imag], axis=1), preferred_element_type=jnp.float32)
    back_real = (half[:ny, :nz] - half[ny:, nz:]).astype(jnp.bfloat16)
    back_imag = (half[:ny, nz:] + half[ny:, :nz]).astype(jnp.bfloat16)
    full = jnp.dot(jnp.concatenate([back_real, back_imag], axis=0), tz, preferred_element_type=jnp.float32)
    grad_real = full[:ny, :nz] - full[ny:, nz:]
    grad_imag = full[ny:, :nz] + full[:ny, nz:]
    out_ref[0] += sens_real * grad_real + sens_imag * grad_imag
    out_ref[1] += sens_real * grad_imag - sens_imag * grad_real


def coil_adjoint(planes, sens, measured, mask):
    ny = planes.shape[2]
    nz = planes.shape[3]
    cos_y, sin_y = dft_tables(ny)
    cos_z, sin_z = dft_tables(nz)
    ty = jnp.concatenate([cos_y, sin_y], axis=0)
    tz = jnp.concatenate([cos_z, sin_z], axis=1)
    coils = sens.shape[0]
    return pl.pallas_call(
        adjoint_kernel,
        grid=(coils,),
        in_specs=[
            pl.BlockSpec((2, None, ny, nz), lambda c: (0, 0, 0, 0)),
            pl.BlockSpec((None, 2, None, ny, nz), lambda c: (c, 0, 0, 0, 0)),
            pl.BlockSpec((None, 2, None, ny, nz), lambda c: (c, 0, 0, 0, 0)),
            pl.BlockSpec((ny, nz), lambda c: (0, 0)),
            pl.BlockSpec((2 * ny, ny), lambda c: (0, 0)),
            pl.BlockSpec((nz, 2 * nz), lambda c: (0, 0)),
        ],
        out_specs=pl.BlockSpec((2, None, ny, nz), lambda c: (0, 0, 0, 0)),
        out_shape=jax.ShapeDtypeStruct(planes.shape, jnp.float32),
    )(planes, sens, measured, mask, ty, tz)


def net_kernel(x_ref, w1_ref, b1_ref, w2_ref, b2_ref, w3_ref, b3_ref, wl_ref, q_ref):
    h = jnp.dot(w1_ref[...], x_ref[0], preferred_element_type=jnp.float32) + b1_ref[...]
    h = jax.nn.silu(h).astype(jnp.bfloat16)
    h = jnp.dot(w2_ref[...], h, preferred_element_type=jnp.float32) + b2_ref[...]
    h = jax.nn.silu(h).astype(jnp.bfloat16)
    h = jnp.dot(w3_ref[...], h, preferred_element_type=jnp.float32) + b3_ref[...]
    h = jax.nn.silu(h).astype(jnp.bfloat16)
    q = jnp.dot(wl_ref[...], h, preferred_element_type=jnp.float32)
    cols = q_ref.shape[3]
    for row in range(q_ref.shape[1]):
        q_ref[0, row] = q[:, row * cols : (row + 1) * cols]


def score_net(window, w_first, b_first, w_second, b_second, w_third, b_third, w_last):
    slice_count = window.shape[0] - 4
    row_count = window.shape[2]
    col_count = window.shape[3]
    width = w_first.shape[-1]
    pixels = row_count * col_count
    stacked = jnp.concatenate(
        [window[offset : offset + slice_count] for offset in range(5)], axis=1
    )
    framed = jnp.pad(stacked, ((0, 0), (0, 0), (1, 1), (1, 1)))
    columns = jnp.concatenate(
        [
            framed[:, :, shift_x : shift_x + row_count, shift_y : shift_y + col_count]
            for shift_x in range(3)
            for shift_y in range(3)
        ],
        axis=1,
    ).reshape(slice_count, -1, pixels)
    taps_in = columns.shape[1]
    w1 = w_first.reshape(taps_in, width).T
    wl = w_last.reshape(-1, width)
    outs = wl.shape[0]
    chunk = 1536
    full = lambda z, n: (0, 0)
    q = pl.pallas_call(
        net_kernel,
        grid=(slice_count, pixels // chunk),
        in_specs=[
            pl.BlockSpec((1, taps_in, chunk), lambda z, n: (z, 0, n)),
            pl.BlockSpec((width, taps_in), full),
            pl.BlockSpec((width, 1), full),
            pl.BlockSpec((width, width), full),
            pl.BlockSpec((width, 1), full),
            pl.BlockSpec((width, width), full),
            pl.BlockSpec((width, 1), full),
            pl.BlockSpec((outs, width), full),
        ],
        out_specs=pl.BlockSpec((1, chunk // col_count, outs, col_count), lambda z, n: (z, n, 0, 0)),
        out_shape=jax.ShapeDtypeStruct((slice_count, row_count, outs, col_count), jnp.float32),
    )(
        columns,
        w1,
        b_first.reshape(width, 1),
        w_second.T,
        b_second.reshape(width, 1),
        w_third.T,
        b_third.reshape(width, 1),
        wl,
    )
    q = jnp.pad(q, ((0, 0), (1, 1), (0, 0), (1, 1)))
    score_field = jnp.zeros((slice_count, row_count, 2, col_count), jnp.float32)
    for shift_x in range(3):
        for shift_y in range(3):
            tap = (shift_x * 3 + shift_y) * 2
            score_field = score_field + q[
                :, shift_x : shift_x + row_count, tap : tap + 2, shift_y : shift_y + col_count
            ]
    score_field = jnp.transpose(score_field, (0, 2, 1, 3))
    return score_field


def slab_slices(image):
    return lax.all_gather(image, "coil", axis=0, tiled=True)


def on_device(
    image,
    noise,
    sens,
    measured,
    mask,
    w_first,
    b_first,
    w_second,
    b_second,
    w_third,
    b_third,
    w_last,
):
    window = with_halo(image.astype(jnp.bfloat16), ((("slab", "coil"), 0),), 2)
    score_field = score_net(window, w_first, b_first, w_second, b_second, w_third, b_third, w_last)
    planes_in = lax.all_to_all(slab_slices(image), "slab", split_axis=2, concat_axis=0, tiled=True)
    planes = jnp.transpose(planes_in, (1, 2, 3, 0))
    partial_sum = coil_adjoint(planes, sens, measured, mask)
    by_depth = jnp.transpose(partial_sum, (3, 0, 1, 2))
    slab_part = lax.all_to_all(
        by_depth.astype(jnp.bfloat16), "slab", split_axis=0, concat_axis=2, tiled=True
    ).astype(by_depth.dtype)
    gradient = lax.psum_scatter(
        slab_part.astype(jnp.bfloat16), "coil", scatter_dimension=0, tiled=True
    ).astype(jnp.float32)
    return image + STEP_SIZE * (score_field - gradient) + noise


def solution(mesh):
    in_specs = (
        P(("slab", "coil"), None, None, None),
        P(("slab", "coil"), None, None, None),
        P("coil", None, "slab", None, None),
        P("coil", None, "slab", None, None),
        P(),
        P(),
        P(),
        P(),
        P(),
        P(),
        P(),
        P(),
    )
    out_specs = P(("slab", "coil"), None, None, None)
    return jax.shard_map(
        on_device, mesh=mesh, in_specs=in_specs, out_specs=out_specs, check_vma=False
    )
```

```python
import jax
import jax.numpy as jnp
from jax import lax
from jax.sharding import PartitionSpec as P
from jax.experimental import pallas as pl
from jax.experimental.pallas import tpu as pltpu

STEP_SIZE = 0.5


def with_halo(shard, sides, width):
    for axis, dim in sides:
        devices, length = (lax.axis_size(axis), shard.shape[dim])
        up = [(i, (i + 1) % devices) for i in range(devices - 1)]
        down = [(j, i) for i, j in up]
        last = lax.slice_in_dim(shard, length - width, length, axis=dim)
        first = lax.slice_in_dim(shard, 0, width, axis=dim)
        before = lax.ppermute(last, axis, up)
        after = lax.ppermute(first, axis, down)
        shard = jnp.concatenate([before, shard, after], axis=dim)
    return shard


def dft_tables(length):
    line_index = jnp.arange(length, dtype=jnp.int32)
    phase_turns = line_index[:, None] * line_index[None, :] % length
    phase_angle = phase_turns.astype(jnp.float32) * (2.0 * jnp.pi / length)
    norm_scale = 1.0 / jnp.sqrt(jnp.float32(length))
    return (
        (jnp.cos(phase_angle) * norm_scale).astype(jnp.bfloat16),
        (jnp.sin(phase_angle) * norm_scale).astype(jnp.bfloat16),
    )


def along_y(values, table):
    return jnp.einsum("...yz,yk->...kz", values, table, preferred_element_type=jnp.float32)


def along_z(values, table):
    return jnp.einsum("...z,zk->...k", values, table, preferred_element_type=jnp.float32)


def spectrum(real_part, imag_part, cos_y, sin_y, cos_z, sin_z, forward):
    sign = 1.0 if forward else -1.0
    out_real = (along_y(real_part, cos_y) + sign * along_y(imag_part, sin_y)).astype(jnp.bfloat16)
    out_imag = (along_y(imag_part, cos_y) - sign * along_y(real_part, sin_y)).astype(jnp.bfloat16)
    last_real = along_z(out_real, cos_z) + sign * along_z(out_imag, sin_z)
    last_imag = along_z(out_imag, cos_z) - sign * along_z(out_real, sin_z)
    return (last_real, last_imag)


def adjoint_kernel(planes_ref, sens_ref, meas_ref, mask_ref, ty_ref, tz_ref, out_ref):
    ny = planes_ref.shape[1]
    nz = planes_ref.shape[2]

    @pl.when(pl.program_id(0) == 0)
    def _():
        out_ref[...] = jnp.zeros_like(out_ref)

    ty = ty_ref[...]
    tz = tz_ref[...]
    sens_real = sens_ref[0].astype(jnp.float32)
    sens_imag = sens_ref[1].astype(jnp.float32)
    image_real = planes_ref[0]
    image_imag = planes_ref[1]
    coil_real = (sens_real * image_real - sens_imag * image_imag).astype(jnp.bfloat16)
    coil_imag = (sens_real * image_imag + sens_imag * image_real).astype(jnp.bfloat16)
    half = jnp.dot(ty, jnp.concatenate([coil_real, coil_imag], axis=1), preferred_element_type=jnp.float32)
    half_real = (half[:ny, :nz] + half[ny:, nz:]).astype(jnp.bfloat16)
    half_imag = (half[:ny, nz:] - half[ny:, :nz]).astype(jnp.bfloat16)
    full = jnp.dot(jnp.concatenate([half_real, half_imag], axis=0), tz, preferred_element_type=jnp.float32)
    spec_real = full[:ny, :nz] + full[ny:, nz:]
    spec_imag = full[ny:, :nz] - full[:ny, nz:]
    sampled = mask_ref[...].astype(jnp.float32)
    miss_real = (sampled * (spec_real - meas_ref[0].astype(jnp.float32))).astype(jnp.bfloat16)
    miss_imag = (sampled * (spec_imag - meas_ref[1].astype(jnp.float32))).astype(jnp.bfloat16)
    half = jnp.dot(ty, jnp.concatenate([miss_real, miss_imag], axis=1), preferred_element_type=jnp.float32)
    back_real = (half[:ny, :nz] - half[ny:, nz:]).astype(jnp.bfloat16)
    back_imag = (half[:ny, nz:] + half[ny:, :nz]).astype(jnp.bfloat16)
    full = jnp.dot(jnp.concatenate([back_real, back_imag], axis=0), tz, preferred_element_type=jnp.float32)
    grad_real = full[:ny, :nz] - full[ny:, nz:]
    grad_imag = full[ny:, :nz] + full[:ny, nz:]
    out_ref[0] += sens_real * grad_real + sens_imag * grad_imag
    out_ref[1] += sens_real * grad_imag - sens_imag * grad_real


def coil_adjoint(planes, sens, measured, mask):
    ny = planes.shape[2]
    nz = planes.shape[3]
    cos_y, sin_y = dft_tables(ny)
    cos_z, sin_z = dft_tables(nz)
    ty = jnp.concatenate([cos_y, sin_y], axis=0)
    tz = jnp.concatenate([cos_z, sin_z], axis=1)
    coils = sens.shape[0]
    return pl.pallas_call(
        adjoint_kernel,
        grid=(coils,),
        in_specs=[
            pl.BlockSpec((2, None, ny, nz), lambda c: (0, 0, 0, 0)),
            pl.BlockSpec((None, 2, None, ny, nz), lambda c: (c, 0, 0, 0, 0)),
            pl.BlockSpec((None, 2, None, ny, nz), lambda c: (c, 0, 0, 0, 0)),
            pl.BlockSpec((ny, nz), lambda c: (0, 0)),
            pl.BlockSpec((2 * ny, ny), lambda c: (0, 0)),
            pl.BlockSpec((nz, 2 * nz), lambda c: (0, 0)),
        ],
        out_specs=pl.BlockSpec((2, None, ny, nz), lambda c: (0, 0, 0, 0)),
        out_shape=jax.ShapeDtypeStruct(planes.shape, jnp.float32),
    )(planes, sens, measured, mask, ty, tz)


def net_kernel(x_ref, w1_ref, b1_ref, w2_ref, b2_ref, w3_ref, b3_ref, wl_ref, q_ref):
    h = jnp.dot(w1_ref[...], x_ref[0], preferred_element_type=jnp.float32) + b1_ref[...]
    h = jax.nn.silu(h).astype(jnp.bfloat16)
    h = jnp.dot(w2_ref[...], h, preferred_element_type=jnp.float32) + b2_ref[...]
    h = jax.nn.silu(h).astype(jnp.bfloat16)
    h = jnp.dot(w3_ref[...], h, preferred_element_type=jnp.float32) + b3_ref[...]
    h = jax.nn.silu(h).astype(jnp.bfloat16)
    q = jnp.dot(wl_ref[...], h, preferred_element_type=jnp.float32)
    cols = q_ref.shape[3]
    for row in range(q_ref.shape[1]):
        q_ref[0, row] = q[:, row * cols : (row + 1) * cols]


def score_net(window, w_first, b_first, w_second, b_second, w_third, b_third, w_last):
    slice_count = window.shape[0] - 4
    row_count = window.shape[2]
    col_count = window.shape[3]
    width = w_first.shape[-1]
    pixels = row_count * col_count
    stacked = jnp.concatenate(
        [window[offset : offset + slice_count] for offset in range(5)], axis=1
    )
    framed = jnp.pad(stacked, ((0, 0), (0, 0), (1, 1), (1, 1)))
    columns = jnp.concatenate(
        [
            framed[:, :, shift_x : shift_x + row_count, shift_y : shift_y + col_count]
            for shift_x in range(3)
            for shift_y in range(3)
        ],
        axis=1,
    ).reshape(slice_count, -1, pixels)
    taps_in = columns.shape[1]
    w1 = w_first.reshape(taps_in, width).T
    wl = w_last.reshape(-1, width)
    outs = wl.shape[0]
    chunk = 1536
    full = lambda z, n: (0, 0)
    q = pl.pallas_call(
        net_kernel,
        grid=(slice_count, pixels // chunk),
        in_specs=[
            pl.BlockSpec((1, taps_in, chunk), lambda z, n: (z, 0, n)),
            pl.BlockSpec((width, taps_in), full),
            pl.BlockSpec((width, 1), full),
            pl.BlockSpec((width, width), full),
            pl.BlockSpec((width, 1), full),
            pl.BlockSpec((width, width), full),
            pl.BlockSpec((width, 1), full),
            pl.BlockSpec((outs, width), full),
        ],
        out_specs=pl.BlockSpec((1, chunk // col_count, outs, col_count), lambda z, n: (z, n, 0, 0)),
        out_shape=jax.ShapeDtypeStruct((slice_count, row_count, outs, col_count), jnp.float32),
    )(
        columns,
        w1,
        b_first.reshape(width, 1),
        w_second.T,
        b_second.reshape(width, 1),
        w_third.T,
        b_third.reshape(width, 1),
        wl,
    )
    q = jnp.pad(q, ((0, 0), (1, 1), (0, 0), (1, 1)))
    score_field = jnp.zeros((slice_count, row_count, 2, col_count), jnp.float32)
    for shift_x in range(3):
        for shift_y in range(3):
            tap = (shift_x * 3 + shift_y) * 2
            score_field = score_field + q[
                :, shift_x : shift_x + row_count, tap : tap + 2, shift_y : shift_y + col_count
            ]
    score_field = jnp.transpose(score_field, (0, 2, 1, 3))
    return score_field


def slab_slices(image):
    return lax.all_gather(image, "coil", axis=0, tiled=True)


def on_device(
    image,
    noise,
    sens,
    measured,
    mask,
    w_first,
    b_first,
    w_second,
    b_second,
    w_third,
    b_third,
    w_last,
):
    window = with_halo(image.astype(jnp.bfloat16), ((("slab", "coil"), 0),), 2)
    score_field = score_net(window, w_first, b_first, w_second, b_second, w_third, b_third, w_last)
    slabs = lax.axis_size("slab")
    groups = lax.axis_size("coil")
    depth, parts, _, lines = image.shape
    sent = lax.all_to_all(image, "slab", split_axis=2, concat_axis=0, tiled=True)
    gathered = lax.all_gather(sent, "coil", axis=0, tiled=False)
    gathered = gathered.reshape(groups, slabs, depth, parts, 1, lines)
    planes = jnp.transpose(gathered, (3, 4, 5, 1, 0, 2)).reshape(parts, 1, lines, -1)
    partial_sum = coil_adjoint(planes, sens, measured, mask).astype(jnp.bfloat16)
    partial_sum = partial_sum.reshape(parts, 1, lines, slabs, groups, depth)
    by_group = jnp.transpose(partial_sum, (4, 3, 5, 0, 1, 2)).reshape(-1, parts, 1, lines)
    group_sum = lax.psum_scatter(by_group, "coil", scatter_dimension=0, tiled=True)
    gradient = lax.all_to_all(
        group_sum, "slab", split_axis=0, concat_axis=2, tiled=True
    ).astype(jnp.float32)
    return image + STEP_SIZE * (score_field - gradient) + noise


def solution(mesh):
    in_specs = (
        P(("slab", "coil"), None, None, None),
        P(("slab", "coil"), None, None, None),
        P("coil", None, "slab", None, None),
        P("coil", None, "slab", None, None),
        P(),
        P(),
        P(),
        P(),
        P(),
        P(),
        P(),
        P(),
    )
    out_specs = P(("slab", "coil"), None, None, None)
    return jax.shard_map(
        on_device, mesh=mesh, in_specs=in_specs, out_specs=out_specs, check_vma=False
    )
```

```python
import jax
import jax.numpy as jnp
from jax import lax
from jax.sharding import PartitionSpec as P
from jax.experimental import pallas as pl
from jax.experimental.pallas import tpu as pltpu

STEP_SIZE = 0.5


def with_halo(shard, sides, width):
    for axis, dim in sides:
        devices, length = (lax.axis_size(axis), shard.shape[dim])
        up = [(i, (i + 1) % devices) for i in range(devices - 1)]
        down = [(j, i) for i, j in up]
        last = lax.slice_in_dim(shard, length - width, length, axis=dim)
        first = lax.slice_in_dim(shard, 0, width, axis=dim)
        before = lax.ppermute(last, axis, up)
        after = lax.ppermute(first, axis, down)
        shard = jnp.concatenate([before, shard, after], axis=dim)
    return shard


def dft_tables(length):
    line_index = jnp.arange(length, dtype=jnp.int32)
    phase_turns = line_index[:, None] * line_index[None, :] % length
    phase_angle = phase_turns.astype(jnp.float32) * (2.0 * jnp.pi / length)
    norm_scale = 1.0 / jnp.sqrt(jnp.float32(length))
    return (
        (jnp.cos(phase_angle) * norm_scale).astype(jnp.bfloat16),
        (jnp.sin(phase_angle) * norm_scale).astype(jnp.bfloat16),
    )


def along_y(values, table):
    return jnp.einsum("...yz,yk->...kz", values, table, preferred_element_type=jnp.float32)


def along_z(values, table):
    return jnp.einsum("...z,zk->...k", values, table, preferred_element_type=jnp.float32)


def spectrum(real_part, imag_part, cos_y, sin_y, cos_z, sin_z, forward):
    sign = 1.0 if forward else -1.0
    out_real = (along_y(real_part, cos_y) + sign * along_y(imag_part, sin_y)).astype(jnp.bfloat16)
    out_imag = (along_y(imag_part, cos_y) - sign * along_y(real_part, sin_y)).astype(jnp.bfloat16)
    last_real = along_z(out_real, cos_z) + sign * along_z(out_imag, sin_z)
    last_imag = along_z(out_imag, cos_z) - sign * along_z(out_real, sin_z)
    return (last_real, last_imag)


def adjoint_kernel(planes_ref, sens_ref, meas_ref, mask_ref, ty_ref, tz_ref, out_ref):
    ny = planes_ref.shape[1]
    nz = planes_ref.shape[2]

    @pl.when(pl.program_id(0) == 0)
    def _():
        out_ref[...] = jnp.zeros_like(out_ref)

    ty = ty_ref[...]
    tz = tz_ref[...]
    sens_real = sens_ref[0].astype(jnp.float32)
    sens_imag = sens_ref[1].astype(jnp.float32)
    image_real = planes_ref[0]
    image_imag = planes_ref[1]
    coil_real = (sens_real * image_real - sens_imag * image_imag).astype(jnp.bfloat16)
    coil_imag = (sens_real * image_imag + sens_imag * image_real).astype(jnp.bfloat16)
    half = jnp.dot(ty, jnp.concatenate([coil_real, coil_imag], axis=1), preferred_element_type=jnp.float32)
    half_real = (half[:ny, :nz] + half[ny:, nz:]).astype(jnp.bfloat16)
    half_imag = (half[:ny, nz:] - half[ny:, :nz]).astype(jnp.bfloat16)
    full = jnp.dot(jnp.concatenate([half_real, half_imag], axis=0), tz, preferred_element_type=jnp.float32)
    spec_real = full[:ny, :nz] + full[ny:, nz:]
    spec_imag = full[ny:, :nz] - full[:ny, nz:]
    sampled = mask_ref[...].astype(jnp.float32)
    miss_real = (sampled * (spec_real - meas_ref[0].astype(jnp.float32))).astype(jnp.bfloat16)
    miss_imag = (sampled * (spec_imag - meas_ref[1].astype(jnp.float32))).astype(jnp.bfloat16)
    half = jnp.dot(ty, jnp.concatenate([miss_real, miss_imag], axis=1), preferred_element_type=jnp.float32)
    back_real = (half[:ny, :nz] - half[ny:, nz:]).astype(jnp.bfloat16)
    back_imag = (half[:ny, nz:] + half[ny:, :nz]).astype(jnp.bfloat16)
    full = jnp.dot(jnp.concatenate([back_real, back_imag], axis=0), tz, preferred_element_type=jnp.float32)
    grad_real = full[:ny, :nz] - full[ny:, nz:]
    grad_imag = full[ny:, :nz] + full[:ny, nz:]
    out_ref[0] += sens_real * grad_real + sens_imag * grad_imag
    out_ref[1] += sens_real * grad_imag - sens_imag * grad_real


def coil_adjoint(planes, sens, measured, mask):
    ny = planes.shape[2]
    nz = planes.shape[3]
    cos_y, sin_y = dft_tables(ny)
    cos_z, sin_z = dft_tables(nz)
    ty = jnp.concatenate([cos_y, sin_y], axis=0)
    tz = jnp.concatenate([cos_z, sin_z], axis=1)
    coils = sens.shape[0]
    return pl.pallas_call(
        adjoint_kernel,
        grid=(coils,),
        in_specs=[
            pl.BlockSpec((2, None, ny, nz), lambda c: (0, 0, 0, 0)),
            pl.BlockSpec((None, 2, None, ny, nz), lambda c: (c, 0, 0, 0, 0)),
            pl.BlockSpec((None, 2, None, ny, nz), lambda c: (c, 0, 0, 0, 0)),
            pl.BlockSpec((ny, nz), lambda c: (0, 0)),
            pl.BlockSpec((2 * ny, ny), lambda c: (0, 0)),
            pl.BlockSpec((nz, 2 * nz), lambda c: (0, 0)),
        ],
        out_specs=pl.BlockSpec((2, None, ny, nz), lambda c: (0, 0, 0, 0)),
        out_shape=jax.ShapeDtypeStruct(planes.shape, jnp.float32),
    )(planes, sens, measured, mask, ty, tz)


def net_kernel(x_ref, w1_ref, b1_ref, w2_ref, b2_ref, w3_ref, b3_ref, wl_ref, q_ref):
    h = jnp.dot(w1_ref[...], x_ref[0], preferred_element_type=jnp.float32) + b1_ref[...]
    h = jax.nn.silu(h).astype(jnp.bfloat16)
    h = jnp.dot(w2_ref[...], h, preferred_element_type=jnp.float32) + b2_ref[...]
    h = jax.nn.silu(h).astype(jnp.bfloat16)
    h = jnp.dot(w3_ref[...], h, preferred_element_type=jnp.float32) + b3_ref[...]
    h = jax.nn.silu(h).astype(jnp.bfloat16)
    q = jnp.dot(wl_ref[...], h, preferred_element_type=jnp.float32)
    cols = q_ref.shape[3]
    for row in range(q_ref.shape[1]):
        q_ref[0, row] = q[:, row * cols : (row + 1) * cols]


def score_net(window, w_first, b_first, w_second, b_second, w_third, b_third, w_last):
    slice_count = window.shape[0] - 4
    row_count = window.shape[2]
    col_count = window.shape[3]
    width = w_first.shape[-1]
    pixels = row_count * col_count
    stacked = jnp.concatenate(
        [window[offset : offset + slice_count] for offset in range(5)], axis=1
    )
    framed = jnp.pad(stacked, ((0, 0), (0, 0), (1, 1), (1, 1)))
    columns = jnp.concatenate(
        [
            framed[:, :, shift_x : shift_x + row_count, shift_y : shift_y + col_count]
            for shift_x in range(3)
            for shift_y in range(3)
        ],
        axis=1,
    ).reshape(slice_count, -1, pixels)
    taps_in = columns.shape[1]
    w1 = w_first.reshape(taps_in, width).T
    wl = w_last.reshape(-1, width)
    outs = wl.shape[0]
    chunk = 1536
    full = lambda z, n: (0, 0)
    q = pl.pallas_call(
        net_kernel,
        grid=(slice_count, pixels // chunk),
        in_specs=[
            pl.BlockSpec((1, taps_in, chunk), lambda z, n: (z, 0, n)),
            pl.BlockSpec((width, taps_in), full),
            pl.BlockSpec((width, 1), full),
            pl.BlockSpec((width, width), full),
            pl.BlockSpec((width, 1), full),
            pl.BlockSpec((width, width), full),
            pl.BlockSpec((width, 1), full),
            pl.BlockSpec((outs, width), full),
        ],
        out_specs=pl.BlockSpec((1, chunk // col_count, outs, col_count), lambda z, n: (z, n, 0, 0)),
        out_shape=jax.ShapeDtypeStruct((slice_count, row_count, outs, col_count), jnp.float32),
    )(
        columns,
        w1,
        b_first.reshape(width, 1),
        w_second.T,
        b_second.reshape(width, 1),
        w_third.T,
        b_third.reshape(width, 1),
        wl,
    )
    q = jnp.pad(q, ((0, 0), (1, 1), (0, 0), (1, 1)))
    score_field = jnp.zeros((slice_count, row_count, 2, col_count), jnp.float32)
    for shift_x in range(3):
        for shift_y in range(3):
            tap = (shift_x * 3 + shift_y) * 2
            score_field = score_field + q[
                :, shift_x : shift_x + row_count, tap : tap + 2, shift_y : shift_y + col_count
            ]
    score_field = jnp.transpose(score_field, (0, 2, 1, 3))
    return score_field


def slab_slices(image):
    return lax.all_gather(image, "coil", axis=0, tiled=True)


def on_device(
    image,
    noise,
    sens,
    measured,
    mask,
    w_first,
    b_first,
    w_second,
    b_second,
    w_third,
    b_third,
    w_last,
):
    window = with_halo(image.astype(jnp.bfloat16), ((("slab", "coil"), 0),), 2)
    score_field = score_net(window, w_first, b_first, w_second, b_second, w_third, b_third, w_last)
    slabs = lax.axis_size("slab")
    groups = lax.axis_size("coil")
    depth, parts, _, lines = image.shape
    sent = lax.all_to_all(image, "slab", split_axis=2, concat_axis=0, tiled=True)
    gathered = lax.all_gather(sent, "coil", axis=0, tiled=False)
    gathered = gathered.reshape(groups, slabs, depth, parts, 1, lines)
    planes = jnp.transpose(gathered, (3, 4, 5, 1, 0, 2)).reshape(parts, 1, lines, -1)
    partial_sum = coil_adjoint(planes, sens, measured, mask)
    by_depth = jnp.transpose(partial_sum, (3, 0, 1, 2)).astype(jnp.bfloat16)
    slab_part = lax.all_to_all(by_depth, "slab", split_axis=0, concat_axis=2, tiled=True)
    gradient = lax.psum_scatter(
        slab_part, "coil", scatter_dimension=0, tiled=True
    ).astype(jnp.float32)
    return image + STEP_SIZE * (score_field - gradient) + noise


def solution(mesh):
    in_specs = (
        P(("slab", "coil"), None, None, None),
        P(("slab", "coil"), None, None, None),
        P("coil", None, "slab", None, None),
        P("coil", None, "slab", None, None),
        P(),
        P(),
        P(),
        P(),
        P(),
        P(),
        P(),
        P(),
    )
    out_specs = P(("slab", "coil"), None, None, None)
    return jax.shard_map(
        on_device, mesh=mesh, in_specs=in_specs, out_specs=out_specs, check_vma=False
    )
```

```python
import jax
import jax.numpy as jnp
from jax import lax
from jax.sharding import PartitionSpec as P
from jax.experimental import pallas as pl
from jax.experimental.pallas import tpu as pltpu

STEP_SIZE = 0.5


def with_halo(shard, sides, width):
    for axis, dim in sides:
        devices, length = (lax.axis_size(axis), shard.shape[dim])
        up = [(i, (i + 1) % devices) for i in range(devices - 1)]
        down = [(j, i) for i, j in up]
        last = lax.slice_in_dim(shard, length - width, length, axis=dim)
        first = lax.slice_in_dim(shard, 0, width, axis=dim)
        before = lax.ppermute(last, axis, up)
        after = lax.ppermute(first, axis, down)
        shard = jnp.concatenate([before, shard, after], axis=dim)
    return shard


def dft_tables(length):
    line_index = jnp.arange(length, dtype=jnp.int32)
    phase_turns = line_index[:, None] * line_index[None, :] % length
    phase_angle = phase_turns.astype(jnp.float32) * (2.0 * jnp.pi / length)
    norm_scale = 1.0 / jnp.sqrt(jnp.float32(length))
    return (
        (jnp.cos(phase_angle) * norm_scale).astype(jnp.bfloat16),
        (jnp.sin(phase_angle) * norm_scale).astype(jnp.bfloat16),
    )


def along_y(values, table):
    return jnp.einsum("...yz,yk->...kz", values, table, preferred_element_type=jnp.float32)


def along_z(values, table):
    return jnp.einsum("...z,zk->...k", values, table, preferred_element_type=jnp.float32)


def spectrum(real_part, imag_part, cos_y, sin_y, cos_z, sin_z, forward):
    sign = 1.0 if forward else -1.0
    out_real = (along_y(real_part, cos_y) + sign * along_y(imag_part, sin_y)).astype(jnp.bfloat16)
    out_imag = (along_y(imag_part, cos_y) - sign * along_y(real_part, sin_y)).astype(jnp.bfloat16)
    last_real = along_z(out_real, cos_z) + sign * along_z(out_imag, sin_z)
    last_imag = along_z(out_imag, cos_z) - sign * along_z(out_real, sin_z)
    return (last_real, last_imag)


def adjoint_kernel(planes_ref, sens_ref, meas_ref, mask_ref, ty_ref, tz_ref, out_ref):
    ny = planes_ref.shape[1]
    nz = planes_ref.shape[2]

    @pl.when(pl.program_id(0) == 0)
    def _():
        out_ref[...] = jnp.zeros_like(out_ref)

    ty = ty_ref[...]
    tz = tz_ref[...]
    sens_real = sens_ref[0].astype(jnp.float32)
    sens_imag = sens_ref[1].astype(jnp.float32)
    image_real = planes_ref[0]
    image_imag = planes_ref[1]
    coil_real = (sens_real * image_real - sens_imag * image_imag).astype(jnp.bfloat16)
    coil_imag = (sens_real * image_imag + sens_imag * image_real).astype(jnp.bfloat16)
    half = jnp.dot(ty, jnp.concatenate([coil_real, coil_imag], axis=1), preferred_element_type=jnp.float32)
    half_real = (half[:ny, :nz] + half[ny:, nz:]).astype(jnp.bfloat16)
    half_imag = (half[:ny, nz:] - half[ny:, :nz]).astype(jnp.bfloat16)
    full = jnp.dot(jnp.concatenate([half_real, half_imag], axis=0), tz, preferred_element_type=jnp.float32)
    spec_real = full[:ny, :nz] + full[ny:, nz:]
    spec_imag = full[ny:, :nz] - full[:ny, nz:]
    sampled = mask_ref[...].astype(jnp.float32)
    miss_real = (sampled * (spec_real - meas_ref[0].astype(jnp.float32))).astype(jnp.bfloat16)
    miss_imag = (sampled * (spec_imag - meas_ref[1].astype(jnp.float32))).astype(jnp.bfloat16)
    half = jnp.dot(ty, jnp.concatenate([miss_real, miss_imag], axis=1), preferred_element_type=jnp.float32)
    back_real = (half[:ny, :nz] - half[ny:, nz:]).astype(jnp.bfloat16)
    back_imag = (half[:ny, nz:] + half[ny:, :nz]).astype(jnp.bfloat16)
    full = jnp.dot(jnp.concatenate([back_real, back_imag], axis=0), tz, preferred_element_type=jnp.float32)
    grad_real = full[:ny, :nz] - full[ny:, nz:]
    grad_imag = full[ny:, :nz] + full[:ny, nz:]
    out_ref[0] += sens_real * grad_real + sens_imag * grad_imag
    out_ref[1] += sens_real * grad_imag - sens_imag * grad_real


def coil_adjoint(planes, sens, measured, mask):
    ny = planes.shape[2]
    nz = planes.shape[3]
    cos_y, sin_y = dft_tables(ny)
    cos_z, sin_z = dft_tables(nz)
    ty = jnp.concatenate([cos_y, sin_y], axis=0)
    tz = jnp.concatenate([cos_z, sin_z], axis=1)
    coils = sens.shape[0]
    return pl.pallas_call(
        adjoint_kernel,
        grid=(coils,),
        in_specs=[
            pl.BlockSpec((2, None, ny, nz), lambda c: (0, 0, 0, 0)),
            pl.BlockSpec((None, 2, None, ny, nz), lambda c: (c, 0, 0, 0, 0)),
            pl.BlockSpec((None, 2, None, ny, nz), lambda c: (c, 0, 0, 0, 0)),
            pl.BlockSpec((ny, nz), lambda c: (0, 0)),
            pl.BlockSpec((2 * ny, ny), lambda c: (0, 0)),
            pl.BlockSpec((nz, 2 * nz), lambda c: (0, 0)),
        ],
        out_specs=pl.BlockSpec((2, None, ny, nz), lambda c: (0, 0, 0, 0)),
        out_shape=jax.ShapeDtypeStruct(planes.shape, jnp.float32),
    )(planes, sens, measured, mask, ty, tz)


def net_kernel(x_ref, p_ref, q_ref):
    width = p_ref.shape[1] // 4
    taps_in = x_ref.shape[1]
    rows = x_ref.shape[2]
    cols = x_ref.shape[3]
    outs = q_ref.shape[2]
    x = jnp.concatenate([x_ref[0, :, row, :] for row in range(rows)], axis=1)
    w1 = p_ref[:width, 0:taps_in].astype(jnp.bfloat16)
    w2 = p_ref[:width, width : 2 * width].astype(jnp.bfloat16)
    w3 = p_ref[:width, 2 * width : 3 * width].astype(jnp.bfloat16)
    wl = p_ref[width : width + outs, 0:width].astype(jnp.bfloat16)
    b1 = p_ref[:width, 3 * width : 3 * width + 1]
    b2 = p_ref[:width, 3 * width + 1 : 3 * width + 2]
    b3 = p_ref[:width, 3 * width + 2 : 3 * width + 3]
    h = jnp.dot(w1, x, preferred_element_type=jnp.float32) + b1
    h = jax.nn.silu(h).astype(jnp.bfloat16)
    h = jnp.dot(w2, h, preferred_element_type=jnp.float32) + b2
    h = jax.nn.silu(h).astype(jnp.bfloat16)
    h = jnp.dot(w3, h, preferred_element_type=jnp.float32) + b3
    h = jax.nn.silu(h).astype(jnp.bfloat16)
    q = jnp.dot(wl, h, preferred_element_type=jnp.float32)
    for row in range(rows):
        q_ref[0, row] = q[:, row * cols : (row + 1) * cols]


def score_net(window, w_first, b_first, w_second, b_second, w_third, b_third, w_last):
    slice_count = window.shape[0] - 4
    row_count = window.shape[2]
    col_count = window.shape[3]
    width = w_first.shape[-1]
    stacked = jnp.concatenate(
        [window[offset : offset + slice_count] for offset in range(5)], axis=1
    )
    framed = jnp.pad(stacked, ((0, 0), (0, 0), (1, 1), (1, 1)))
    columns = jnp.concatenate(
        [
            framed[:, :, shift_x : shift_x + row_count, shift_y : shift_y + col_count]
            for shift_x in range(3)
            for shift_y in range(3)
        ],
        axis=1,
    )
    taps_in = columns.shape[1]
    wl = w_last.reshape(-1, width)
    outs = wl.shape[0]
    top = jnp.concatenate(
        [
            jnp.pad(w_first.reshape(taps_in, width).T, ((0, 0), (0, width - taps_in))).astype(jnp.float32),
            w_second.T.astype(jnp.float32),
            w_third.T.astype(jnp.float32),
            jnp.pad(
                jnp.stack([b_first, b_second, b_third], axis=1),
                ((0, 0), (0, width - 3)),
            ),
        ],
        axis=1,
    ).astype(jnp.float32)
    bottom = jnp.pad(wl.astype(jnp.float32), ((0, -(-outs // 8) * 8 - outs), (0, 3 * width)))
    packed = jnp.concatenate([top, bottom], axis=0)
    rows = 16
    q = pl.pallas_call(
        net_kernel,
        grid=(slice_count, row_count // rows),
        in_specs=[
            pl.BlockSpec((1, taps_in, rows, col_count), lambda z, n: (z, 0, n, 0)),
            pl.BlockSpec(packed.shape, lambda z, n: (0, 0)),
        ],
        out_specs=pl.BlockSpec((1, rows, outs, col_count), lambda z, n: (z, n, 0, 0)),
        out_shape=jax.ShapeDtypeStruct((slice_count, row_count, outs, col_count), jnp.float32),
    )(columns, packed)
    q = jnp.pad(q, ((0, 0), (1, 1), (0, 0), (1, 1)))
    score_field = jnp.zeros((slice_count, row_count, 2, col_count), jnp.float32)
    for shift_x in range(3):
        for shift_y in range(3):
            tap = (shift_x * 3 + shift_y) * 2
            score_field = score_field + q[
                :, shift_x : shift_x + row_count, tap : tap + 2, shift_y : shift_y + col_count
            ]
    return jnp.transpose(score_field, (0, 2, 1, 3))


def slab_slices(image):
    return lax.all_gather(image, "coil", axis=0, tiled=True)


def on_device(
    image,
    noise,
    sens,
    measured,
    mask,
    w_first,
    b_first,
    w_second,
    b_second,
    w_third,
    b_third,
    w_last,
):
    window = with_halo(image.astype(jnp.bfloat16), ((("slab", "coil"), 0),), 2)
    score_field = score_net(window, w_first, b_first, w_second, b_second, w_third, b_third, w_last)
    planes_in = lax.all_to_all(slab_slices(image), "slab", split_axis=2, concat_axis=0, tiled=True)
    planes = jnp.transpose(planes_in, (1, 2, 3, 0))
    partial_sum = coil_adjoint(planes, sens, measured, mask)
    by_depth = jnp.transpose(partial_sum, (3, 0, 1, 2))
    slab_part = lax.all_to_all(
        by_depth.astype(jnp.bfloat16), "slab", split_axis=0, concat_axis=2, tiled=True
    ).astype(by_depth.dtype)
    gradient = lax.psum_scatter(
        slab_part.astype(jnp.bfloat16), "coil", scatter_dimension=0, tiled=True
    ).astype(jnp.float32)
    return image + STEP_SIZE * (score_field - gradient) + noise


def solution(mesh):
    in_specs = (
        P(("slab", "coil"), None, None, None),
        P(("slab", "coil"), None, None, None),
        P("coil", None, "slab", None, None),
        P("coil", None, "slab", None, None),
        P(),
        P(),
        P(),
        P(),
        P(),
        P(),
        P(),
        P(),
    )
    out_specs = P(("slab", "coil"), None, None, None)
    return jax.shard_map(
        on_device, mesh=mesh, in_specs=in_specs, out_specs=out_specs, check_vma=False
    )
```

```python
import jax
import jax.numpy as jnp
from jax import lax
from jax.sharding import PartitionSpec as P
from jax.experimental import pallas as pl
from jax.experimental.pallas import tpu as pltpu

STEP_SIZE = 0.5


def with_halo(shard, sides, width):
    for axis, dim in sides:
        devices, length = (lax.axis_size(axis), shard.shape[dim])
        up = [(i, (i + 1) % devices) for i in range(devices - 1)]
        down = [(j, i) for i, j in up]
        last = lax.slice_in_dim(shard, length - width, length, axis=dim)
        first = lax.slice_in_dim(shard, 0, width, axis=dim)
        before = lax.ppermute(last, axis, up)
        after = lax.ppermute(first, axis, down)
        shard = jnp.concatenate([before, shard, after], axis=dim)
    return shard


def dft_tables(length):
    line_index = jnp.arange(length, dtype=jnp.int32)
    phase_turns = line_index[:, None] * line_index[None, :] % length
    phase_angle = phase_turns.astype(jnp.float32) * (2.0 * jnp.pi / length)
    norm_scale = 1.0 / jnp.sqrt(jnp.float32(length))
    return (
        (jnp.cos(phase_angle) * norm_scale).astype(jnp.bfloat16),
        (jnp.sin(phase_angle) * norm_scale).astype(jnp.bfloat16),
    )


def along_y(values, table):
    return jnp.einsum("...yz,yk->...kz", values, table, preferred_element_type=jnp.float32)


def along_z(values, table):
    return jnp.einsum("...z,zk->...k", values, table, preferred_element_type=jnp.float32)


def spectrum(real_part, imag_part, cos_y, sin_y, cos_z, sin_z, forward):
    sign = 1.0 if forward else -1.0
    out_real = (along_y(real_part, cos_y) + sign * along_y(imag_part, sin_y)).astype(jnp.bfloat16)
    out_imag = (along_y(imag_part, cos_y) - sign * along_y(real_part, sin_y)).astype(jnp.bfloat16)
    last_real = along_z(out_real, cos_z) + sign * along_z(out_imag, sin_z)
    last_imag = along_z(out_imag, cos_z) - sign * along_z(out_real, sin_z)
    return (last_real, last_imag)


def adjoint_kernel(planes_ref, sens_ref, meas_ref, mask_ref, ty_ref, tz_ref, out_ref):
    ny = planes_ref.shape[1]
    nz = planes_ref.shape[2]

    @pl.when(pl.program_id(0) == 0)
    def _():
        out_ref[...] = jnp.zeros_like(out_ref)

    ty = ty_ref[...]
    tz = tz_ref[...]
    sens_real = sens_ref[0].astype(jnp.float32)
    sens_imag = sens_ref[1].astype(jnp.float32)
    image_real = planes_ref[0]
    image_imag = planes_ref[1]
    coil_real = (sens_real * image_real - sens_imag * image_imag).astype(jnp.bfloat16)
    coil_imag = (sens_real * image_imag + sens_imag * image_real).astype(jnp.bfloat16)
    half = jnp.dot(ty, jnp.concatenate([coil_real, coil_imag], axis=1), preferred_element_type=jnp.float32)
    half_real = (half[:ny, :nz] + half[ny:, nz:]).astype(jnp.bfloat16)
    half_imag = (half[:ny, nz:] - half[ny:, :nz]).astype(jnp.bfloat16)
    full = jnp.dot(jnp.concatenate([half_real, half_imag], axis=0), tz, preferred_element_type=jnp.float32)
    spec_real = full[:ny, :nz] + full[ny:, nz:]
    spec_imag = full[ny:, :nz] - full[:ny, nz:]
    sampled = mask_ref[...].astype(jnp.float32)
    miss_real = (sampled * (spec_real - meas_ref[0].astype(jnp.float32))).astype(jnp.bfloat16)
    miss_imag = (sampled * (spec_imag - meas_ref[1].astype(jnp.float32))).astype(jnp.bfloat16)
    half = jnp.dot(ty, jnp.concatenate([miss_real, miss_imag], axis=1), preferred_element_type=jnp.float32)
    back_real = (half[:ny, :nz] - half[ny:, nz:]).astype(jnp.bfloat16)
    back_imag = (half[:ny, nz:] + half[ny:, :nz]).astype(jnp.bfloat16)
    full = jnp.dot(jnp.concatenate([back_real, back_imag], axis=0), tz, preferred_element_type=jnp.float32)
    grad_real = full[:ny, :nz] - full[ny:, nz:]
    grad_imag = full[ny:, :nz] + full[:ny, nz:]
    out_ref[0] += sens_real * grad_real + sens_imag * grad_imag
    out_ref[1] += sens_real * grad_imag - sens_imag * grad_real


def coil_adjoint(planes, sens, measured, mask):
    ny = planes.shape[2]
    nz = planes.shape[3]
    cos_y, sin_y = dft_tables(ny)
    cos_z, sin_z = dft_tables(nz)
    ty = jnp.concatenate([cos_y, sin_y], axis=0)
    tz = jnp.concatenate([cos_z, sin_z], axis=1)
    coils = sens.shape[0]
    return pl.pallas_call(
        adjoint_kernel,
        grid=(coils,),
        in_specs=[
            pl.BlockSpec((2, None, ny, nz), lambda c: (0, 0, 0, 0)),
            pl.BlockSpec((None, 2, None, ny, nz), lambda c: (c, 0, 0, 0, 0)),
            pl.BlockSpec((None, 2, None, ny, nz), lambda c: (c, 0, 0, 0, 0)),
            pl.BlockSpec((ny, nz), lambda c: (0, 0)),
            pl.BlockSpec((2 * ny, ny), lambda c: (0, 0)),
            pl.BlockSpec((nz, 2 * nz), lambda c: (0, 0)),
        ],
        out_specs=pl.BlockSpec((2, None, ny, nz), lambda c: (0, 0, 0, 0)),
        out_shape=jax.ShapeDtypeStruct(planes.shape, jnp.float32),
    )(planes, sens, measured, mask, ty, tz)


def silu(h):
    return h * (0.5 + 0.5 * jnp.tanh(0.5 * h))


def net_kernel(x_ref, p_ref, q_ref):
    width = p_ref.shape[1] // 4
    taps_in = x_ref.shape[1]
    rows = x_ref.shape[2]
    cols = x_ref.shape[3]
    outs = q_ref.shape[2]
    x = jnp.concatenate([x_ref[0, :, row, :] for row in range(rows)], axis=1)
    w1 = p_ref[:width, 0:taps_in].astype(jnp.bfloat16)
    w2 = p_ref[:width, width : 2 * width].astype(jnp.bfloat16)
    w3 = p_ref[:width, 2 * width : 3 * width].astype(jnp.bfloat16)
    wl = p_ref[width : width + outs, 0:width].astype(jnp.bfloat16)
    b1 = p_ref[:width, 3 * width : 3 * width + 1]
    b2 = p_ref[:width, 3 * width + 1 : 3 * width + 2]
    b3 = p_ref[:width, 3 * width + 2 : 3 * width + 3]
    h = jnp.dot(w1, x, preferred_element_type=jnp.float32) + b1
    h = silu(h).astype(jnp.bfloat16)
    h = jnp.dot(w2, h, preferred_element_type=jnp.float32) + b2
    h = silu(h).astype(jnp.bfloat16)
    h = jnp.dot(w3, h, preferred_element_type=jnp.float32) + b3
    h = silu(h).astype(jnp.bfloat16)
    q = jnp.dot(wl, h, preferred_element_type=jnp.float32)
    for row in range(rows):
        q_ref[0, row] = q[:, row * cols : (row + 1) * cols]


def score_net(window, w_first, b_first, w_second, b_second, w_third, b_third, w_last):
    slice_count = window.shape[0] - 4
    row_count = window.shape[2]
    col_count = window.shape[3]
    width = w_first.shape[-1]
    stacked = jnp.concatenate(
        [window[offset : offset + slice_count] for offset in range(5)], axis=1
    )
    framed = jnp.pad(stacked, ((0, 0), (0, 0), (1, 1), (1, 1)))
    columns = jnp.concatenate(
        [
            framed[:, :, shift_x : shift_x + row_count, shift_y : shift_y + col_count]
            for shift_x in range(3)
            for shift_y in range(3)
        ],
        axis=1,
    )
    taps_in = columns.shape[1]
    wl = w_last.reshape(-1, width)
    outs = wl.shape[0]
    top = jnp.concatenate(
        [
            jnp.pad(w_first.reshape(taps_in, width).T, ((0, 0), (0, width - taps_in))).astype(jnp.float32),
            w_second.T.astype(jnp.float32),
            w_third.T.astype(jnp.float32),
            jnp.pad(
                jnp.stack([b_first, b_second, b_third], axis=1),
                ((0, 0), (0, width - 3)),
            ),
        ],
        axis=1,
    ).astype(jnp.float32)
    bottom = jnp.pad(wl.astype(jnp.float32), ((0, -(-outs // 8) * 8 - outs), (0, 3 * width)))
    packed = jnp.concatenate([top, bottom], axis=0)
    rows = 16
    q = pl.pallas_call(
        net_kernel,
        grid=(slice_count, row_count // rows),
        in_specs=[
            pl.BlockSpec((1, taps_in, rows, col_count), lambda z, n: (z, 0, n, 0)),
            pl.BlockSpec(packed.shape, lambda z, n: (0, 0)),
        ],
        out_specs=pl.BlockSpec((1, rows, outs, col_count), lambda z, n: (z, n, 0, 0)),
        out_shape=jax.ShapeDtypeStruct((slice_count, row_count, outs, col_count), jnp.float32),
    )(columns, packed)
    q = jnp.pad(q, ((0, 0), (1, 1), (0, 0), (1, 1)))
    score_field = jnp.zeros((slice_count, row_count, 2, col_count), jnp.float32)
    for shift_x in range(3):
        for shift_y in range(3):
            tap = (shift_x * 3 + shift_y) * 2
            score_field = score_field + q[
                :, shift_x : shift_x + row_count, tap : tap + 2, shift_y : shift_y + col_count
            ]
    return jnp.transpose(score_field, (0, 2, 1, 3))


def slab_slices(image):
    return lax.all_gather(image, "coil", axis=0, tiled=True)


def on_device(
    image,
    noise,
    sens,
    measured,
    mask,
    w_first,
    b_first,
    w_second,
    b_second,
    w_third,
    b_third,
    w_last,
):
    window = with_halo(image.astype(jnp.bfloat16), ((("slab", "coil"), 0),), 2)
    score_field = score_net(window, w_first, b_first, w_second, b_second, w_third, b_third, w_last)
    planes_in = lax.all_to_all(slab_slices(image), "slab", split_axis=2, concat_axis=0, tiled=True)
    planes = jnp.transpose(planes_in, (1, 2, 3, 0))
    partial_sum = coil_adjoint(planes, sens, measured, mask)
    by_depth = jnp.transpose(partial_sum, (3, 0, 1, 2))
    slab_part = lax.all_to_all(
        by_depth.astype(jnp.bfloat16), "slab", split_axis=0, concat_axis=2, tiled=True
    ).astype(by_depth.dtype)
    gradient = lax.psum_scatter(
        slab_part.astype(jnp.bfloat16), "coil", scatter_dimension=0, tiled=True
    ).astype(jnp.float32)
    return image + STEP_SIZE * (score_field - gradient) + noise


def solution(mesh):
    in_specs = (
        P(("slab", "coil"), None, None, None),
        P(("slab", "coil"), None, None, None),
        P("coil", None, "slab", None, None),
        P("coil", None, "slab", None, None),
        P(),
        P(),
        P(),
        P(),
        P(),
        P(),
        P(),
        P(),
    )
    out_specs = P(("slab", "coil"), None, None, None)
    return jax.shard_map(
        on_device, mesh=mesh, in_specs=in_specs, out_specs=out_specs, check_vma=False
    )
```

```python
import jax
import jax.numpy as jnp
from jax import lax
from jax.sharding import PartitionSpec as P
from jax.experimental import pallas as pl
from jax.experimental.pallas import tpu as pltpu

STEP_SIZE = 0.5


def with_halo(shard, sides, width):
    for axis, dim in sides:
        devices, length = (lax.axis_size(axis), shard.shape[dim])
        up = [(i, (i + 1) % devices) for i in range(devices - 1)]
        down = [(j, i) for i, j in up]
        last = lax.slice_in_dim(shard, length - width, length, axis=dim)
        first = lax.slice_in_dim(shard, 0, width, axis=dim)
        before = lax.ppermute(last, axis, up)
        after = lax.ppermute(first, axis, down)
        shard = jnp.concatenate([before, shard, after], axis=dim)
    return shard


def dft_tables(length):
    line_index = jnp.arange(length, dtype=jnp.int32)
    phase_turns = line_index[:, None] * line_index[None, :] % length
    phase_angle = phase_turns.astype(jnp.float32) * (2.0 * jnp.pi / length)
    norm_scale = 1.0 / jnp.sqrt(jnp.float32(length))
    return (
        (jnp.cos(phase_angle) * norm_scale).astype(jnp.bfloat16),
        (jnp.sin(phase_angle) * norm_scale).astype(jnp.bfloat16),
    )


def along_y(values, table):
    return jnp.einsum("...yz,yk->...kz", values, table, preferred_element_type=jnp.float32)


def along_z(values, table):
    return jnp.einsum("...z,zk->...k", values, table, preferred_element_type=jnp.float32)


def spectrum(real_part, imag_part, cos_y, sin_y, cos_z, sin_z, forward):
    sign = 1.0 if forward else -1.0
    out_real = (along_y(real_part, cos_y) + sign * along_y(imag_part, sin_y)).astype(jnp.bfloat16)
    out_imag = (along_y(imag_part, cos_y) - sign * along_y(real_part, sin_y)).astype(jnp.bfloat16)
    last_real = along_z(out_real, cos_z) + sign * along_z(out_imag, sin_z)
    last_imag = along_z(out_imag, cos_z) - sign * along_z(out_real, sin_z)
    return (last_real, last_imag)


def adjoint_kernel(planes_ref, sens_ref, meas_ref, mask_ref, ty_ref, tz_ref, out_ref):
    ny = planes_ref.shape[1]
    nz = planes_ref.shape[2]

    @pl.when(pl.program_id(0) == 0)
    def _():
        out_ref[...] = jnp.zeros_like(out_ref)

    ty = ty_ref[...]
    tz = tz_ref[...]
    sens_real = sens_ref[0].astype(jnp.float32)
    sens_imag = sens_ref[1].astype(jnp.float32)
    image_real = planes_ref[0]
    image_imag = planes_ref[1]
    coil_real = (sens_real * image_real - sens_imag * image_imag).astype(jnp.bfloat16)
    coil_imag = (sens_real * image_imag + sens_imag * image_real).astype(jnp.bfloat16)
    half = jnp.dot(ty, jnp.concatenate([coil_real, coil_imag], axis=1), preferred_element_type=jnp.float32)
    half_real = (half[:ny, :nz] + half[ny:, nz:]).astype(jnp.bfloat16)
    half_imag = (half[:ny, nz:] - half[ny:, :nz]).astype(jnp.bfloat16)
    full = jnp.dot(jnp.concatenate([half_real, half_imag], axis=0), tz, preferred_element_type=jnp.float32)
    spec_real = full[:ny, :nz] + full[ny:, nz:]
    spec_imag = full[ny:, :nz] - full[:ny, nz:]
    sampled = mask_ref[...].astype(jnp.float32)
    miss_real = (sampled * (spec_real - meas_ref[0].astype(jnp.float32))).astype(jnp.bfloat16)
    miss_imag = (sampled * (spec_imag - meas_ref[1].astype(jnp.float32))).astype(jnp.bfloat16)
    half = jnp.dot(ty, jnp.concatenate([miss_real, miss_imag], axis=1), preferred_element_type=jnp.float32)
    back_real = (half[:ny, :nz] - half[ny:, nz:]).astype(jnp.bfloat16)
    back_imag = (half[:ny, nz:] + half[ny:, :nz]).astype(jnp.bfloat16)
    full = jnp.dot(jnp.concatenate([back_real, back_imag], axis=0), tz, preferred_element_type=jnp.float32)
    grad_real = full[:ny, :nz] - full[ny:, nz:]
    grad_imag = full[ny:, :nz] + full[:ny, nz:]
    out_ref[0] += sens_real * grad_real + sens_imag * grad_imag
    out_ref[1] += sens_real * grad_imag - sens_imag * grad_real


def coil_adjoint(planes, sens, measured, mask):
    ny = planes.shape[2]
    nz = planes.shape[3]
    cos_y, sin_y = dft_tables(ny)
    cos_z, sin_z = dft_tables(nz)
    ty = jnp.concatenate([cos_y, sin_y], axis=0)
    tz = jnp.concatenate([cos_z, sin_z], axis=1)
    coils = sens.shape[0]
    return pl.pallas_call(
        adjoint_kernel,
        grid=(coils,),
        in_specs=[
            pl.BlockSpec((2, None, ny, nz), lambda c: (0, 0, 0, 0)),
            pl.BlockSpec((None, 2, None, ny, nz), lambda c: (c, 0, 0, 0, 0)),
            pl.BlockSpec((None, 2, None, ny, nz), lambda c: (c, 0, 0, 0, 0)),
            pl.BlockSpec((ny, nz), lambda c: (0, 0)),
            pl.BlockSpec((2 * ny, ny), lambda c: (0, 0)),
            pl.BlockSpec((nz, 2 * nz), lambda c: (0, 0)),
        ],
        out_specs=pl.BlockSpec((2, None, ny, nz), lambda c: (0, 0, 0, 0)),
        out_shape=jax.ShapeDtypeStruct(planes.shape, jnp.float32),
        cost_estimate=pl.CostEstimate(
            flops=coils * 8 * ny * nz * (ny + nz) * 2,
            transcendentals=0,
            bytes_accessed=(sens.size + measured.size) * 2 + planes.size * 8,
        ),
    )(planes, sens, measured, mask, ty, tz)


def net_kernel(x_ref, p_ref, q_ref):
    width = p_ref.shape[1] // 4
    taps_in = x_ref.shape[1]
    rows = x_ref.shape[2]
    cols = x_ref.shape[3]
    outs = q_ref.shape[2]
    x = jnp.concatenate([x_ref[0, :, row, :] for row in range(rows)], axis=1)
    w1 = p_ref[:width, 0:taps_in].astype(jnp.bfloat16)
    w2 = p_ref[:width, width : 2 * width].astype(jnp.bfloat16)
    w3 = p_ref[:width, 2 * width : 3 * width].astype(jnp.bfloat16)
    wl = p_ref[width : width + outs, 0:width].astype(jnp.bfloat16)
    b1 = p_ref[:width, 3 * width : 3 * width + 1]
    b2 = p_ref[:width, 3 * width + 1 : 3 * width + 2]
    b3 = p_ref[:width, 3 * width + 2 : 3 * width + 3]
    h = jnp.dot(w1, x, preferred_element_type=jnp.float32) + b1
    h = jax.nn.silu(h).astype(jnp.bfloat16)
    h = jnp.dot(w2, h, preferred_element_type=jnp.float32) + b2
    h = jax.nn.silu(h).astype(jnp.bfloat16)
    h = jnp.dot(w3, h, preferred_element_type=jnp.float32) + b3
    h = jax.nn.silu(h).astype(jnp.bfloat16)
    q = jnp.dot(wl, h, preferred_element_type=jnp.float32)
    for row in range(rows):
        q_ref[0, row] = q[:, row * cols : (row + 1) * cols]


def score_net(window, w_first, b_first, w_second, b_second, w_third, b_third, w_last):
    slice_count = window.shape[0] - 4
    row_count = window.shape[2]
    col_count = window.shape[3]
    width = w_first.shape[-1]
    stacked = jnp.concatenate(
        [window[offset : offset + slice_count] for offset in range(5)], axis=1
    )
    framed = jnp.pad(stacked, ((0, 0), (0, 0), (1, 1), (1, 1)))
    columns = jnp.concatenate(
        [
            framed[:, :, shift_x : shift_x + row_count, shift_y : shift_y + col_count]
            for shift_x in range(3)
            for shift_y in range(3)
        ],
        axis=1,
    )
    taps_in = columns.shape[1]
    wl = w_last.reshape(-1, width)
    outs = wl.shape[0]
    top = jnp.concatenate(
        [
            jnp.pad(w_first.reshape(taps_in, width).T, ((0, 0), (0, width - taps_in))).astype(jnp.float32),
            w_second.T.astype(jnp.float32),
            w_third.T.astype(jnp.float32),
            jnp.pad(
                jnp.stack([b_first, b_second, b_third], axis=1),
                ((0, 0), (0, width - 3)),
            ),
        ],
        axis=1,
    ).astype(jnp.float32)
    bottom = jnp.pad(wl.astype(jnp.float32), ((0, -(-outs // 8) * 8 - outs), (0, 3 * width)))
    packed = jnp.concatenate([top, bottom], axis=0)
    rows = 16
    q = pl.pallas_call(
        net_kernel,
        grid=(slice_count, row_count // rows),
        in_specs=[
            pl.BlockSpec((1, taps_in, rows, col_count), lambda z, n: (z, 0, n, 0)),
            pl.BlockSpec(packed.shape, lambda z, n: (0, 0)),
        ],
        out_specs=pl.BlockSpec((1, rows, outs, col_count), lambda z, n: (z, n, 0, 0)),
        out_shape=jax.ShapeDtypeStruct((slice_count, row_count, outs, col_count), jnp.float32),
        cost_estimate=pl.CostEstimate(
            flops=2 * slice_count * row_count * col_count * width * (taps_in + 2 * width + outs),
            transcendentals=3 * slice_count * row_count * col_count * width,
            bytes_accessed=columns.size * 2 + slice_count * row_count * outs * col_count * 4,
        ),
    )(columns, packed)
    q = jnp.pad(q, ((0, 0), (1, 1), (0, 0), (1, 1)))
    score_field = jnp.zeros((slice_count, row_count, 2, col_count), jnp.float32)
    for shift_x in range(3):
        for shift_y in range(3):
            tap = (shift_x * 3 + shift_y) * 2
            score_field = score_field + q[
                :, shift_x : shift_x + row_count, tap : tap + 2, shift_y : shift_y + col_count
            ]
    return jnp.transpose(score_field, (0, 2, 1, 3))


def slab_slices(image):
    groups = lax.axis_size("coil")
    received = [image] + [
        lax.ppermute(image, "coil", [(i, (i + shift) % groups) for i in range(groups)])
        for shift in range(1, groups)
    ]
    order = (lax.axis_index("coil") - jnp.arange(groups)) % groups
    return jnp.take(jnp.stack(received), order, axis=0).reshape((-1,) + image.shape[1:])


def on_device(
    image,
    noise,
    sens,
    measured,
    mask,
    w_first,
    b_first,
    w_second,
    b_second,
    w_third,
    b_third,
    w_last,
):
    window = with_halo(image.astype(jnp.bfloat16), ((("slab", "coil"), 0),), 2)
    score_field = score_net(window, w_first, b_first, w_second, b_second, w_third, b_third, w_last)
    planes_in = lax.all_to_all(slab_slices(image), "slab", split_axis=2, concat_axis=0, tiled=True)
    planes = jnp.transpose(planes_in, (1, 2, 3, 0))
    partial_sum = coil_adjoint(planes, sens, measured, mask)
    by_depth = jnp.transpose(partial_sum, (3, 0, 1, 2))
    slab_part = lax.all_to_all(
        by_depth.astype(jnp.bfloat16), "slab", split_axis=0, concat_axis=2, tiled=True
    ).astype(by_depth.dtype)
    gradient = lax.psum_scatter(
        slab_part.astype(jnp.bfloat16), "coil", scatter_dimension=0, tiled=True
    ).astype(jnp.float32)
    return image + STEP_SIZE * (score_field - gradient) + noise


def solution(mesh):
    in_specs = (
        P(("slab", "coil"), None, None, None),
        P(("slab", "coil"), None, None, None),
        P("coil", None, "slab", None, None),
        P("coil", None, "slab", None, None),
        P(),
        P(),
        P(),
        P(),
        P(),
        P(),
        P(),
        P(),
    )
    out_specs = P(("slab", "coil"), None, None, None)
    return jax.shard_map(
        on_device, mesh=mesh, in_specs=in_specs, out_specs=out_specs, check_vma=False
    )
```

```python
import jax
import jax.numpy as jnp
from jax import lax
from jax.sharding import PartitionSpec as P
from jax.experimental import pallas as pl
from jax.experimental.pallas import tpu as pltpu

STEP_SIZE = 0.5


def with_halo(shard, sides, width):
    for axis, dim in sides:
        devices, length = (lax.axis_size(axis), shard.shape[dim])
        up = [(i, (i + 1) % devices) for i in range(devices - 1)]
        down = [(j, i) for i, j in up]
        last = lax.slice_in_dim(shard, length - width, length, axis=dim)
        first = lax.slice_in_dim(shard, 0, width, axis=dim)
        before = lax.ppermute(last, axis, up)
        after = lax.ppermute(first, axis, down)
        shard = jnp.concatenate([before, shard, after], axis=dim)
    return shard


def dft_tables(length):
    line_index = jnp.arange(length, dtype=jnp.int32)
    phase_turns = line_index[:, None] * line_index[None, :] % length
    phase_angle = phase_turns.astype(jnp.float32) * (2.0 * jnp.pi / length)
    norm_scale = 1.0 / jnp.sqrt(jnp.float32(length))
    return (
        (jnp.cos(phase_angle) * norm_scale).astype(jnp.bfloat16),
        (jnp.sin(phase_angle) * norm_scale).astype(jnp.bfloat16),
    )


def along_y(values, table):
    return jnp.einsum("...yz,yk->...kz", values, table, preferred_element_type=jnp.float32)


def along_z(values, table):
    return jnp.einsum("...z,zk->...k", values, table, preferred_element_type=jnp.float32)


def spectrum(real_part, imag_part, cos_y, sin_y, cos_z, sin_z, forward):
    sign = 1.0 if forward else -1.0
    out_real = (along_y(real_part, cos_y) + sign * along_y(imag_part, sin_y)).astype(jnp.bfloat16)
    out_imag = (along_y(imag_part, cos_y) - sign * along_y(real_part, sin_y)).astype(jnp.bfloat16)
    last_real = along_z(out_real, cos_z) + sign * along_z(out_imag, sin_z)
    last_imag = along_z(out_imag, cos_z) - sign * along_z(out_real, sin_z)
    return (last_real, last_imag)


def adjoint_kernel(planes_ref, sens_ref, meas_ref, mask_ref, ty_ref, tz_ref, out_ref):
    ny = planes_ref.shape[1]
    nz = planes_ref.shape[2]

    @pl.when(pl.program_id(0) == 0)
    def _():
        out_ref[...] = jnp.zeros_like(out_ref)

    ty = ty_ref[...]
    tz = tz_ref[...]
    sens_real = sens_ref[0].astype(jnp.float32)
    sens_imag = sens_ref[1].astype(jnp.float32)
    image_real = planes_ref[0]
    image_imag = planes_ref[1]
    coil_real = (sens_real * image_real - sens_imag * image_imag).astype(jnp.bfloat16)
    coil_imag = (sens_real * image_imag + sens_imag * image_real).astype(jnp.bfloat16)
    half = jnp.dot(ty, jnp.concatenate([coil_real, coil_imag], axis=1), preferred_element_type=jnp.float32)
    half_real = (half[:ny, :nz] + half[ny:, nz:]).astype(jnp.bfloat16)
    half_imag = (half[:ny, nz:] - half[ny:, :nz]).astype(jnp.bfloat16)
    full = jnp.dot(jnp.concatenate([half_real, half_imag], axis=0), tz, preferred_element_type=jnp.float32)
    spec_real = full[:ny, :nz] + full[ny:, nz:]
    spec_imag = full[ny:, :nz] - full[:ny, nz:]
    sampled = mask_ref[...].astype(jnp.float32)
    miss_real = (sampled * (spec_real - meas_ref[0].astype(jnp.float32))).astype(jnp.bfloat16)
    miss_imag = (sampled * (spec_imag - meas_ref[1].astype(jnp.float32))).astype(jnp.bfloat16)
    half = jnp.dot(ty, jnp.concatenate([miss_real, miss_imag], axis=1), preferred_element_type=jnp.float32)
    back_real = (half[:ny, :nz] - half[ny:, nz:]).astype(jnp.bfloat16)
    back_imag = (half[:ny, nz:] + half[ny:, :nz]).astype(jnp.bfloat16)
    full = jnp.dot(jnp.concatenate([back_real, back_imag], axis=0), tz, preferred_element_type=jnp.float32)
    grad_real = full[:ny, :nz] - full[ny:, nz:]
    grad_imag = full[ny:, :nz] + full[:ny, nz:]
    out_ref[0] += sens_real * grad_real + sens_imag * grad_imag
    out_ref[1] += sens_real * grad_imag - sens_imag * grad_real


def coil_adjoint(planes, sens, measured, mask):
    ny = planes.shape[2]
    nz = planes.shape[3]
    cos_y, sin_y = dft_tables(ny)
    cos_z, sin_z = dft_tables(nz)
    ty = jnp.concatenate([cos_y, sin_y], axis=0)
    tz = jnp.concatenate([cos_z, sin_z], axis=1)
    coils = sens.shape[0]
    return pl.pallas_call(
        adjoint_kernel,
        grid=(coils,),
        in_specs=[
            pl.BlockSpec((2, None, ny, nz), lambda c: (0, 0, 0, 0)),
            pl.BlockSpec((None, 2, None, ny, nz), lambda c: (c, 0, 0, 0, 0)),
            pl.BlockSpec((None, 2, None, ny, nz), lambda c: (c, 0, 0, 0, 0)),
            pl.BlockSpec((ny, nz), lambda c: (0, 0)),
            pl.BlockSpec((2 * ny, ny), lambda c: (0, 0)),
            pl.BlockSpec((nz, 2 * nz), lambda c: (0, 0)),
        ],
        out_specs=pl.BlockSpec((2, None, ny, nz), lambda c: (0, 0, 0, 0)),
        out_shape=jax.ShapeDtypeStruct(planes.shape, jnp.float32),
    )(planes, sens, measured, mask, ty, tz)


def net_kernel(x_ref, p_ref, q_ref):
    width = p_ref.shape[1] // 4
    taps_in = x_ref.shape[1]
    rows = x_ref.shape[2]
    cols = x_ref.shape[3]
    outs = q_ref.shape[2]
    x = jnp.concatenate([x_ref[0, :, row, :] for row in range(rows)], axis=1)
    w1 = p_ref[:width, 0:taps_in].astype(jnp.bfloat16)
    w2 = p_ref[:width, width : 2 * width].astype(jnp.bfloat16)
    w3 = p_ref[:width, 2 * width : 3 * width].astype(jnp.bfloat16)
    wl = p_ref[width : width + outs, 0:width].astype(jnp.bfloat16)
    b1 = p_ref[:width, 3 * width : 3 * width + 1]
    b2 = p_ref[:width, 3 * width + 1 : 3 * width + 2]
    b3 = p_ref[:width, 3 * width + 2 : 3 * width + 3]
    h = jnp.dot(w1, x, preferred_element_type=jnp.float32) + b1
    h = jax.nn.silu(h).astype(jnp.bfloat16)
    h = jnp.dot(w2, h, preferred_element_type=jnp.float32) + b2
    h = jax.nn.silu(h).astype(jnp.bfloat16)
    h = jnp.dot(w3, h, preferred_element_type=jnp.float32) + b3
    h = jax.nn.silu(h).astype(jnp.bfloat16)
    q = jnp.dot(wl, h, preferred_element_type=jnp.float32)
    for row in range(rows):
        q_ref[0, row] = q[:, row * cols : (row + 1) * cols]


def score_net(window, w_first, b_first, w_second, b_second, w_third, b_third, w_last):
    slice_count = window.shape[0] - 4
    row_count = window.shape[2]
    col_count = window.shape[3]
    width = w_first.shape[-1]
    stacked = jnp.concatenate(
        [window[offset : offset + slice_count] for offset in range(5)], axis=1
    )
    framed = jnp.pad(stacked, ((0, 0), (0, 0), (1, 1), (1, 1)))
    columns = jnp.concatenate(
        [
            framed[:, :, shift_x : shift_x + row_count, shift_y : shift_y + col_count]
            for shift_x in range(3)
            for shift_y in range(3)
        ],
        axis=1,
    )
    taps_in = columns.shape[1]
    wl = w_last.reshape(-1, width)
    outs = wl.shape[0]
    top = jnp.concatenate(
        [
            jnp.pad(w_first.reshape(taps_in, width).T, ((0, 0), (0, width - taps_in))).astype(jnp.float32),
            w_second.T.astype(jnp.float32),
            w_third.T.astype(jnp.float32),
            jnp.pad(
                jnp.stack([b_first, b_second, b_third], axis=1),
                ((0, 0), (0, width - 3)),
            ),
        ],
        axis=1,
    ).astype(jnp.float32)
    bottom = jnp.pad(wl.astype(jnp.float32), ((0, -(-outs // 8) * 8 - outs), (0, 3 * width)))
    packed = jnp.concatenate([top, bottom], axis=0)
    rows = 16
    q = pl.pallas_call(
        net_kernel,
        grid=(slice_count, row_count // rows),
        in_specs=[
            pl.BlockSpec((1, taps_in, rows, col_count), lambda z, n: (z, 0, n, 0)),
            pl.BlockSpec(packed.shape, lambda z, n: (0, 0)),
        ],
        out_specs=pl.BlockSpec((1, rows, outs, col_count), lambda z, n: (z, n, 0, 0)),
        out_shape=jax.ShapeDtypeStruct((slice_count, row_count, outs, col_count), jnp.float32),
    )(columns, packed)
    q = jnp.pad(q, ((0, 0), (1, 1), (0, 0), (1, 1)))
    score_field = jnp.zeros((slice_count, row_count, 2, col_count), jnp.float32)
    for shift_x in range(3):
        for shift_y in range(3):
            tap = (shift_x * 3 + shift_y) * 2
            score_field = score_field + q[
                :, shift_x : shift_x + row_count, tap : tap + 2, shift_y : shift_y + col_count
            ]
    return jnp.transpose(score_field, (0, 2, 1, 3))


def slab_slices(image):
    return lax.all_gather(image, "coil", axis=0, tiled=True)


def on_device(
    image,
    noise,
    sens,
    measured,
    mask,
    w_first,
    b_first,
    w_second,
    b_second,
    w_third,
    b_third,
    w_last,
):
    window = with_halo(image.astype(jnp.bfloat16), ((("slab", "coil"), 0),), 2)
    score_field = score_net(window, w_first, b_first, w_second, b_second, w_third, b_third, w_last)
    groups = lax.axis_size("coil")
    depth, parts, rows, lines = image.shape
    copies = jnp.broadcast_to(image[:, :, :, None], (depth, parts, rows, groups, lines))
    copies = copies.reshape(depth, parts, rows * groups, lines)
    planes_in = lax.all_to_all(copies, ("slab", "coil"), split_axis=2, concat_axis=0, tiled=True)
    planes = jnp.transpose(planes_in, (1, 2, 3, 0))
    partial_sum = coil_adjoint(planes, sens, measured, mask)
    by_depth = jnp.transpose(partial_sum, (3, 0, 1, 2)).astype(jnp.bfloat16)
    by_device = lax.all_to_all(by_depth, ("slab", "coil"), split_axis=0, concat_axis=2, tiled=True)
    by_device = by_device.astype(jnp.float32).reshape(depth, parts, rows, groups, lines)
    gradient = jnp.sum(by_device, axis=3)
    return image + STEP_SIZE * (score_field - gradient) + noise


def solution(mesh):
    in_specs = (
        P(("slab", "coil"), None, None, None),
        P(("slab", "coil"), None, None, None),
        P("coil", None, "slab", None, None),
        P("coil", None, "slab", None, None),
        P(),
        P(),
        P(),
        P(),
        P(),
        P(),
        P(),
        P(),
    )
    out_specs = P(("slab", "coil"), None, None, None)
    return jax.shard_map(
        on_device, mesh=mesh, in_specs=in_specs, out_specs=out_specs, check_vma=False
    )
```

```python
import jax
import jax.numpy as jnp
from jax import lax
from jax.sharding import PartitionSpec as P
from jax.experimental import pallas as pl
from jax.experimental.pallas import tpu as pltpu

STEP_SIZE = 0.5


def with_halo(shard, sides, width):
    for axis, dim in sides:
        devices, length = (lax.axis_size(axis), shard.shape[dim])
        up = [(i, (i + 1) % devices) for i in range(devices - 1)]
        down = [(j, i) for i, j in up]
        last = lax.slice_in_dim(shard, length - width, length, axis=dim)
        first = lax.slice_in_dim(shard, 0, width, axis=dim)
        before = lax.ppermute(last, axis, up)
        after = lax.ppermute(first, axis, down)
        shard = jnp.concatenate([before, shard, after], axis=dim)
    return shard


def dft_tables(length):
    line_index = jnp.arange(length, dtype=jnp.int32)
    phase_turns = line_index[:, None] * line_index[None, :] % length
    phase_angle = phase_turns.astype(jnp.float32) * (2.0 * jnp.pi / length)
    norm_scale = 1.0 / jnp.sqrt(jnp.float32(length))
    return (
        (jnp.cos(phase_angle) * norm_scale).astype(jnp.bfloat16),
        (jnp.sin(phase_angle) * norm_scale).astype(jnp.bfloat16),
    )


def along_y(values, table):
    return jnp.einsum("...yz,yk->...kz", values, table, preferred_element_type=jnp.float32)


def along_z(values, table):
    return jnp.einsum("...z,zk->...k", values, table, preferred_element_type=jnp.float32)


def spectrum(real_part, imag_part, cos_y, sin_y, cos_z, sin_z, forward):
    sign = 1.0 if forward else -1.0
    out_real = (along_y(real_part, cos_y) + sign * along_y(imag_part, sin_y)).astype(jnp.bfloat16)
    out_imag = (along_y(imag_part, cos_y) - sign * along_y(real_part, sin_y)).astype(jnp.bfloat16)
    last_real = along_z(out_real, cos_z) + sign * along_z(out_imag, sin_z)
    last_imag = along_z(out_imag, cos_z) - sign * along_z(out_real, sin_z)
    return (last_real, last_imag)


def adjoint_kernel(planes_ref, sens_ref, meas_ref, mask_ref, ty_ref, tz_ref, out_ref):
    ny = planes_ref.shape[1]
    nz = planes_ref.shape[2]

    @pl.when(pl.program_id(0) == 0)
    def _():
        out_ref[...] = jnp.zeros_like(out_ref)

    ty = ty_ref[...]
    tz = tz_ref[...]
    sens_real = sens_ref[0].astype(jnp.float32)
    sens_imag = sens_ref[1].astype(jnp.float32)
    image_real = planes_ref[0]
    image_imag = planes_ref[1]
    coil_real = (sens_real * image_real - sens_imag * image_imag).astype(jnp.bfloat16)
    coil_imag = (sens_real * image_imag + sens_imag * image_real).astype(jnp.bfloat16)
    half = jnp.dot(ty, jnp.concatenate([coil_real, coil_imag], axis=1), preferred_element_type=jnp.float32)
    half_real = (half[:ny, :nz] + half[ny:, nz:]).astype(jnp.bfloat16)
    half_imag = (half[:ny, nz:] - half[ny:, :nz]).astype(jnp.bfloat16)
    full = jnp.dot(jnp.concatenate([half_real, half_imag], axis=0), tz, preferred_element_type=jnp.float32)
    spec_real = full[:ny, :nz] + full[ny:, nz:]
    spec_imag = full[ny:, :nz] - full[:ny, nz:]
    sampled = mask_ref[...].astype(jnp.float32)
    miss_real = (sampled * (spec_real - meas_ref[0].astype(jnp.float32))).astype(jnp.bfloat16)
    miss_imag = (sampled * (spec_imag - meas_ref[1].astype(jnp.float32))).astype(jnp.bfloat16)
    half = jnp.dot(ty, jnp.concatenate([miss_real, miss_imag], axis=1), preferred_element_type=jnp.float32)
    back_real = (half[:ny, :nz] - half[ny:, nz:]).astype(jnp.bfloat16)
    back_imag = (half[:ny, nz:] + half[ny:, :nz]).astype(jnp.bfloat16)
    full = jnp.dot(jnp.concatenate([back_real, back_imag], axis=0), tz, preferred_element_type=jnp.float32)
    grad_real = full[:ny, :nz] - full[ny:, nz:]
    grad_imag = full[ny:, :nz] + full[:ny, nz:]
    out_ref[0] += sens_real * grad_real + sens_imag * grad_imag
    out_ref[1] += sens_real * grad_imag - sens_imag * grad_real


def coil_adjoint(planes, sens, measured, mask):
    ny = planes.shape[2]
    nz = planes.shape[3]
    cos_y, sin_y = dft_tables(ny)
    cos_z, sin_z = dft_tables(nz)
    ty = jnp.concatenate([cos_y, sin_y], axis=0)
    tz = jnp.concatenate([cos_z, sin_z], axis=1)
    coils = sens.shape[0]
    return pl.pallas_call(
        adjoint_kernel,
        grid=(coils,),
        in_specs=[
            pl.BlockSpec((2, None, ny, nz), lambda c: (0, 0, 0, 0)),
            pl.BlockSpec((None, 2, None, ny, nz), lambda c: (c, 0, 0, 0, 0)),
            pl.BlockSpec((None, 2, None, ny, nz), lambda c: (c, 0, 0, 0, 0)),
            pl.BlockSpec((ny, nz), lambda c: (0, 0)),
            pl.BlockSpec((2 * ny, ny), lambda c: (0, 0)),
            pl.BlockSpec((nz, 2 * nz), lambda c: (0, 0)),
        ],
        out_specs=pl.BlockSpec((2, None, ny, nz), lambda c: (0, 0, 0, 0)),
        out_shape=jax.ShapeDtypeStruct(planes.shape, jnp.float32),
    )(planes, sens, measured, mask, ty, tz)


def net_kernel(x_ref, p_ref, q_ref):
    width = p_ref.shape[1] // 4
    taps_in = x_ref.shape[1]
    rows = x_ref.shape[2]
    cols = x_ref.shape[3]
    outs = q_ref.shape[2]
    x = jnp.concatenate([x_ref[0, :, row, :] for row in range(rows)], axis=1)
    w1 = p_ref[:width, 0:taps_in].astype(jnp.bfloat16)
    w2 = p_ref[:width, width : 2 * width].astype(jnp.bfloat16)
    w3 = p_ref[:width, 2 * width : 3 * width].astype(jnp.bfloat16)
    wl = p_ref[width : width + outs, 0:width].astype(jnp.bfloat16)
    b1 = p_ref[:width, 3 * width : 3 * width + 1]
    b2 = p_ref[:width, 3 * width + 1 : 3 * width + 2]
    b3 = p_ref[:width, 3 * width + 2 : 3 * width + 3]
    h = jnp.dot(w1, x, preferred_element_type=jnp.float32) + b1
    h = jax.nn.silu(h).astype(jnp.bfloat16)
    h = jnp.dot(w2, h, preferred_element_type=jnp.float32) + b2
    h = jax.nn.silu(h).astype(jnp.bfloat16)
    h = jnp.dot(w3, h, preferred_element_type=jnp.float32) + b3
    h = jax.nn.silu(h).astype(jnp.bfloat16)
    q = jnp.dot(wl, h, preferred_element_type=jnp.float32)
    for row in range(rows):
        q_ref[0, row] = q[:, row * cols : (row + 1) * cols]


def score_net(window, w_first, b_first, w_second, b_second, w_third, b_third, w_last):
    slice_count = window.shape[0] - 4
    row_count = window.shape[2]
    col_count = window.shape[3]
    width = w_first.shape[-1]
    stacked = jnp.concatenate(
        [window[offset : offset + slice_count] for offset in range(5)], axis=1
    )
    framed = jnp.pad(stacked, ((0, 0), (0, 0), (1, 1), (1, 1)))
    columns = jnp.concatenate(
        [
            framed[:, :, shift_x : shift_x + row_count, shift_y : shift_y + col_count]
            for shift_x in range(3)
            for shift_y in range(3)
        ],
        axis=1,
    )
    taps_in = columns.shape[1]
    wl = w_last.reshape(-1, width)
    outs = wl.shape[0]
    top = jnp.concatenate(
        [
            jnp.pad(w_first.reshape(taps_in, width).T, ((0, 0), (0, width - taps_in))).astype(jnp.float32),
            w_second.T.astype(jnp.float32),
            w_third.T.astype(jnp.float32),
            jnp.pad(
                jnp.stack([b_first, b_second, b_third], axis=1),
                ((0, 0), (0, width - 3)),
            ),
        ],
        axis=1,
    ).astype(jnp.float32)
    bottom = jnp.pad(wl.astype(jnp.float32), ((0, -(-outs // 8) * 8 - outs), (0, 3 * width)))
    packed = jnp.concatenate([top, bottom], axis=0)
    rows = 16
    q = pl.pallas_call(
        net_kernel,
        grid=(slice_count, row_count // rows),
        in_specs=[
            pl.BlockSpec((1, taps_in, rows, col_count), lambda z, n: (z, 0, n, 0)),
            pl.BlockSpec(packed.shape, lambda z, n: (0, 0)),
        ],
        out_specs=pl.BlockSpec((1, rows, outs, col_count), lambda z, n: (z, n, 0, 0)),
        out_shape=jax.ShapeDtypeStruct((slice_count, row_count, outs, col_count), jnp.float32),
    )(columns, packed)
    q = jnp.pad(q, ((0, 0), (1, 1), (0, 0), (1, 1)))
    score_field = jnp.zeros((slice_count, row_count, 2, col_count), jnp.float32)
    for shift_x in range(3):
        for shift_y in range(3):
            tap = (shift_x * 3 + shift_y) * 2
            score_field = score_field + q[
                :, shift_x : shift_x + row_count, tap : tap + 2, shift_y : shift_y + col_count
            ]
    return jnp.transpose(score_field, (0, 2, 1, 3))


def slab_slices(image):
    return lax.all_gather(image, "coil", axis=0, tiled=True)


def on_device(
    image,
    noise,
    sens,
    measured,
    mask,
    w_first,
    b_first,
    w_second,
    b_second,
    w_third,
    b_third,
    w_last,
):
    window = with_halo(image.astype(jnp.bfloat16), ((("slab", "coil"), 0),), 2)
    score_field = score_net(window, w_first, b_first, w_second, b_second, w_third, b_third, w_last)
    groups = lax.axis_size("coil")
    depth, parts, rows, lines = image.shape
    copies = jnp.broadcast_to(image.astype(jnp.bfloat16)[:, :, :, None], (depth, parts, rows, groups, lines))
    copies = copies.reshape(depth, parts, rows * groups, lines)
    planes_in = lax.all_to_all(copies, ("slab", "coil"), split_axis=2, concat_axis=0, tiled=True)
    planes = jnp.transpose(planes_in, (1, 2, 3, 0)).astype(jnp.float32)
    partial_sum = coil_adjoint(planes, sens, measured, mask)
    by_depth = jnp.transpose(partial_sum, (3, 0, 1, 2)).astype(jnp.bfloat16)
    by_device = lax.all_to_all(by_depth, ("slab", "coil"), split_axis=0, concat_axis=2, tiled=True)
    by_device = by_device.astype(jnp.float32).reshape(depth, parts, rows, groups, lines)
    gradient = jnp.sum(by_device, axis=3)
    return image + STEP_SIZE * (score_field - gradient) + noise


def solution(mesh):
    in_specs = (
        P(("slab", "coil"), None, None, None),
        P(("slab", "coil"), None, None, None),
        P("coil", None, "slab", None, None),
        P("coil", None, "slab", None, None),
        P(),
        P(),
        P(),
        P(),
        P(),
        P(),
        P(),
        P(),
    )
    out_specs = P(("slab", "coil"), None, None, None)
    return jax.shard_map(
        on_device, mesh=mesh, in_specs=in_specs, out_specs=out_specs, check_vma=False
    )
```

```python
import ml_dtypes
import numpy as np
import jax
import jax.numpy as jnp
from jax import lax
from jax.sharding import PartitionSpec as P
from jax.experimental import pallas as pl
from jax.experimental.pallas import tpu as pltpu

STEP_SIZE = 0.5


def with_halo(shard, sides, width):
    for axis, dim in sides:
        devices, length = (lax.axis_size(axis), shard.shape[dim])
        up = [(i, (i + 1) % devices) for i in range(devices - 1)]
        down = [(j, i) for i, j in up]
        last = lax.slice_in_dim(shard, length - width, length, axis=dim)
        first = lax.slice_in_dim(shard, 0, width, axis=dim)
        before = lax.ppermute(last, axis, up)
        after = lax.ppermute(first, axis, down)
        shard = jnp.concatenate([before, shard, after], axis=dim)
    return shard


def dft_tables(length):
    line_index = np.arange(length, dtype=np.int64)
    phase_turns = line_index[:, None] * line_index[None, :] % length
    phase_angle = phase_turns.astype(np.float32) * np.float32(2.0 * np.pi / length)
    norm_scale = np.float32(1.0) / np.sqrt(np.float32(length))
    return (
        (np.cos(phase_angle) * norm_scale).astype(ml_dtypes.bfloat16),
        (np.sin(phase_angle) * norm_scale).astype(ml_dtypes.bfloat16),
    )


def along_y(values, table):
    return jnp.einsum("...yz,yk->...kz", values, table, preferred_element_type=jnp.float32)


def along_z(values, table):
    return jnp.einsum("...z,zk->...k", values, table, preferred_element_type=jnp.float32)


def spectrum(real_part, imag_part, cos_y, sin_y, cos_z, sin_z, forward):
    sign = 1.0 if forward else -1.0
    out_real = (along_y(real_part, cos_y) + sign * along_y(imag_part, sin_y)).astype(jnp.bfloat16)
    out_imag = (along_y(imag_part, cos_y) - sign * along_y(real_part, sin_y)).astype(jnp.bfloat16)
    last_real = along_z(out_real, cos_z) + sign * along_z(out_imag, sin_z)
    last_imag = along_z(out_imag, cos_z) - sign * along_z(out_real, sin_z)
    return (last_real, last_imag)


def adjoint_kernel(planes_ref, sens_ref, meas_ref, mask_ref, ty_ref, tz_ref, out_ref):
    ny = planes_ref.shape[1]
    nz = planes_ref.shape[2]

    @pl.when(pl.program_id(0) == 0)
    def _():
        out_ref[...] = jnp.zeros_like(out_ref)

    ty = ty_ref[...]
    tz = tz_ref[...]
    sens_real = sens_ref[0].astype(jnp.float32)
    sens_imag = sens_ref[1].astype(jnp.float32)
    image_real = planes_ref[0]
    image_imag = planes_ref[1]
    coil_real = (sens_real * image_real - sens_imag * image_imag).astype(jnp.bfloat16)
    coil_imag = (sens_real * image_imag + sens_imag * image_real).astype(jnp.bfloat16)
    half = jnp.dot(ty, jnp.concatenate([coil_real, coil_imag], axis=1), preferred_element_type=jnp.float32)
    half_real = (half[:ny, :nz] + half[ny:, nz:]).astype(jnp.bfloat16)
    half_imag = (half[:ny, nz:] - half[ny:, :nz]).astype(jnp.bfloat16)
    full = jnp.dot(jnp.concatenate([half_real, half_imag], axis=0), tz, preferred_element_type=jnp.float32)
    spec_real = full[:ny, :nz] + full[ny:, nz:]
    spec_imag = full[ny:, :nz] - full[:ny, nz:]
    sampled = mask_ref[...].astype(jnp.float32)
    miss_real = (sampled * (spec_real - meas_ref[0].astype(jnp.float32))).astype(jnp.bfloat16)
    miss_imag = (sampled * (spec_imag - meas_ref[1].astype(jnp.float32))).astype(jnp.bfloat16)
    half = jnp.dot(ty, jnp.concatenate([miss_real, miss_imag], axis=1), preferred_element_type=jnp.float32)
    back_real = (half[:ny, :nz] - half[ny:, nz:]).astype(jnp.bfloat16)
    back_imag = (half[:ny, nz:] + half[ny:, :nz]).astype(jnp.bfloat16)
    full = jnp.dot(jnp.concatenate([back_real, back_imag], axis=0), tz, preferred_element_type=jnp.float32)
    grad_real = full[:ny, :nz] - full[ny:, nz:]
    grad_imag = full[ny:, :nz] + full[:ny, nz:]
    out_ref[0] += sens_real * grad_real + sens_imag * grad_imag
    out_ref[1] += sens_real * grad_imag - sens_imag * grad_real


def coil_adjoint(planes, sens, measured, mask):
    ny = planes.shape[2]
    nz = planes.shape[3]
    cos_y, sin_y = dft_tables(ny)
    cos_z, sin_z = dft_tables(nz)
    ty = jnp.asarray(np.concatenate([cos_y, sin_y], axis=0))
    tz = jnp.asarray(np.concatenate([cos_z, sin_z], axis=1))
    coils = sens.shape[0]
    return pl.pallas_call(
        adjoint_kernel,
        grid=(coils,),
        in_specs=[
            pl.BlockSpec((2, None, ny, nz), lambda c: (0, 0, 0, 0)),
            pl.BlockSpec((None, 2, None, ny, nz), lambda c: (c, 0, 0, 0, 0)),
            pl.BlockSpec((None, 2, None, ny, nz), lambda c: (c, 0, 0, 0, 0)),
            pl.BlockSpec((ny, nz), lambda c: (0, 0)),
            pl.BlockSpec((2 * ny, ny), lambda c: (0, 0)),
            pl.BlockSpec((nz, 2 * nz), lambda c: (0, 0)),
        ],
        out_specs=pl.BlockSpec((2, None, ny, nz), lambda c: (0, 0, 0, 0)),
        out_shape=jax.ShapeDtypeStruct(planes.shape, jnp.float32),
    )(planes, sens, measured, mask, ty, tz)


def net_kernel(x_ref, p_ref, q_ref):
    width = p_ref.shape[1] // 4
    taps_in = x_ref.shape[1]
    rows = x_ref.shape[2]
    cols = x_ref.shape[3]
    outs = q_ref.shape[2]
    x = jnp.concatenate([x_ref[0, :, row, :] for row in range(rows)], axis=1)
    w1 = p_ref[:width, 0:taps_in].astype(jnp.bfloat16)
    w2 = p_ref[:width, width : 2 * width].astype(jnp.bfloat16)
    w3 = p_ref[:width, 2 * width : 3 * width].astype(jnp.bfloat16)
    wl = p_ref[width : width + outs, 0:width].astype(jnp.bfloat16)
    b1 = p_ref[:width, 3 * width : 3 * width + 1]
    b2 = p_ref[:width, 3 * width + 1 : 3 * width + 2]
    b3 = p_ref[:width, 3 * width + 2 : 3 * width + 3]
    h = jnp.dot(w1, x, preferred_element_type=jnp.float32) + b1
    h = jax.nn.silu(h).astype(jnp.bfloat16)
    h = jnp.dot(w2, h, preferred_element_type=jnp.float32) + b2
    h = jax.nn.silu(h).astype(jnp.bfloat16)
    h = jnp.dot(w3, h, preferred_element_type=jnp.float32) + b3
    h = jax.nn.silu(h).astype(jnp.bfloat16)
    q = jnp.dot(wl, h, preferred_element_type=jnp.float32)
    for row in range(rows):
        q_ref[0, row] = q[:, row * cols : (row + 1) * cols]


def score_net(window, w_first, b_first, w_second, b_second, w_third, b_third, w_last):
    slice_count = window.shape[0] - 4
    row_count = window.shape[2]
    col_count = window.shape[3]
    width = w_first.shape[-1]
    stacked = jnp.concatenate(
        [window[offset : offset + slice_count] for offset in range(5)], axis=1
    )
    framed = jnp.pad(stacked, ((0, 0), (0, 0), (1, 1), (1, 1)))
    columns = jnp.concatenate(
        [
            framed[:, :, shift_x : shift_x + row_count, shift_y : shift_y + col_count]
            for shift_x in range(3)
            for shift_y in range(3)
        ],
        axis=1,
    )
    taps_in = columns.shape[1]
    wl = w_last.reshape(-1, width)
    outs = wl.shape[0]
    top = jnp.concatenate(
        [
            jnp.pad(w_first.reshape(taps_in, width).T, ((0, 0), (0, width - taps_in))).astype(jnp.float32),
            w_second.T.astype(jnp.float32),
            w_third.T.astype(jnp.float32),
            jnp.pad(
                jnp.stack([b_first, b_second, b_third], axis=1),
                ((0, 0), (0, width - 3)),
            ),
        ],
        axis=1,
    ).astype(jnp.float32)
    bottom = jnp.pad(wl.astype(jnp.float32), ((0, -(-outs // 8) * 8 - outs), (0, 3 * width)))
    packed = jnp.concatenate([top, bottom], axis=0)
    rows = 16
    q = pl.pallas_call(
        net_kernel,
        grid=(slice_count, row_count // rows),
        in_specs=[
            pl.BlockSpec((1, taps_in, rows, col_count), lambda z, n: (z, 0, n, 0)),
            pl.BlockSpec(packed.shape, lambda z, n: (0, 0)),
        ],
        out_specs=pl.BlockSpec((1, rows, outs, col_count), lambda z, n: (z, n, 0, 0)),
        out_shape=jax.ShapeDtypeStruct((slice_count, row_count, outs, col_count), jnp.float32),
    )(columns, packed)
    q = jnp.pad(q, ((0, 0), (1, 1), (0, 0), (1, 1)))
    score_field = jnp.zeros((slice_count, row_count, 2, col_count), jnp.float32)
    for shift_x in range(3):
        for shift_y in range(3):
            tap = (shift_x * 3 + shift_y) * 2
            score_field = score_field + q[
                :, shift_x : shift_x + row_count, tap : tap + 2, shift_y : shift_y + col_count
            ]
    return jnp.transpose(score_field, (0, 2, 1, 3))


def slab_slices(image):
    return lax.all_gather(image, "coil", axis=0, tiled=True)


def on_device(
    image,
    noise,
    sens,
    measured,
    mask,
    w_first,
    b_first,
    w_second,
    b_second,
    w_third,
    b_third,
    w_last,
):
    window = with_halo(image.astype(jnp.bfloat16), ((("slab", "coil"), 0),), 2)
    score_field = score_net(window, w_first, b_first, w_second, b_second, w_third, b_third, w_last)
    groups = lax.axis_size("coil")
    depth, parts, rows, lines = image.shape
    copies = jnp.broadcast_to(image[:, :, :, None], (depth, parts, rows, groups, lines))
    copies = copies.reshape(depth, parts, rows * groups, lines)
    planes_in = lax.all_to_all(copies, ("slab", "coil"), split_axis=2, concat_axis=0, tiled=True)
    planes = jnp.transpose(planes_in, (1, 2, 3, 0))
    partial_sum = coil_adjoint(planes, sens, measured, mask)
    by_depth = jnp.transpose(partial_sum, (3, 0, 1, 2)).astype(jnp.bfloat16)
    by_device = lax.all_to_all(by_depth, ("slab", "coil"), split_axis=0, concat_axis=2, tiled=True)
    by_device = by_device.astype(jnp.float32).reshape(depth, parts, rows, groups, lines)
    gradient = jnp.sum(by_device, axis=3)
    return image + STEP_SIZE * (score_field - gradient) + noise


def solution(mesh):
    in_specs = (
        P(("slab", "coil"), None, None, None),
        P(("slab", "coil"), None, None, None),
        P("coil", None, "slab", None, None),
        P("coil", None, "slab", None, None),
        P(),
        P(),
        P(),
        P(),
        P(),
        P(),
        P(),
        P(),
    )
    out_specs = P(("slab", "coil"), None, None, None)
    return jax.shard_map(
        on_device, mesh=mesh, in_specs=in_specs, out_specs=out_specs, check_vma=False
    )
```

```python
import ml_dtypes
import numpy as np
import jax
import jax.numpy as jnp
from jax import lax
from jax.sharding import PartitionSpec as P
from jax.experimental import pallas as pl
from jax.experimental.pallas import tpu as pltpu

STEP_SIZE = 0.5


def with_halo(shard, sides, width):
    for axis, dim in sides:
        devices, length = (lax.axis_size(axis), shard.shape[dim])
        up = [(i, (i + 1) % devices) for i in range(devices - 1)]
        down = [(j, i) for i, j in up]
        last = lax.slice_in_dim(shard, length - width, length, axis=dim)
        first = lax.slice_in_dim(shard, 0, width, axis=dim)
        before = lax.ppermute(last, axis, up)
        after = lax.ppermute(first, axis, down)
        shard = jnp.concatenate([before, shard, after], axis=dim)
    return shard


def dft_tables(length):
    line_index = np.arange(length, dtype=np.int64)
    phase_turns = line_index[:, None] * line_index[None, :] % length
    phase_angle = phase_turns.astype(np.float32) * np.float32(2.0 * np.pi / length)
    norm_scale = np.float32(1.0) / np.sqrt(np.float32(length))
    return (
        (np.cos(phase_angle) * norm_scale).astype(ml_dtypes.bfloat16),
        (np.sin(phase_angle) * norm_scale).astype(ml_dtypes.bfloat16),
    )


def along_y(values, table):
    return jnp.einsum("...yz,yk->...kz", values, table, preferred_element_type=jnp.float32)


def along_z(values, table):
    return jnp.einsum("...z,zk->...k", values, table, preferred_element_type=jnp.float32)


def spectrum(real_part, imag_part, cos_y, sin_y, cos_z, sin_z, forward):
    sign = 1.0 if forward else -1.0
    out_real = (along_y(real_part, cos_y) + sign * along_y(imag_part, sin_y)).astype(jnp.bfloat16)
    out_imag = (along_y(imag_part, cos_y) - sign * along_y(real_part, sin_y)).astype(jnp.bfloat16)
    last_real = along_z(out_real, cos_z) + sign * along_z(out_imag, sin_z)
    last_imag = along_z(out_imag, cos_z) - sign * along_z(out_real, sin_z)
    return (last_real, last_imag)


def adjoint_kernel(planes_ref, sens_ref, meas_ref, mask_ref, ty_ref, tz_ref, out_ref):
    ny = planes_ref.shape[1]
    nz = planes_ref.shape[2]

    @pl.when(pl.program_id(0) == 0)
    def _():
        out_ref[...] = jnp.zeros_like(out_ref)

    ty = ty_ref[...]
    tz = tz_ref[...]
    sens_real = sens_ref[0].astype(jnp.float32)
    sens_imag = sens_ref[1].astype(jnp.float32)
    image_real = planes_ref[0]
    image_imag = planes_ref[1]
    coil_real = (sens_real * image_real - sens_imag * image_imag).astype(jnp.bfloat16)
    coil_imag = (sens_real * image_imag + sens_imag * image_real).astype(jnp.bfloat16)
    half = jnp.dot(ty, jnp.concatenate([coil_real, coil_imag], axis=1), preferred_element_type=jnp.float32)
    half_real = (half[:ny, :nz] + half[ny:, nz:]).astype(jnp.bfloat16)
    half_imag = (half[:ny, nz:] - half[ny:, :nz]).astype(jnp.bfloat16)
    full = jnp.dot(jnp.concatenate([half_real, half_imag], axis=0), tz, preferred_element_type=jnp.float32)
    spec_real = full[:ny, :nz] + full[ny:, nz:]
    spec_imag = full[ny:, :nz] - full[:ny, nz:]
    sampled = mask_ref[...].astype(jnp.float32)
    miss_real = (sampled * (spec_real - meas_ref[0].astype(jnp.float32))).astype(jnp.bfloat16)
    miss_imag = (sampled * (spec_imag - meas_ref[1].astype(jnp.float32))).astype(jnp.bfloat16)
    half = jnp.dot(ty, jnp.concatenate([miss_real, miss_imag], axis=1), preferred_element_type=jnp.float32)
    back_real = (half[:ny, :nz] - half[ny:, nz:]).astype(jnp.bfloat16)
    back_imag = (half[:ny, nz:] + half[ny:, :nz]).astype(jnp.bfloat16)
    full = jnp.dot(jnp.concatenate([back_real, back_imag], axis=0), tz, preferred_element_type=jnp.float32)
    grad_real = full[:ny, :nz] - full[ny:, nz:]
    grad_imag = full[ny:, :nz] + full[:ny, nz:]
    out_ref[0] += sens_real * grad_real + sens_imag * grad_imag
    out_ref[1] += sens_real * grad_imag - sens_imag * grad_real


def coil_adjoint(planes, sens, measured, mask):
    ny = planes.shape[2]
    nz = planes.shape[3]
    cos_y, sin_y = dft_tables(ny)
    cos_z, sin_z = dft_tables(nz)
    ty = jnp.asarray(np.concatenate([cos_y, sin_y], axis=0))
    tz = jnp.asarray(np.concatenate([cos_z, sin_z], axis=1))
    coils = sens.shape[0]
    return pl.pallas_call(
        adjoint_kernel,
        grid=(coils,),
        in_specs=[
            pl.BlockSpec((2, None, ny, nz), lambda c: (0, 0, 0, 0)),
            pl.BlockSpec((None, 2, None, ny, nz), lambda c: (c, 0, 0, 0, 0)),
            pl.BlockSpec((None, 2, None, ny, nz), lambda c: (c, 0, 0, 0, 0)),
            pl.BlockSpec((ny, nz), lambda c: (0, 0)),
            pl.BlockSpec((2 * ny, ny), lambda c: (0, 0)),
            pl.BlockSpec((nz, 2 * nz), lambda c: (0, 0)),
        ],
        out_specs=pl.BlockSpec((2, None, ny, nz), lambda c: (0, 0, 0, 0)),
        out_shape=jax.ShapeDtypeStruct(planes.shape, jnp.float32),
    )(planes, sens, measured, mask, ty, tz)


def net_kernel(x_ref, p_ref, q_ref):
    width = p_ref.shape[1] // 4
    taps_in = x_ref.shape[1]
    rows = x_ref.shape[2]
    cols = x_ref.shape[3]
    outs = q_ref.shape[1]
    x = jnp.concatenate([x_ref[0, :, row, :] for row in range(rows)], axis=1)
    w1 = p_ref[:width, 0:taps_in].astype(jnp.bfloat16)
    w2 = p_ref[:width, width : 2 * width].astype(jnp.bfloat16)
    w3 = p_ref[:width, 2 * width : 3 * width].astype(jnp.bfloat16)
    wl = p_ref[width : width + outs, 0:width].astype(jnp.bfloat16)
    b1 = p_ref[:width, 3 * width : 3 * width + 1]
    b2 = p_ref[:width, 3 * width + 1 : 3 * width + 2]
    b3 = p_ref[:width, 3 * width + 2 : 3 * width + 3]
    h = jnp.dot(w1, x, preferred_element_type=jnp.float32) + b1
    h = jax.nn.silu(h).astype(jnp.bfloat16)
    h = jnp.dot(w2, h, preferred_element_type=jnp.float32) + b2
    h = jax.nn.silu(h).astype(jnp.bfloat16)
    h = jnp.dot(w3, h, preferred_element_type=jnp.float32) + b3
    h = jax.nn.silu(h).astype(jnp.bfloat16)
    q = jnp.dot(wl, h, preferred_element_type=jnp.float32)
    for row in range(rows):
        q_ref[0, :, row, :] = q[:, row * cols : (row + 1) * cols]


def score_net(window, w_first, b_first, w_second, b_second, w_third, b_third, w_last):
    slice_count = window.shape[0] - 4
    row_count = window.shape[2]
    col_count = window.shape[3]
    width = w_first.shape[-1]
    stacked = jnp.concatenate(
        [window[offset : offset + slice_count] for offset in range(5)], axis=1
    )
    framed = jnp.pad(stacked, ((0, 0), (0, 0), (1, 1), (1, 1)))
    columns = jnp.concatenate(
        [
            framed[:, :, shift_x : shift_x + row_count, shift_y : shift_y + col_count]
            for shift_x in range(3)
            for shift_y in range(3)
        ],
        axis=1,
    )
    taps_in = columns.shape[1]
    wl = w_last.reshape(-1, width)
    outs = wl.shape[0]
    top = jnp.concatenate(
        [
            jnp.pad(w_first.reshape(taps_in, width).T, ((0, 0), (0, width - taps_in))).astype(jnp.float32),
            w_second.T.astype(jnp.float32),
            w_third.T.astype(jnp.float32),
            jnp.pad(
                jnp.stack([b_first, b_second, b_third], axis=1),
                ((0, 0), (0, width - 3)),
            ),
        ],
        axis=1,
    ).astype(jnp.float32)
    bottom = jnp.pad(wl.astype(jnp.float32), ((0, -(-outs // 8) * 8 - outs), (0, 3 * width)))
    packed = jnp.concatenate([top, bottom], axis=0)
    rows = 16
    q = pl.pallas_call(
        net_kernel,
        grid=(slice_count, row_count // rows),
        in_specs=[
            pl.BlockSpec((1, taps_in, rows, col_count), lambda z, n: (z, 0, n, 0)),
            pl.BlockSpec(packed.shape, lambda z, n: (0, 0)),
        ],
        out_specs=pl.BlockSpec((1, outs, rows, col_count), lambda z, n: (z, 0, n, 0)),
        out_shape=jax.ShapeDtypeStruct((slice_count, outs, row_count, col_count), jnp.float32),
    )(columns, packed)
    q = jnp.pad(q, ((0, 0), (0, 0), (1, 1), (1, 1)))
    score_field = jnp.zeros((slice_count, 2, row_count, col_count), jnp.float32)
    for shift_x in range(3):
        for shift_y in range(3):
            tap = (shift_x * 3 + shift_y) * 2
            score_field = score_field + q[
                :, tap : tap + 2, shift_x : shift_x + row_count, shift_y : shift_y + col_count
            ]
    return score_field


def slab_slices(image):
    return lax.all_gather(image, "coil", axis=0, tiled=True)


def on_device(
    image,
    noise,
    sens,
    measured,
    mask,
    w_first,
    b_first,
    w_second,
    b_second,
    w_third,
    b_third,
    w_last,
):
    window = with_halo(image.astype(jnp.bfloat16), ((("slab", "coil"), 0),), 2)
    score_field = score_net(window, w_first, b_first, w_second, b_second, w_third, b_third, w_last)
    groups = lax.axis_size("coil")
    depth, parts, rows, lines = image.shape
    copies = jnp.broadcast_to(image[:, :, :, None], (depth, parts, rows, groups, lines))
    copies = copies.reshape(depth, parts, rows * groups, lines)
    planes_in = lax.all_to_all(copies, ("slab", "coil"), split_axis=2, concat_axis=0, tiled=True)
    planes = jnp.transpose(planes_in, (1, 2, 3, 0))
    partial_sum = coil_adjoint(planes, sens, measured, mask)
    by_depth = jnp.transpose(partial_sum, (3, 0, 1, 2)).astype(jnp.bfloat16)
    by_device = lax.all_to_all(by_depth, ("slab", "coil"), split_axis=0, concat_axis=2, tiled=True)
    by_device = by_device.astype(jnp.float32).reshape(depth, parts, rows, groups, lines)
    gradient = jnp.sum(by_device, axis=3)
    return image + STEP_SIZE * (score_field - gradient) + noise


def solution(mesh):
    in_specs = (
        P(("slab", "coil"), None, None, None),
        P(("slab", "coil"), None, None, None),
        P("coil", None, "slab", None, None),
        P("coil", None, "slab", None, None),
        P(),
        P(),
        P(),
        P(),
        P(),
        P(),
        P(),
        P(),
    )
    out_specs = P(("slab", "coil"), None, None, None)
    return jax.shard_map(
        on_device, mesh=mesh, in_specs=in_specs, out_specs=out_specs, check_vma=False
    )
```

```python
import ml_dtypes
import numpy as np
import jax
import jax.numpy as jnp
from jax import lax
from jax.sharding import PartitionSpec as P
from jax.experimental import pallas as pl
from jax.experimental.pallas import tpu as pltpu

STEP_SIZE = 0.5


def with_halo(shard, sides, width):
    for axis, dim in sides:
        devices, length = (lax.axis_size(axis), shard.shape[dim])
        up = [(i, (i + 1) % devices) for i in range(devices - 1)]
        down = [(j, i) for i, j in up]
        last = lax.slice_in_dim(shard, length - width, length, axis=dim)
        first = lax.slice_in_dim(shard, 0, width, axis=dim)
        before = lax.ppermute(last, axis, up)
        after = lax.ppermute(first, axis, down)
        shard = jnp.concatenate([before, shard, after], axis=dim)
    return shard


def dft_tables(length):
    line_index = np.arange(length, dtype=np.int64)
    phase_turns = line_index[:, None] * line_index[None, :] % length
    phase_angle = phase_turns.astype(np.float32) * np.float32(2.0 * np.pi / length)
    norm_scale = np.float32(1.0) / np.sqrt(np.float32(length))
    return (
        (np.cos(phase_angle) * norm_scale).astype(ml_dtypes.bfloat16),
        (np.sin(phase_angle) * norm_scale).astype(ml_dtypes.bfloat16),
    )


def along_y(values, table):
    return jnp.einsum("...yz,yk->...kz", values, table, preferred_element_type=jnp.float32)


def along_z(values, table):
    return jnp.einsum("...z,zk->...k", values, table, preferred_element_type=jnp.float32)


def spectrum(real_part, imag_part, cos_y, sin_y, cos_z, sin_z, forward):
    sign = 1.0 if forward else -1.0
    out_real = (along_y(real_part, cos_y) + sign * along_y(imag_part, sin_y)).astype(jnp.bfloat16)
    out_imag = (along_y(imag_part, cos_y) - sign * along_y(real_part, sin_y)).astype(jnp.bfloat16)
    last_real = along_z(out_real, cos_z) + sign * along_z(out_imag, sin_z)
    last_imag = along_z(out_imag, cos_z) - sign * along_z(out_real, sin_z)
    return (last_real, last_imag)


def adjoint_kernel(planes_ref, sens_ref, meas_ref, mask_ref, ty_ref, tz_ref, out_ref):
    ny = planes_ref.shape[1]
    nz = planes_ref.shape[2]

    @pl.when(pl.program_id(0) == 0)
    def _():
        out_ref[...] = jnp.zeros_like(out_ref)

    ty = ty_ref[...]
    tz = tz_ref[...]
    sens_real = sens_ref[0].astype(jnp.float32)
    sens_imag = sens_ref[1].astype(jnp.float32)
    image_real = planes_ref[0]
    image_imag = planes_ref[1]
    coil_real = (sens_real * image_real - sens_imag * image_imag).astype(jnp.bfloat16)
    coil_imag = (sens_real * image_imag + sens_imag * image_real).astype(jnp.bfloat16)
    half = jnp.dot(ty, jnp.concatenate([coil_real, coil_imag], axis=1), preferred_element_type=jnp.float32)
    half_real = (half[:ny, :nz] + half[ny:, nz:]).astype(jnp.bfloat16)
    half_imag = (half[:ny, nz:] - half[ny:, :nz]).astype(jnp.bfloat16)
    full = jnp.dot(jnp.concatenate([half_real, half_imag], axis=0), tz, preferred_element_type=jnp.float32)
    spec_real = full[:ny, :nz] + full[ny:, nz:]
    spec_imag = full[ny:, :nz] - full[:ny, nz:]
    sampled = mask_ref[...].astype(jnp.float32)
    miss_real = (sampled * (spec_real - meas_ref[0].astype(jnp.float32))).astype(jnp.bfloat16)
    miss_imag = (sampled * (spec_imag - meas_ref[1].astype(jnp.float32))).astype(jnp.bfloat16)
    half = jnp.dot(ty, jnp.concatenate([miss_real, miss_imag], axis=1), preferred_element_type=jnp.float32)
    back_real = (half[:ny, :nz] - half[ny:, nz:]).astype(jnp.bfloat16)
    back_imag = (half[:ny, nz:] + half[ny:, :nz]).astype(jnp.bfloat16)
    full = jnp.dot(jnp.concatenate([back_real, back_imag], axis=0), tz, preferred_element_type=jnp.float32)
    grad_real = full[:ny, :nz] - full[ny:, nz:]
    grad_imag = full[ny:, :nz] + full[:ny, nz:]
    out_ref[0] += sens_real * grad_real + sens_imag * grad_imag
    out_ref[1] += sens_real * grad_imag - sens_imag * grad_real


def coil_adjoint(planes, sens, measured, mask):
    ny = planes.shape[2]
    nz = planes.shape[3]
    cos_y, sin_y = dft_tables(ny)
    cos_z, sin_z = dft_tables(nz)
    ty = jnp.asarray(np.concatenate([cos_y, sin_y], axis=0))
    tz = jnp.asarray(np.concatenate([cos_z, sin_z], axis=1))
    coils = sens.shape[0]
    return pl.pallas_call(
        adjoint_kernel,
        grid=(coils,),
        in_specs=[
            pl.BlockSpec((2, None, ny, nz), lambda c: (0, 0, 0, 0)),
            pl.BlockSpec((None, 2, None, ny, nz), lambda c: (c, 0, 0, 0, 0)),
            pl.BlockSpec((None, 2, None, ny, nz), lambda c: (c, 0, 0, 0, 0)),
            pl.BlockSpec((ny, nz), lambda c: (0, 0)),
            pl.BlockSpec((2 * ny, ny), lambda c: (0, 0)),
            pl.BlockSpec((nz, 2 * nz), lambda c: (0, 0)),
        ],
        out_specs=pl.BlockSpec((2, None, ny, nz), lambda c: (0, 0, 0, 0)),
        out_shape=jax.ShapeDtypeStruct(planes.shape, jnp.float32),
    )(planes, sens, measured, mask, ty, tz)


def net_kernel(x_ref, p_ref, q_ref):
    width = p_ref.shape[1] // 4
    taps_in = x_ref.shape[1]
    rows = x_ref.shape[2]
    cols = x_ref.shape[3]
    outs = q_ref.shape[1]
    x = jnp.concatenate([x_ref[0, :, row, :] for row in range(rows)], axis=1)
    w1 = p_ref[:width, 0:taps_in].astype(jnp.bfloat16)
    w2 = p_ref[:width, width : 2 * width].astype(jnp.bfloat16)
    w3 = p_ref[:width, 2 * width : 3 * width].astype(jnp.bfloat16)
    wl = p_ref[width : width + outs, 0:width].astype(jnp.bfloat16)
    b1 = p_ref[:width, 3 * width : 3 * width + 1]
    b2 = p_ref[:width, 3 * width + 1 : 3 * width + 2]
    b3 = p_ref[:width, 3 * width + 2 : 3 * width + 3]
    h = jnp.dot(w1, x, preferred_element_type=jnp.float32) + b1
    h = jax.nn.silu(h).astype(jnp.bfloat16)
    h = jnp.dot(w2, h, preferred_element_type=jnp.float32) + b2
    h = jax.nn.silu(h).astype(jnp.bfloat16)
    h = jnp.dot(w3, h, preferred_element_type=jnp.float32) + b3
    h = jax.nn.silu(h).astype(jnp.bfloat16)
    q = jnp.dot(wl, h, preferred_element_type=jnp.float32)
    for row in range(rows):
        q_ref[0, :, row, :] = q[:, row * cols : (row + 1) * cols]


def score_net(window, w_first, b_first, w_second, b_second, w_third, b_third, w_last, tie):
    slice_count = window.shape[0] - 4
    row_count = window.shape[2]
    col_count = window.shape[3]
    width = w_first.shape[-1]
    stacked = jnp.concatenate(
        [window[offset : offset + slice_count] for offset in range(5)], axis=1
    )
    framed = jnp.pad(stacked, ((0, 0), (0, 0), (1, 1), (1, 1)))
    columns = jnp.concatenate(
        [
            framed[:, :, shift_x : shift_x + row_count, shift_y : shift_y + col_count]
            for shift_x in range(3)
            for shift_y in range(3)
        ],
        axis=1,
    )
    taps_in = columns.shape[1]
    wl = w_last.reshape(-1, width)
    outs = wl.shape[0]
    top = jnp.concatenate(
        [
            jnp.pad(w_first.reshape(taps_in, width).T, ((0, 0), (0, width - taps_in))).astype(jnp.float32),
            w_second.T.astype(jnp.float32),
            w_third.T.astype(jnp.float32),
            jnp.pad(
                jnp.stack([b_first, b_second, b_third], axis=1),
                ((0, 0), (0, width - 3)),
            ),
        ],
        axis=1,
    ).astype(jnp.float32)
    bottom = jnp.pad(wl.astype(jnp.float32), ((0, -(-outs // 8) * 8 - outs), (0, 3 * width)))
    packed = jnp.concatenate([top, bottom], axis=0)
    rows = 16
    net_call = pl.pallas_call(
        net_kernel,
        grid=(1, row_count // rows),
        in_specs=[
            pl.BlockSpec((1, taps_in, rows, col_count), lambda z, n: (0, 0, n, 0)),
            pl.BlockSpec(packed.shape, lambda z, n: (0, 0)),
        ],
        out_specs=pl.BlockSpec((1, outs, rows, col_count), lambda z, n: (0, 0, n, 0)),
        out_shape=jax.ShapeDtypeStruct((1, outs, row_count, col_count), jnp.float32),
    )
    planes = []
    for depth in range(slice_count):
        plane = net_call(columns[depth : depth + 1], packed)
        if depth == 0:
            plane, tie = lax.optimization_barrier((plane, tie))
        planes.append(plane)
    q = jnp.concatenate(planes, axis=0)
    q = jnp.pad(q, ((0, 0), (0, 0), (1, 1), (1, 1)))
    score_field = jnp.zeros((slice_count, 2, row_count, col_count), jnp.float32)
    for shift_x in range(3):
        for shift_y in range(3):
            tap = (shift_x * 3 + shift_y) * 2
            score_field = score_field + q[
                :, tap : tap + 2, shift_x : shift_x + row_count, shift_y : shift_y + col_count
            ]
    return score_field, tie


def slab_slices(image):
    return lax.all_gather(image, "coil", axis=0, tiled=True)


def on_device(
    image,
    noise,
    sens,
    measured,
    mask,
    w_first,
    b_first,
    w_second,
    b_second,
    w_third,
    b_third,
    w_last,
):
    window = with_halo(image.astype(jnp.bfloat16), ((("slab", "coil"), 0),), 2)
    groups = lax.axis_size("coil")
    depth, parts, rows, lines = image.shape
    copies = jnp.broadcast_to(image[:, :, :, None], (depth, parts, rows, groups, lines))
    copies = copies.reshape(depth, parts, rows * groups, lines)
    planes_in = lax.all_to_all(copies, ("slab", "coil"), split_axis=2, concat_axis=0, tiled=True)
    score_field, planes_in = score_net(
        window, w_first, b_first, w_second, b_second, w_third, b_third, w_last, planes_in
    )
    planes = jnp.transpose(planes_in, (1, 2, 3, 0))
    partial_sum = coil_adjoint(planes, sens, measured, mask)
    by_depth = jnp.transpose(partial_sum, (3, 0, 1, 2)).astype(jnp.bfloat16)
    by_device = lax.all_to_all(by_depth, ("slab", "coil"), split_axis=0, concat_axis=2, tiled=True)
    by_device = by_device.astype(jnp.float32).reshape(depth, parts, rows, groups, lines)
    gradient = jnp.sum(by_device, axis=3)
    return image + STEP_SIZE * (score_field - gradient) + noise


def solution(mesh):
    in_specs = (
        P(("slab", "coil"), None, None, None),
        P(("slab", "coil"), None, None, None),
        P("coil", None, "slab", None, None),
        P("coil", None, "slab", None, None),
        P(),
        P(),
        P(),
        P(),
        P(),
        P(),
        P(),
        P(),
    )
    out_specs = P(("slab", "coil"), None, None, None)
    return jax.shard_map(
        on_device, mesh=mesh, in_specs=in_specs, out_specs=out_specs, check_vma=False
    )
```

```python
import ml_dtypes
import numpy as np
import jax
import jax.numpy as jnp
from jax import lax
from jax.sharding import PartitionSpec as P
from jax.experimental import pallas as pl
from jax.experimental.pallas import tpu as pltpu

STEP_SIZE = 0.5


def with_halo(shard, sides, width):
    for axis, dim in sides:
        devices, length = (lax.axis_size(axis), shard.shape[dim])
        up = [(i, (i + 1) % devices) for i in range(devices - 1)]
        down = [(j, i) for i, j in up]
        last = lax.slice_in_dim(shard, length - width, length, axis=dim)
        first = lax.slice_in_dim(shard, 0, width, axis=dim)
        before = lax.ppermute(last, axis, up)
        after = lax.ppermute(first, axis, down)
        shard = jnp.concatenate([before, shard, after], axis=dim)
    return shard


def dft_tables(length):
    line_index = np.arange(length, dtype=np.int64)
    phase_turns = line_index[:, None] * line_index[None, :] % length
    phase_angle = phase_turns.astype(np.float32) * np.float32(2.0 * np.pi / length)
    norm_scale = np.float32(1.0) / np.sqrt(np.float32(length))
    return (
        (np.cos(phase_angle) * norm_scale).astype(ml_dtypes.bfloat16),
        (np.sin(phase_angle) * norm_scale).astype(ml_dtypes.bfloat16),
    )


def along_y(values, table):
    return jnp.einsum("...yz,yk->...kz", values, table, preferred_element_type=jnp.float32)


def along_z(values, table):
    return jnp.einsum("...z,zk->...k", values, table, preferred_element_type=jnp.float32)


def spectrum(real_part, imag_part, cos_y, sin_y, cos_z, sin_z, forward):
    sign = 1.0 if forward else -1.0
    out_real = (along_y(real_part, cos_y) + sign * along_y(imag_part, sin_y)).astype(jnp.bfloat16)
    out_imag = (along_y(imag_part, cos_y) - sign * along_y(real_part, sin_y)).astype(jnp.bfloat16)
    last_real = along_z(out_real, cos_z) + sign * along_z(out_imag, sin_z)
    last_imag = along_z(out_imag, cos_z) - sign * along_z(out_real, sin_z)
    return (last_real, last_imag)


def adjoint_kernel(planes_ref, sens_ref, meas_ref, mask_ref, ty_ref, tz_ref, out_ref):
    ny = planes_ref.shape[1]
    nz = planes_ref.shape[2]

    @pl.when(pl.program_id(0) == 0)
    def _():
        out_ref[...] = jnp.zeros_like(out_ref)

    ty = ty_ref[...]
    tz = tz_ref[...]
    sens_real = sens_ref[0].astype(jnp.float32)
    sens_imag = sens_ref[1].astype(jnp.float32)
    image_real = planes_ref[0]
    image_imag = planes_ref[1]
    coil_real = (sens_real * image_real - sens_imag * image_imag).astype(jnp.bfloat16)
    coil_imag = (sens_real * image_imag + sens_imag * image_real).astype(jnp.bfloat16)
    half = jnp.dot(ty, jnp.concatenate([coil_real, coil_imag], axis=1), preferred_element_type=jnp.float32)
    half_real = (half[:ny, :nz] + half[ny:, nz:]).astype(jnp.bfloat16)
    half_imag = (half[:ny, nz:] - half[ny:, :nz]).astype(jnp.bfloat16)
    full = jnp.dot(jnp.concatenate([half_real, half_imag], axis=0), tz, preferred_element_type=jnp.float32)
    spec_real = full[:ny, :nz] + full[ny:, nz:]
    spec_imag = full[ny:, :nz] - full[:ny, nz:]
    sampled = mask_ref[...].astype(jnp.float32)
    miss_real = (sampled * (spec_real - meas_ref[0].astype(jnp.float32))).astype(jnp.bfloat16)
    miss_imag = (sampled * (spec_imag - meas_ref[1].astype(jnp.float32))).astype(jnp.bfloat16)
    half = jnp.dot(ty, jnp.concatenate([miss_real, miss_imag], axis=1), preferred_element_type=jnp.float32)
    back_real = (half[:ny, :nz] - half[ny:, nz:]).astype(jnp.bfloat16)
    back_imag = (half[:ny, nz:] + half[ny:, :nz]).astype(jnp.bfloat16)
    full = jnp.dot(jnp.concatenate([back_real, back_imag], axis=0), tz, preferred_element_type=jnp.float32)
    grad_real = full[:ny, :nz] - full[ny:, nz:]
    grad_imag = full[ny:, :nz] + full[:ny, nz:]
    out_ref[0] += sens_real * grad_real + sens_imag * grad_imag
    out_ref[1] += sens_real * grad_imag - sens_imag * grad_real


def coil_adjoint(planes, sens, measured, mask):
    ny = planes.shape[2]
    nz = planes.shape[3]
    cos_y, sin_y = dft_tables(ny)
    cos_z, sin_z = dft_tables(nz)
    ty = jnp.asarray(np.concatenate([cos_y, sin_y], axis=0))
    tz = jnp.asarray(np.concatenate([cos_z, sin_z], axis=1))
    coils = sens.shape[0]
    return pl.pallas_call(
        adjoint_kernel,
        grid=(coils,),
        in_specs=[
            pl.BlockSpec((2, None, ny, nz), lambda c: (0, 0, 0, 0)),
            pl.BlockSpec((None, 2, None, ny, nz), lambda c: (c, 0, 0, 0, 0)),
            pl.BlockSpec((None, 2, None, ny, nz), lambda c: (c, 0, 0, 0, 0)),
            pl.BlockSpec((ny, nz), lambda c: (0, 0)),
            pl.BlockSpec((2 * ny, ny), lambda c: (0, 0)),
            pl.BlockSpec((nz, 2 * nz), lambda c: (0, 0)),
        ],
        out_specs=pl.BlockSpec((2, None, ny, nz), lambda c: (0, 0, 0, 0)),
        out_shape=jax.ShapeDtypeStruct(planes.shape, jnp.float32),
    )(planes, sens, measured, mask, ty, tz)


def net_kernel(x_ref, p_ref, q_ref):
    width = p_ref.shape[1] // 4
    taps_in = x_ref.shape[1]
    rows = x_ref.shape[2]
    cols = x_ref.shape[3]
    outs = q_ref.shape[1]
    x = jnp.concatenate([x_ref[0, :, row, :] for row in range(rows)], axis=1)
    w1 = p_ref[:width, 0:taps_in].astype(jnp.bfloat16)
    w2 = p_ref[:width, width : 2 * width].astype(jnp.bfloat16)
    w3 = p_ref[:width, 2 * width : 3 * width].astype(jnp.bfloat16)
    wl = p_ref[width : width + outs, 0:width].astype(jnp.bfloat16)
    b1 = p_ref[:width, 3 * width : 3 * width + 1]
    b2 = p_ref[:width, 3 * width + 1 : 3 * width + 2]
    b3 = p_ref[:width, 3 * width + 2 : 3 * width + 3]
    h = jnp.dot(w1, x, preferred_element_type=jnp.float32) + b1
    h = jax.nn.silu(h).astype(jnp.bfloat16)
    h = jnp.dot(w2, h, preferred_element_type=jnp.float32) + b2
    h = jax.nn.silu(h).astype(jnp.bfloat16)
    h = jnp.dot(w3, h, preferred_element_type=jnp.float32) + b3
    h = jax.nn.silu(h).astype(jnp.bfloat16)
    q = jnp.dot(wl, h, preferred_element_type=jnp.float32)
    for row in range(rows):
        q_ref[0, :, row, :] = q[:, row * cols : (row + 1) * cols]


def score_net(window, w_first, b_first, w_second, b_second, w_third, b_third, w_last):
    slice_count = window.shape[0] - 4
    row_count = window.shape[2]
    col_count = window.shape[3]
    width = w_first.shape[-1]
    stacked = jnp.concatenate(
        [window[offset : offset + slice_count] for offset in range(5)], axis=1
    )
    framed = jnp.pad(stacked, ((0, 0), (0, 0), (1, 1), (1, 1)))
    columns = jnp.concatenate(
        [
            framed[:, :, shift_x : shift_x + row_count, shift_y : shift_y + col_count]
            for shift_x in range(3)
            for shift_y in range(3)
        ],
        axis=1,
    )
    taps_in = columns.shape[1]
    wl = w_last.reshape(-1, width)
    outs = wl.shape[0]
    top = jnp.concatenate(
        [
            jnp.pad(w_first.reshape(taps_in, width).T, ((0, 0), (0, width - taps_in))).astype(jnp.float32),
            w_second.T.astype(jnp.float32),
            w_third.T.astype(jnp.float32),
            jnp.pad(
                jnp.stack([b_first, b_second, b_third], axis=1),
                ((0, 0), (0, width - 3)),
            ),
        ],
        axis=1,
    ).astype(jnp.float32)
    bottom = jnp.pad(wl.astype(jnp.float32), ((0, -(-outs // 8) * 8 - outs), (0, 3 * width)))
    packed = jnp.concatenate([top, bottom], axis=0)
    rows = 16
    q = pl.pallas_call(
        net_kernel,
        grid=(slice_count, row_count // rows),
        in_specs=[
            pl.BlockSpec((1, taps_in, rows, col_count), lambda z, n: (z, 0, n, 0)),
            pl.BlockSpec(packed.shape, lambda z, n: (0, 0)),
        ],
        out_specs=pl.BlockSpec((1, outs, rows, col_count), lambda z, n: (z, 0, n, 0)),
        out_shape=jax.ShapeDtypeStruct((slice_count, outs, row_count, col_count), jnp.float32),
    )(columns, packed)
    q = jnp.pad(q, ((0, 0), (0, 0), (1, 1), (1, 1)))
    score_field = jnp.zeros((slice_count, 2, row_count, col_count), jnp.float32)
    for shift_x in range(3):
        for shift_y in range(3):
            tap = (shift_x * 3 + shift_y) * 2
            score_field = score_field + q[
                :, tap : tap + 2, shift_x : shift_x + row_count, shift_y : shift_y + col_count
            ]
    return score_field


def slab_slices(image):
    return lax.all_gather(image, "coil", axis=0, tiled=True)


def on_device(
    image,
    noise,
    sens,
    measured,
    mask,
    w_first,
    b_first,
    w_second,
    b_second,
    w_third,
    b_third,
    w_last,
):
    groups = lax.axis_size("coil")
    depth, parts, rows, lines = image.shape
    copies = jnp.broadcast_to(image[:, :, :, None], (depth, parts, rows, groups, lines))
    copies = copies.reshape(depth, parts, rows * groups, lines)
    planes_in = lax.all_to_all(copies, ("slab", "coil"), split_axis=2, concat_axis=0, tiled=True)
    planes_in, local = lax.optimization_barrier((planes_in, image))
    window = with_halo(local.astype(jnp.bfloat16), ((("slab", "coil"), 0),), 2)
    score_field = score_net(window, w_first, b_first, w_second, b_second, w_third, b_third, w_last)
    planes = jnp.transpose(planes_in, (1, 2, 3, 0))
    partial_sum = coil_adjoint(planes, sens, measured, mask)
    by_depth = jnp.transpose(partial_sum, (3, 0, 1, 2)).astype(jnp.bfloat16)
    by_device = lax.all_to_all(by_depth, ("slab", "coil"), split_axis=0, concat_axis=2, tiled=True)
    by_device = by_device.astype(jnp.float32).reshape(depth, parts, rows, groups, lines)
    gradient = jnp.sum(by_device, axis=3)
    return image + STEP_SIZE * (score_field - gradient) + noise


def solution(mesh):
    in_specs = (
        P(("slab", "coil"), None, None, None),
        P(("slab", "coil"), None, None, None),
        P("coil", None, "slab", None, None),
        P("coil", None, "slab", None, None),
        P(),
        P(),
        P(),
        P(),
        P(),
        P(),
        P(),
        P(),
    )
    out_specs = P(("slab", "coil"), None, None, None)
    return jax.shard_map(
        on_device, mesh=mesh, in_specs=in_specs, out_specs=out_specs, check_vma=False
    )
```

```python
import ml_dtypes
import numpy as np
import jax
import jax.numpy as jnp
from jax import lax
from jax.sharding import PartitionSpec as P
from jax.experimental import pallas as pl
from jax.experimental.pallas import tpu as pltpu

STEP_SIZE = 0.5


def with_halo(shard, sides, width):
    for axis, dim in sides:
        devices, length = (lax.axis_size(axis), shard.shape[dim])
        up = [(i, (i + 1) % devices) for i in range(devices - 1)]
        down = [(j, i) for i, j in up]
        last = lax.slice_in_dim(shard, length - width, length, axis=dim)
        first = lax.slice_in_dim(shard, 0, width, axis=dim)
        before = lax.ppermute(last, axis, up)
        after = lax.ppermute(first, axis, down)
        shard = jnp.concatenate([before, shard, after], axis=dim)
    return shard


def dft_tables(length):
    line_index = np.arange(length, dtype=np.int64)
    phase_turns = line_index[:, None] * line_index[None, :] % length
    phase_angle = phase_turns.astype(np.float32) * np.float32(2.0 * np.pi / length)
    norm_scale = np.float32(1.0) / np.sqrt(np.float32(length))
    return (
        (np.cos(phase_angle) * norm_scale).astype(ml_dtypes.bfloat16),
        (np.sin(phase_angle) * norm_scale).astype(ml_dtypes.bfloat16),
    )


def along_y(values, table):
    return jnp.einsum("...yz,yk->...kz", values, table, preferred_element_type=jnp.float32)


def along_z(values, table):
    return jnp.einsum("...z,zk->...k", values, table, preferred_element_type=jnp.float32)


def spectrum(real_part, imag_part, cos_y, sin_y, cos_z, sin_z, forward):
    sign = 1.0 if forward else -1.0
    out_real = (along_y(real_part, cos_y) + sign * along_y(imag_part, sin_y)).astype(jnp.bfloat16)
    out_imag = (along_y(imag_part, cos_y) - sign * along_y(real_part, sin_y)).astype(jnp.bfloat16)
    last_real = along_z(out_real, cos_z) + sign * along_z(out_imag, sin_z)
    last_imag = along_z(out_imag, cos_z) - sign * along_z(out_real, sin_z)
    return (last_real, last_imag)


def adjoint_kernel(planes_ref, sens_ref, meas_ref, mask_ref, ty_ref, tz_ref, out_ref):
    ny = planes_ref.shape[1]
    nz = planes_ref.shape[2]

    @pl.when(pl.program_id(0) == 0)
    def _():
        out_ref[...] = jnp.zeros_like(out_ref)

    ty = ty_ref[...]
    tz = tz_ref[...]
    sens_real = sens_ref[0].astype(jnp.float32)
    sens_imag = sens_ref[1].astype(jnp.float32)
    image_real = planes_ref[0]
    image_imag = planes_ref[1]
    coil_real = (sens_real * image_real - sens_imag * image_imag).astype(jnp.bfloat16)
    coil_imag = (sens_real * image_imag + sens_imag * image_real).astype(jnp.bfloat16)
    half = jnp.dot(ty, jnp.concatenate([coil_real, coil_imag], axis=1), preferred_element_type=jnp.float32)
    half_real = (half[:ny, :nz] + half[ny:, nz:]).astype(jnp.bfloat16)
    half_imag = (half[:ny, nz:] - half[ny:, :nz]).astype(jnp.bfloat16)
    full = jnp.dot(jnp.concatenate([half_real, half_imag], axis=0), tz, preferred_element_type=jnp.float32)
    spec_real = full[:ny, :nz] + full[ny:, nz:]
    spec_imag = full[ny:, :nz] - full[:ny, nz:]
    sampled = mask_ref[...].astype(jnp.float32)
    miss_real = (sampled * (spec_real - meas_ref[0].astype(jnp.float32))).astype(jnp.bfloat16)
    miss_imag = (sampled * (spec_imag - meas_ref[1].astype(jnp.float32))).astype(jnp.bfloat16)
    half = jnp.dot(ty, jnp.concatenate([miss_real, miss_imag], axis=1), preferred_element_type=jnp.float32)
    back_real = (half[:ny, :nz] - half[ny:, nz:]).astype(jnp.bfloat16)
    back_imag = (half[:ny, nz:] + half[ny:, :nz]).astype(jnp.bfloat16)
    full = jnp.dot(jnp.concatenate([back_real, back_imag], axis=0), tz, preferred_element_type=jnp.float32)
    grad_real = full[:ny, :nz] - full[ny:, nz:]
    grad_imag = full[ny:, :nz] + full[:ny, nz:]
    out_ref[0] += sens_real * grad_real + sens_imag * grad_imag
    out_ref[1] += sens_real * grad_imag - sens_imag * grad_real


def coil_adjoint(planes, sens, measured, mask):
    ny = planes.shape[2]
    nz = planes.shape[3]
    cos_y, sin_y = dft_tables(ny)
    cos_z, sin_z = dft_tables(nz)
    ty = jnp.asarray(np.concatenate([cos_y, sin_y], axis=0))
    tz = jnp.asarray(np.concatenate([cos_z, sin_z], axis=1))
    coils = sens.shape[0]
    return pl.pallas_call(
        adjoint_kernel,
        grid=(coils,),
        in_specs=[
            pl.BlockSpec((2, None, ny, nz), lambda c: (0, 0, 0, 0)),
            pl.BlockSpec((None, 2, None, ny, nz), lambda c: (c, 0, 0, 0, 0)),
            pl.BlockSpec((None, 2, None, ny, nz), lambda c: (c, 0, 0, 0, 0)),
            pl.BlockSpec((ny, nz), lambda c: (0, 0)),
            pl.BlockSpec((2 * ny, ny), lambda c: (0, 0)),
            pl.BlockSpec((nz, 2 * nz), lambda c: (0, 0)),
        ],
        out_specs=pl.BlockSpec((2, None, ny, nz), lambda c: (0, 0, 0, 0)),
        out_shape=jax.ShapeDtypeStruct(planes.shape, jnp.float32),
    )(planes, sens, measured, mask, ty, tz)


def net_kernel(x_ref, p_ref, q_ref):
    width = p_ref.shape[0] - 24
    taps_in = x_ref.shape[1]
    row_count = q_ref.shape[2]
    cols = q_ref.shape[3]
    outs = q_ref.shape[1]
    rows = 16
    w1 = [p_ref[:width, a * width : a * width + taps_in].astype(jnp.bfloat16) for a in range(3)]
    w2 = p_ref[:width, 3 * width : 4 * width].astype(jnp.bfloat16)
    w3 = p_ref[:width, 4 * width : 5 * width].astype(jnp.bfloat16)
    wl = p_ref[width : width + outs, 0:width].astype(jnp.bfloat16)
    b1 = p_ref[:width, 5 * width : 5 * width + 1]
    b2 = p_ref[:width, 5 * width + 1 : 5 * width + 2]
    b3 = p_ref[:width, 5 * width + 2 : 5 * width + 3]
    for chunk in range(row_count // rows):
        first = chunk * rows
        h = b1
        for a in range(3):
            x = jnp.concatenate([x_ref[0, :, first + row + a, :] for row in range(rows)], axis=1)
            h = h + jnp.dot(w1[a], x, preferred_element_type=jnp.float32)
        h = jax.nn.silu(h).astype(jnp.bfloat16)
        h = jnp.dot(w2, h, preferred_element_type=jnp.float32) + b2
        h = jax.nn.silu(h).astype(jnp.bfloat16)
        h = jnp.dot(w3, h, preferred_element_type=jnp.float32) + b3
        h = jax.nn.silu(h).astype(jnp.bfloat16)
        q = jnp.dot(wl, h, preferred_element_type=jnp.float32)
        for row in range(rows):
            q_ref[0, :, first + row, :] = q[:, row * cols : (row + 1) * cols]


def score_net(window, w_first, b_first, w_second, b_second, w_third, b_third, w_last):
    slice_count = window.shape[0] - 4
    row_count = window.shape[2]
    col_count = window.shape[3]
    width = w_first.shape[-1]
    stacked = jnp.concatenate(
        [window[offset : offset + slice_count] for offset in range(5)], axis=1
    )
    framed = jnp.pad(stacked, ((0, 0), (0, 0), (1, 1), (1, 1)))
    shifted = jnp.concatenate(
        [framed[:, :, :, shift_y : shift_y + col_count] for shift_y in range(3)], axis=1
    )
    taps_in = shifted.shape[1]
    wl = w_last.reshape(-1, width)
    outs = wl.shape[0]
    pad_to = lambda m: jnp.pad(m.astype(jnp.float32), ((0, 0), (0, width - m.shape[1])))
    top = jnp.concatenate(
        [pad_to(w_first[shift_x].reshape(taps_in, width).T) for shift_x in range(3)]
        + [
            pad_to(w_second.T),
            pad_to(w_third.T),
            pad_to(jnp.stack([b_first, b_second, b_third], axis=1)),
        ],
        axis=1,
    )
    bottom = jnp.pad(wl.astype(jnp.float32), ((0, 24 - outs), (0, 5 * width)))
    packed = jnp.concatenate([top, bottom], axis=0)
    q = pl.pallas_call(
        net_kernel,
        grid=(slice_count,),
        in_specs=[
            pl.BlockSpec((1,) + shifted.shape[1:], lambda z: (z, 0, 0, 0)),
            pl.BlockSpec(packed.shape, lambda z: (0, 0)),
        ],
        out_specs=pl.BlockSpec((1, outs, row_count, col_count), lambda z: (z, 0, 0, 0)),
        out_shape=jax.ShapeDtypeStruct((slice_count, outs, row_count, col_count), jnp.float32),
    )(shifted, packed)
    q = jnp.pad(q, ((0, 0), (0, 0), (1, 1), (1, 1)))
    score_field = jnp.zeros((slice_count, 2, row_count, col_count), jnp.float32)
    for shift_x in range(3):
        for shift_y in range(3):
            tap = (shift_x * 3 + shift_y) * 2
            score_field = score_field + q[
                :, tap : tap + 2, shift_x : shift_x + row_count, shift_y : shift_y + col_count
            ]
    return score_field


def slab_slices(image):
    return lax.all_gather(image, "coil", axis=0, tiled=True)


def on_device(
    image,
    noise,
    sens,
    measured,
    mask,
    w_first,
    b_first,
    w_second,
    b_second,
    w_third,
    b_third,
    w_last,
):
    window = with_halo(image.astype(jnp.bfloat16), ((("slab", "coil"), 0),), 2)
    score_field = score_net(window, w_first, b_first, w_second, b_second, w_third, b_third, w_last)
    groups = lax.axis_size("coil")
    depth, parts, rows, lines = image.shape
    copies = jnp.broadcast_to(image[:, :, :, None], (depth, parts, rows, groups, lines))
    copies = copies.reshape(depth, parts, rows * groups, lines)
    planes_in = lax.all_to_all(copies, ("slab", "coil"), split_axis=2, concat_axis=0, tiled=True)
    planes = jnp.transpose(planes_in, (1, 2, 3, 0))
    partial_sum = coil_adjoint(planes, sens, measured, mask)
    by_depth = jnp.transpose(partial_sum, (3, 0, 1, 2)).astype(jnp.bfloat16)
    by_device = lax.all_to_all(by_depth, ("slab", "coil"), split_axis=0, concat_axis=2, tiled=True)
    by_device = by_device.astype(jnp.float32).reshape(depth, parts, rows, groups, lines)
    gradient = jnp.sum(by_device, axis=3)
    return image + STEP_SIZE * (score_field - gradient) + noise


def solution(mesh):
    in_specs = (
        P(("slab", "coil"), None, None, None),
        P(("slab", "coil"), None, None, None),
        P("coil", None, "slab", None, None),
        P("coil", None, "slab", None, None),
        P(),
        P(),
        P(),
        P(),
        P(),
        P(),
        P(),
        P(),
    )
    out_specs = P(("slab", "coil"), None, None, None)
    return jax.shard_map(
        on_device, mesh=mesh, in_specs=in_specs, out_specs=out_specs, check_vma=False
    )
```

```python
import ml_dtypes
import numpy as np
import jax
import jax.numpy as jnp
from jax import lax
from jax.sharding import PartitionSpec as P
from jax.experimental import pallas as pl
from jax.experimental.pallas import tpu as pltpu

STEP_SIZE = 0.5


def with_halo(shard, sides, width):
    for axis, dim in sides:
        devices, length = (lax.axis_size(axis), shard.shape[dim])
        up = [(i, (i + 1) % devices) for i in range(devices - 1)]
        down = [(j, i) for i, j in up]
        last = lax.slice_in_dim(shard, length - width, length, axis=dim)
        first = lax.slice_in_dim(shard, 0, width, axis=dim)
        before = lax.ppermute(last, axis, up)
        after = lax.ppermute(first, axis, down)
        shard = jnp.concatenate([before, shard, after], axis=dim)
    return shard


def dft_tables(length):
    line_index = np.arange(length, dtype=np.int64)
    phase_turns = line_index[:, None] * line_index[None, :] % length
    phase_angle = phase_turns.astype(np.float32) * np.float32(2.0 * np.pi / length)
    norm_scale = np.float32(1.0) / np.sqrt(np.float32(length))
    return (
        (np.cos(phase_angle) * norm_scale).astype(ml_dtypes.bfloat16),
        (np.sin(phase_angle) * norm_scale).astype(ml_dtypes.bfloat16),
    )


def along_y(values, table):
    return jnp.einsum("...yz,yk->...kz", values, table, preferred_element_type=jnp.float32)


def along_z(values, table):
    return jnp.einsum("...z,zk->...k", values, table, preferred_element_type=jnp.float32)


def spectrum(real_part, imag_part, cos_y, sin_y, cos_z, sin_z, forward):
    sign = 1.0 if forward else -1.0
    out_real = (along_y(real_part, cos_y) + sign * along_y(imag_part, sin_y)).astype(jnp.bfloat16)
    out_imag = (along_y(imag_part, cos_y) - sign * along_y(real_part, sin_y)).astype(jnp.bfloat16)
    last_real = along_z(out_real, cos_z) + sign * along_z(out_imag, sin_z)
    last_imag = along_z(out_imag, cos_z) - sign * along_z(out_real, sin_z)
    return (last_real, last_imag)


def adjoint_kernel(planes_ref, sens_ref, meas_ref, mask_ref, ty_ref, tz_ref, out_ref):
    ny = planes_ref.shape[1]
    nz = planes_ref.shape[2]

    @pl.when(pl.program_id(0) == 0)
    def _():
        out_ref[...] = jnp.zeros_like(out_ref)

    ty = ty_ref[...]
    tz = tz_ref[...]
    sens_real = sens_ref[0].astype(jnp.float32)
    sens_imag = sens_ref[1].astype(jnp.float32)
    image_real = planes_ref[0]
    image_imag = planes_ref[1]
    coil_real = (sens_real * image_real - sens_imag * image_imag).astype(jnp.bfloat16)
    coil_imag = (sens_real * image_imag + sens_imag * image_real).astype(jnp.bfloat16)
    half = jnp.dot(ty, jnp.concatenate([coil_real, coil_imag], axis=1), preferred_element_type=jnp.float32)
    half_real = (half[:ny, :nz] + half[ny:, nz:]).astype(jnp.bfloat16)
    half_imag = (half[:ny, nz:] - half[ny:, :nz]).astype(jnp.bfloat16)
    full = jnp.dot(jnp.concatenate([half_real, half_imag], axis=0), tz, preferred_element_type=jnp.float32)
    spec_real = full[:ny, :nz] + full[ny:, nz:]
    spec_imag = full[ny:, :nz] - full[:ny, nz:]
    sampled = mask_ref[...].astype(jnp.float32)
    miss_real = (sampled * (spec_real - meas_ref[0].astype(jnp.float32))).astype(jnp.bfloat16)
    miss_imag = (sampled * (spec_imag - meas_ref[1].astype(jnp.float32))).astype(jnp.bfloat16)
    half = jnp.dot(ty, jnp.concatenate([miss_real, miss_imag], axis=1), preferred_element_type=jnp.float32)
    back_real = (half[:ny, :nz] - half[ny:, nz:]).astype(jnp.bfloat16)
    back_imag = (half[:ny, nz:] + half[ny:, :nz]).astype(jnp.bfloat16)
    full = jnp.dot(jnp.concatenate([back_real, back_imag], axis=0), tz, preferred_element_type=jnp.float32)
    grad_real = full[:ny, :nz] - full[ny:, nz:]
    grad_imag = full[ny:, :nz] + full[:ny, nz:]
    out_ref[0] += sens_real * grad_real + sens_imag * grad_imag
    out_ref[1] += sens_real * grad_imag - sens_imag * grad_real


def coil_adjoint(planes, sens, measured, mask):
    ny = planes.shape[2]
    nz = planes.shape[3]
    cos_y, sin_y = dft_tables(ny)
    cos_z, sin_z = dft_tables(nz)
    ty = jnp.asarray(np.concatenate([cos_y, sin_y], axis=0))
    tz = jnp.asarray(np.concatenate([cos_z, sin_z], axis=1))
    coils = sens.shape[0]
    return pl.pallas_call(
        adjoint_kernel,
        grid=(coils,),
        in_specs=[
            pl.BlockSpec((2, None, ny, nz), lambda c: (0, 0, 0, 0)),
            pl.BlockSpec((None, 2, None, ny, nz), lambda c: (c, 0, 0, 0, 0)),
            pl.BlockSpec((None, 2, None, ny, nz), lambda c: (c, 0, 0, 0, 0)),
            pl.BlockSpec((ny, nz), lambda c: (0, 0)),
            pl.BlockSpec((2 * ny, ny), lambda c: (0, 0)),
            pl.BlockSpec((nz, 2 * nz), lambda c: (0, 0)),
        ],
        out_specs=pl.BlockSpec((2, None, ny, nz), lambda c: (0, 0, 0, 0)),
        out_shape=jax.ShapeDtypeStruct(planes.shape, jnp.float32),
    )(planes, sens, measured, mask, ty, tz)


def net_kernel(x_ref, p_ref, q_ref):
    width = p_ref.shape[0] - 24
    taps_in = x_ref.shape[1]
    row_count = q_ref.shape[2]
    cols = q_ref.shape[3]
    outs = q_ref.shape[1]
    rows = 16
    w1 = [p_ref[:width, a * width : a * width + taps_in].astype(jnp.bfloat16) for a in range(3)]
    w2 = p_ref[:width, 3 * width : 4 * width].astype(jnp.bfloat16)
    w3 = p_ref[:width, 4 * width : 5 * width].astype(jnp.bfloat16)
    wl = p_ref[width : width + outs, 0:width].astype(jnp.bfloat16)
    b1 = p_ref[:width, 5 * width : 5 * width + 1]
    b2 = p_ref[:width, 5 * width + 1 : 5 * width + 2]
    b3 = p_ref[:width, 5 * width + 2 : 5 * width + 3]
    for chunk in range(row_count // rows):
        first = chunk * rows
        h = b1
        for a in range(3):
            x = jnp.concatenate([x_ref[0, :, first + row + a, :] for row in range(rows)], axis=1)
            h = h + jnp.dot(w1[a], x, preferred_element_type=jnp.float32)
        h = jax.nn.silu(h).astype(jnp.bfloat16)
        h = jnp.dot(w2, h, preferred_element_type=jnp.float32) + b2
        h = jax.nn.silu(h).astype(jnp.bfloat16)
        h = jnp.dot(w3, h, preferred_element_type=jnp.float32) + b3
        h = jax.nn.silu(h).astype(jnp.bfloat16)
        q = jnp.dot(wl, h, preferred_element_type=jnp.float32)
        for row in range(rows):
            q_ref[0, :, first + row, :] = q[:, row * cols : (row + 1) * cols]


def score_net(window, w_first, b_first, w_second, b_second, w_third, b_third, w_last):
    slice_count = window.shape[0] - 4
    row_count = window.shape[2]
    col_count = window.shape[3]
    width = w_first.shape[-1]
    stacked = jnp.concatenate(
        [window[offset : offset + slice_count] for offset in range(5)], axis=1
    )
    framed = jnp.pad(stacked, ((0, 0), (0, 0), (1, 1), (1, 1)))
    shifted = jnp.concatenate(
        [framed[:, :, :, shift_y : shift_y + col_count] for shift_y in range(3)], axis=1
    )
    taps_in = shifted.shape[1]
    wl = w_last.reshape(-1, width)
    outs = wl.shape[0]
    pad_to = lambda m: jnp.pad(m.astype(jnp.float32), ((0, 0), (0, width - m.shape[1])))
    top = jnp.concatenate(
        [pad_to(w_first[shift_x].reshape(taps_in, width).T) for shift_x in range(3)]
        + [
            pad_to(w_second.T),
            pad_to(w_third.T),
            pad_to(jnp.stack([b_first, b_second, b_third], axis=1)),
        ],
        axis=1,
    )
    bottom = jnp.pad(wl.astype(jnp.float32), ((0, 24 - outs), (0, 5 * width)))
    packed = jnp.concatenate([top, bottom], axis=0)
    q = pl.pallas_call(
        net_kernel,
        grid=(slice_count,),
        in_specs=[
            pl.BlockSpec((1,) + shifted.shape[1:], lambda z: (z, 0, 0, 0)),
            pl.BlockSpec(packed.shape, lambda z: (0, 0)),
        ],
        out_specs=pl.BlockSpec((1, outs, row_count, col_count), lambda z: (z, 0, 0, 0)),
        out_shape=jax.ShapeDtypeStruct((slice_count, outs, row_count, col_count), jnp.float32),
    )(shifted, packed)
    q = jnp.pad(q, ((0, 0), (0, 0), (1, 1), (1, 1)))
    score_field = jnp.zeros((slice_count, 2, row_count, col_count), jnp.float32)
    for shift_x in range(3):
        for shift_y in range(3):
            tap = (shift_x * 3 + shift_y) * 2
            score_field = score_field + q[
                :, tap : tap + 2, shift_x : shift_x + row_count, shift_y : shift_y + col_count
            ]
    return score_field


def slab_slices(image):
    return lax.all_gather(image, "coil", axis=0, tiled=True)


def on_device(
    image,
    noise,
    sens,
    measured,
    mask,
    w_first,
    b_first,
    w_second,
    b_second,
    w_third,
    b_third,
    w_last,
):
    window = with_halo(image.astype(jnp.bfloat16), ((("slab", "coil"), 0),), 2)
    score_field = score_net(window, w_first, b_first, w_second, b_second, w_third, b_third, w_last)
    groups = lax.axis_size("coil")
    depth, parts, rows, lines = image.shape
    copies = jnp.broadcast_to(image[:, :, :, None], (depth, parts, rows, groups, lines))
    copies = copies.reshape(depth, parts, rows * groups, lines)
    planes_in = lax.all_to_all(copies, ("slab", "coil"), split_axis=2, concat_axis=0, tiled=True)
    score_field, planes_in = lax.optimization_barrier((score_field, planes_in))
    planes = jnp.transpose(planes_in, (1, 2, 3, 0))
    partial_sum = coil_adjoint(planes, sens, measured, mask)
    by_depth = jnp.transpose(partial_sum, (3, 0, 1, 2)).astype(jnp.bfloat16)
    by_device = lax.all_to_all(by_depth, ("slab", "coil"), split_axis=0, concat_axis=2, tiled=True)
    by_device = by_device.astype(jnp.float32).reshape(depth, parts, rows, groups, lines)
    gradient = jnp.sum(by_device, axis=3)
    return image + STEP_SIZE * (score_field - gradient) + noise


def solution(mesh):
    in_specs = (
        P(("slab", "coil"), None, None, None),
        P(("slab", "coil"), None, None, None),
        P("coil", None, "slab", None, None),
        P("coil", None, "slab", None, None),
        P(),
        P(),
        P(),
        P(),
        P(),
        P(),
        P(),
        P(),
    )
    out_specs = P(("slab", "coil"), None, None, None)
    return jax.shard_map(
        on_device, mesh=mesh, in_specs=in_specs, out_specs=out_specs, check_vma=False
    )
```

```python
import ml_dtypes
import numpy as np
import jax
import jax.numpy as jnp
from jax import lax
from jax.sharding import PartitionSpec as P
from jax.experimental import pallas as pl
from jax.experimental.pallas import tpu as pltpu

STEP_SIZE = 0.5


def with_halo(shard, sides, width):
    for axis, dim in sides:
        devices, length = (lax.axis_size(axis), shard.shape[dim])
        up = [(i, (i + 1) % devices) for i in range(devices - 1)]
        down = [(j, i) for i, j in up]
        last = lax.slice_in_dim(shard, length - width, length, axis=dim)
        first = lax.slice_in_dim(shard, 0, width, axis=dim)
        before = lax.ppermute(last, axis, up)
        after = lax.ppermute(first, axis, down)
        shard = jnp.concatenate([before, shard, after], axis=dim)
    return shard


def dft_tables(length):
    line_index = np.arange(length, dtype=np.int64)
    phase_turns = line_index[:, None] * line_index[None, :] % length
    phase_angle = phase_turns.astype(np.float32) * np.float32(2.0 * np.pi / length)
    norm_scale = np.float32(1.0) / np.sqrt(np.float32(length))
    return (
        (np.cos(phase_angle) * norm_scale).astype(ml_dtypes.bfloat16),
        (np.sin(phase_angle) * norm_scale).astype(ml_dtypes.bfloat16),
    )


def along_y(values, table):
    return jnp.einsum("...yz,yk->...kz", values, table, preferred_element_type=jnp.float32)


def along_z(values, table):
    return jnp.einsum("...z,zk->...k", values, table, preferred_element_type=jnp.float32)


def spectrum(real_part, imag_part, cos_y, sin_y, cos_z, sin_z, forward):
    sign = 1.0 if forward else -1.0
    out_real = (along_y(real_part, cos_y) + sign * along_y(imag_part, sin_y)).astype(jnp.bfloat16)
    out_imag = (along_y(imag_part, cos_y) - sign * along_y(real_part, sin_y)).astype(jnp.bfloat16)
    last_real = along_z(out_real, cos_z) + sign * along_z(out_imag, sin_z)
    last_imag = along_z(out_imag, cos_z) - sign * along_z(out_real, sin_z)
    return (last_real, last_imag)


def adjoint_kernel(planes_ref, sens_ref, meas_ref, mask_ref, ty_ref, tz_ref, out_ref):
    ny = planes_ref.shape[1]
    nz = planes_ref.shape[2]

    @pl.when(pl.program_id(0) == 0)
    def _():
        out_ref[...] = jnp.zeros_like(out_ref)

    ty = ty_ref[...]
    tz = tz_ref[...]
    sens_real = sens_ref[0].astype(jnp.float32)
    sens_imag = sens_ref[1].astype(jnp.float32)
    image_real = planes_ref[0]
    image_imag = planes_ref[1]
    coil_real = (sens_real * image_real - sens_imag * image_imag).astype(jnp.bfloat16)
    coil_imag = (sens_real * image_imag + sens_imag * image_real).astype(jnp.bfloat16)
    half = jnp.dot(ty, jnp.concatenate([coil_real, coil_imag], axis=1), preferred_element_type=jnp.float32)
    half_real = (half[:ny, :nz] + half[ny:, nz:]).astype(jnp.bfloat16)
    half_imag = (half[:ny, nz:] - half[ny:, :nz]).astype(jnp.bfloat16)
    full = jnp.dot(jnp.concatenate([half_real, half_imag], axis=0), tz, preferred_element_type=jnp.float32)
    spec_real = full[:ny, :nz] + full[ny:, nz:]
    spec_imag = full[ny:, :nz] - full[:ny, nz:]
    sampled = mask_ref[...].astype(jnp.float32)
    miss_real = (sampled * (spec_real - meas_ref[0].astype(jnp.float32))).astype(jnp.bfloat16)
    miss_imag = (sampled * (spec_imag - meas_ref[1].astype(jnp.float32))).astype(jnp.bfloat16)
    half = jnp.dot(ty, jnp.concatenate([miss_real, miss_imag], axis=1), preferred_element_type=jnp.float32)
    back_real = (half[:ny, :nz] - half[ny:, nz:]).astype(jnp.bfloat16)
    back_imag = (half[:ny, nz:] + half[ny:, :nz]).astype(jnp.bfloat16)
    full = jnp.dot(jnp.concatenate([back_real, back_imag], axis=0), tz, preferred_element_type=jnp.float32)
    grad_real = full[:ny, :nz] - full[ny:, nz:]
    grad_imag = full[ny:, :nz] + full[:ny, nz:]
    out_ref[0] += sens_real * grad_real + sens_imag * grad_imag
    out_ref[1] += sens_real * grad_imag - sens_imag * grad_real


def coil_adjoint(planes, sens, measured, mask):
    ny = planes.shape[2]
    nz = planes.shape[3]
    cos_y, sin_y = dft_tables(ny)
    cos_z, sin_z = dft_tables(nz)
    ty = jnp.asarray(np.concatenate([cos_y, sin_y], axis=0))
    tz = jnp.asarray(np.concatenate([cos_z, sin_z], axis=1))
    coils = sens.shape[0]
    return pl.pallas_call(
        adjoint_kernel,
        grid=(coils,),
        in_specs=[
            pl.BlockSpec((2, None, ny, nz), lambda c: (0, 0, 0, 0)),
            pl.BlockSpec((None, 2, None, ny, nz), lambda c: (c, 0, 0, 0, 0)),
            pl.BlockSpec((None, 2, None, ny, nz), lambda c: (c, 0, 0, 0, 0)),
            pl.BlockSpec((ny, nz), lambda c: (0, 0)),
            pl.BlockSpec((2 * ny, ny), lambda c: (0, 0)),
            pl.BlockSpec((nz, 2 * nz), lambda c: (0, 0)),
        ],
        out_specs=pl.BlockSpec((2, None, ny, nz), lambda c: (0, 0, 0, 0)),
        out_shape=jax.ShapeDtypeStruct(planes.shape, jnp.float32),
    )(planes, sens, measured, mask, ty, tz)


def net_kernel(x_ref, p_ref, q_ref):
    width = p_ref.shape[0] - 24
    taps_in = x_ref.shape[1]
    row_count = q_ref.shape[2]
    cols = q_ref.shape[3]
    outs = q_ref.shape[1]
    rows = 16
    w1 = [p_ref[:width, a * width : a * width + taps_in].astype(jnp.bfloat16) for a in range(3)]
    w2 = p_ref[:width, 3 * width : 4 * width].astype(jnp.bfloat16)
    w3 = p_ref[:width, 4 * width : 5 * width].astype(jnp.bfloat16)
    wl = p_ref[width : width + outs, 0:width].astype(jnp.bfloat16)
    b1 = p_ref[:width, 5 * width : 5 * width + 1]
    b2 = p_ref[:width, 5 * width + 1 : 5 * width + 2]
    b3 = p_ref[:width, 5 * width + 2 : 5 * width + 3]
    for chunk in range(row_count // rows):
        first = chunk * rows
        h = b1
        for a in range(3):
            x = jnp.concatenate([x_ref[0, :, first + row + a, :] for row in range(rows)], axis=1)
            h = h + jnp.dot(w1[a], x, preferred_element_type=jnp.float32)
        h = jax.nn.silu(h).astype(jnp.bfloat16)
        h = jnp.dot(w2, h, preferred_element_type=jnp.float32) + b2
        h = jax.nn.silu(h).astype(jnp.bfloat16)
        h = jnp.dot(w3, h, preferred_element_type=jnp.float32) + b3
        h = jax.nn.silu(h).astype(jnp.bfloat16)
        q = jnp.dot(wl, h, preferred_element_type=jnp.float32)
        for row in range(rows):
            q_ref[0, :, first + row, :] = q[:, row * cols : (row + 1) * cols]


def score_net(window, w_first, b_first, w_second, b_second, w_third, b_third, w_last):
    slice_count = window.shape[0] - 4
    row_count = window.shape[2]
    col_count = window.shape[3]
    width = w_first.shape[-1]
    stacked = jnp.concatenate(
        [window[offset : offset + slice_count] for offset in range(5)], axis=1
    )
    framed = jnp.pad(stacked, ((0, 0), (0, 0), (1, 1), (1, 1)))
    shifted = jnp.concatenate(
        [framed[:, :, :, shift_y : shift_y + col_count] for shift_y in range(3)], axis=1
    )
    taps_in = shifted.shape[1]
    wl = w_last.reshape(-1, width)
    outs = wl.shape[0]
    pad_to = lambda m: jnp.pad(m.astype(jnp.float32), ((0, 0), (0, width - m.shape[1])))
    top = jnp.concatenate(
        [pad_to(w_first[shift_x].reshape(taps_in, width).T) for shift_x in range(3)]
        + [
            pad_to(w_second.T),
            pad_to(w_third.T),
            pad_to(jnp.stack([b_first, b_second, b_third], axis=1)),
        ],
        axis=1,
    )
    bottom = jnp.pad(wl.astype(jnp.float32), ((0, 24 - outs), (0, 5 * width)))
    packed = jnp.concatenate([top, bottom], axis=0)
    q = pl.pallas_call(
        net_kernel,
        grid=(slice_count,),
        in_specs=[
            pl.BlockSpec((1,) + shifted.shape[1:], lambda z: (z, 0, 0, 0)),
            pl.BlockSpec(packed.shape, lambda z: (0, 0)),
        ],
        out_specs=pl.BlockSpec((1, outs, row_count, col_count), lambda z: (z, 0, 0, 0)),
        out_shape=jax.ShapeDtypeStruct((slice_count, outs, row_count, col_count), jnp.float32),
    )(shifted, packed)
    q = jnp.pad(q, ((0, 0), (0, 0), (1, 1), (1, 1)))
    score_field = jnp.zeros((slice_count, 2, row_count, col_count), jnp.float32)
    for shift_x in range(3):
        for shift_y in range(3):
            tap = (shift_x * 3 + shift_y) * 2
            score_field = score_field + q[
                :, tap : tap + 2, shift_x : shift_x + row_count, shift_y : shift_y + col_count
            ]
    return score_field


def slab_slices(image):
    return lax.all_gather(image, "coil", axis=0, tiled=True)


def on_device(
    image,
    noise,
    sens,
    measured,
    mask,
    w_first,
    b_first,
    w_second,
    b_second,
    w_third,
    b_third,
    w_last,
):
    groups = lax.axis_size("coil")
    depth, parts, rows, lines = image.shape
    copies = jnp.broadcast_to(image[:, :, :, None], (depth, parts, rows, groups, lines))
    copies = copies.reshape(depth, parts, rows * groups, lines)
    planes_in = lax.all_to_all(copies, ("slab", "coil"), split_axis=2, concat_axis=0, tiled=True)
    planes_in, local = lax.optimization_barrier((planes_in, image))
    window = with_halo(local.astype(jnp.bfloat16), ((("slab", "coil"), 0),), 2)
    score_field = score_net(window, w_first, b_first, w_second, b_second, w_third, b_third, w_last)
    planes = jnp.transpose(planes_in, (1, 2, 3, 0))
    partial_sum = coil_adjoint(planes, sens, measured, mask)
    by_depth = jnp.transpose(partial_sum, (3, 0, 1, 2)).astype(jnp.bfloat16)
    by_device = lax.all_to_all(by_depth, ("slab", "coil"), split_axis=0, concat_axis=2, tiled=True)
    by_device = by_device.astype(jnp.float32).reshape(depth, parts, rows, groups, lines)
    gradient = jnp.sum(by_device, axis=3)
    return image + STEP_SIZE * (score_field - gradient) + noise


def solution(mesh):
    in_specs = (
        P(("slab", "coil"), None, None, None),
        P(("slab", "coil"), None, None, None),
        P("coil", None, "slab", None, None),
        P("coil", None, "slab", None, None),
        P(),
        P(),
        P(),
        P(),
        P(),
        P(),
        P(),
        P(),
    )
    out_specs = P(("slab", "coil"), None, None, None)
    return jax.shard_map(
        on_device, mesh=mesh, in_specs=in_specs, out_specs=out_specs, check_vma=False
    )
```

```python
import ml_dtypes
import numpy as np
import jax
import jax.numpy as jnp
from jax import lax
from jax.sharding import PartitionSpec as P
from jax.experimental import pallas as pl
from jax.experimental.pallas import tpu as pltpu

STEP_SIZE = 0.5


def with_halo(shard, sides, width):
    for axis, dim in sides:
        devices, length = (lax.axis_size(axis), shard.shape[dim])
        up = [(i, (i + 1) % devices) for i in range(devices - 1)]
        down = [(j, i) for i, j in up]
        last = lax.slice_in_dim(shard, length - width, length, axis=dim)
        first = lax.slice_in_dim(shard, 0, width, axis=dim)
        before = lax.ppermute(last, axis, up)
        after = lax.ppermute(first, axis, down)
        shard = jnp.concatenate([before, shard, after], axis=dim)
    return shard


def dft_tables(length):
    line_index = np.arange(length, dtype=np.int64)
    phase_turns = line_index[:, None] * line_index[None, :] % length
    phase_angle = phase_turns.astype(np.float32) * np.float32(2.0 * np.pi / length)
    norm_scale = np.float32(1.0) / np.sqrt(np.float32(length))
    return (
        (np.cos(phase_angle) * norm_scale).astype(ml_dtypes.bfloat16),
        (np.sin(phase_angle) * norm_scale).astype(ml_dtypes.bfloat16),
    )


def along_y(values, table):
    return jnp.einsum("...yz,yk->...kz", values, table, preferred_element_type=jnp.float32)


def along_z(values, table):
    return jnp.einsum("...z,zk->...k", values, table, preferred_element_type=jnp.float32)


def spectrum(real_part, imag_part, cos_y, sin_y, cos_z, sin_z, forward):
    sign = 1.0 if forward else -1.0
    out_real = (along_y(real_part, cos_y) + sign * along_y(imag_part, sin_y)).astype(jnp.bfloat16)
    out_imag = (along_y(imag_part, cos_y) - sign * along_y(real_part, sin_y)).astype(jnp.bfloat16)
    last_real = along_z(out_real, cos_z) + sign * along_z(out_imag, sin_z)
    last_imag = along_z(out_imag, cos_z) - sign * along_z(out_real, sin_z)
    return (last_real, last_imag)


def adjoint_kernel(planes_ref, sens_ref, meas_ref, mask_ref, ty_ref, tz_ref, out_ref):
    ny = planes_ref.shape[1]
    nz = planes_ref.shape[2]

    @pl.when(pl.program_id(0) == 0)
    def _():
        out_ref[...] = jnp.zeros_like(out_ref)

    ty = ty_ref[...]
    tz = tz_ref[...]
    sens_real = sens_ref[0].astype(jnp.float32)
    sens_imag = sens_ref[1].astype(jnp.float32)
    image_real = planes_ref[0]
    image_imag = planes_ref[1]
    coil_real = (sens_real * image_real - sens_imag * image_imag).astype(jnp.bfloat16)
    coil_imag = (sens_real * image_imag + sens_imag * image_real).astype(jnp.bfloat16)
    half = jnp.dot(ty, jnp.concatenate([coil_real, coil_imag], axis=1), preferred_element_type=jnp.float32)
    half_real = (half[:ny, :nz] + half[ny:, nz:]).astype(jnp.bfloat16)
    half_imag = (half[:ny, nz:] - half[ny:, :nz]).astype(jnp.bfloat16)
    full = jnp.dot(jnp.concatenate([half_real, half_imag], axis=0), tz, preferred_element_type=jnp.float32)
    spec_real = full[:ny, :nz] + full[ny:, nz:]
    spec_imag = full[ny:, :nz] - full[:ny, nz:]
    sampled = mask_ref[...].astype(jnp.float32)
    miss_real = (sampled * (spec_real - meas_ref[0].astype(jnp.float32))).astype(jnp.bfloat16)
    miss_imag = (sampled * (spec_imag - meas_ref[1].astype(jnp.float32))).astype(jnp.bfloat16)
    half = jnp.dot(ty, jnp.concatenate([miss_real, miss_imag], axis=1), preferred_element_type=jnp.float32)
    back_real = (half[:ny, :nz] - half[ny:, nz:]).astype(jnp.bfloat16)
    back_imag = (half[:ny, nz:] + half[ny:, :nz]).astype(jnp.bfloat16)
    full = jnp.dot(jnp.concatenate([back_real, back_imag], axis=0), tz, preferred_element_type=jnp.float32)
    grad_real = full[:ny, :nz] - full[ny:, nz:]
    grad_imag = full[ny:, :nz] + full[:ny, nz:]
    out_ref[0] += sens_real * grad_real + sens_imag * grad_imag
    out_ref[1] += sens_real * grad_imag - sens_imag * grad_real


def coil_adjoint(planes, sens, measured, mask):
    ny = planes.shape[2]
    nz = planes.shape[3]
    cos_y, sin_y = dft_tables(ny)
    cos_z, sin_z = dft_tables(nz)
    ty = jnp.asarray(np.concatenate([cos_y, sin_y], axis=0))
    tz = jnp.asarray(np.concatenate([cos_z, sin_z], axis=1))
    coils = sens.shape[0]
    return pl.pallas_call(
        adjoint_kernel,
        grid=(coils,),
        in_specs=[
            pl.BlockSpec((2, None, ny, nz), lambda c: (0, 0, 0, 0)),
            pl.BlockSpec((None, 2, None, ny, nz), lambda c: (c, 0, 0, 0, 0)),
            pl.BlockSpec((None, 2, None, ny, nz), lambda c: (c, 0, 0, 0, 0)),
            pl.BlockSpec((ny, nz), lambda c: (0, 0)),
            pl.BlockSpec((2 * ny, ny), lambda c: (0, 0)),
            pl.BlockSpec((nz, 2 * nz), lambda c: (0, 0)),
        ],
        out_specs=pl.BlockSpec((2, None, ny, nz), lambda c: (0, 0, 0, 0)),
        out_shape=jax.ShapeDtypeStruct(planes.shape, jnp.float32),
    )(planes, sens, measured, mask, ty, tz)


def net_kernel(x_ref, p_ref, q_ref):
    width = p_ref.shape[0] - 24
    taps_in = x_ref.shape[1]
    row_count = q_ref.shape[2]
    cols = q_ref.shape[3]
    outs = q_ref.shape[1]
    rows = 16
    w1 = [p_ref[:width, a * width : a * width + taps_in].astype(jnp.bfloat16) for a in range(3)]
    w2 = p_ref[:width, 3 * width : 4 * width].astype(jnp.bfloat16)
    w3 = p_ref[:width, 4 * width : 5 * width].astype(jnp.bfloat16)
    wl = p_ref[width : width + outs, 0:width].astype(jnp.bfloat16)
    b1 = p_ref[:width, 5 * width : 5 * width + 1]
    b2 = p_ref[:width, 5 * width + 1 : 5 * width + 2]
    b3 = p_ref[:width, 5 * width + 2 : 5 * width + 3]
    for chunk in range(row_count // rows):
        first = chunk * rows
        h = b1
        for a in range(3):
            x = jnp.concatenate([x_ref[0, :, first + row + a, :] for row in range(rows)], axis=1)
            h = h + jnp.dot(w1[a], x, preferred_element_type=jnp.float32)
        h = jax.nn.silu(h).astype(jnp.bfloat16)
        h = jnp.dot(w2, h, preferred_element_type=jnp.float32) + b2
        h = jax.nn.silu(h).astype(jnp.bfloat16)
        h = jnp.dot(w3, h, preferred_element_type=jnp.float32) + b3
        h = jax.nn.silu(h).astype(jnp.bfloat16)
        q = jnp.dot(wl, h, preferred_element_type=jnp.float32)
        for row in range(rows):
            q_ref[0, :, first + row, :] = q[:, row * cols : (row + 1) * cols]


def score_net(window, w_first, b_first, w_second, b_second, w_third, b_third, w_last):
    slice_count = window.shape[0] - 4
    row_count = window.shape[2]
    col_count = window.shape[3]
    width = w_first.shape[-1]
    stacked = jnp.concatenate(
        [window[offset : offset + slice_count] for offset in range(5)], axis=1
    )
    framed = jnp.pad(stacked, ((0, 0), (0, 0), (1, 1), (1, 1)))
    shifted = jnp.concatenate(
        [framed[:, :, :, shift_y : shift_y + col_count] for shift_y in range(3)], axis=1
    )
    taps_in = shifted.shape[1]
    wl = w_last.reshape(-1, width)
    outs = wl.shape[0]
    pad_to = lambda m: jnp.pad(m.astype(jnp.float32), ((0, 0), (0, width - m.shape[1])))
    top = jnp.concatenate(
        [pad_to(w_first[shift_x].reshape(taps_in, width).T) for shift_x in range(3)]
        + [
            pad_to(w_second.T),
            pad_to(w_third.T),
            pad_to(jnp.stack([b_first, b_second, b_third], axis=1)),
        ],
        axis=1,
    )
    bottom = jnp.pad(wl.astype(jnp.float32), ((0, 24 - outs), (0, 5 * width)))
    packed = jnp.concatenate([top, bottom], axis=0)
    q = pl.pallas_call(
        net_kernel,
        grid=(slice_count,),
        in_specs=[
            pl.BlockSpec((1,) + shifted.shape[1:], lambda z: (z, 0, 0, 0)),
            pl.BlockSpec(packed.shape, lambda z: (0, 0)),
        ],
        out_specs=pl.BlockSpec((1, outs, row_count, col_count), lambda z: (z, 0, 0, 0)),
        out_shape=jax.ShapeDtypeStruct((slice_count, outs, row_count, col_count), jnp.float32),
    )(shifted, packed)
    q = jnp.pad(q, ((0, 0), (0, 0), (1, 1), (1, 1)))
    score_field = jnp.zeros((slice_count, 2, row_count, col_count), jnp.float32)
    for shift_x in range(3):
        for shift_y in range(3):
            tap = (shift_x * 3 + shift_y) * 2
            score_field = score_field + q[
                :, tap : tap + 2, shift_x : shift_x + row_count, shift_y : shift_y + col_count
            ]
    return score_field


def slab_slices(image):
    return lax.all_gather(image, "coil", axis=0, tiled=True)


def on_device(
    image,
    noise,
    sens,
    measured,
    mask,
    w_first,
    b_first,
    w_second,
    b_second,
    w_third,
    b_third,
    w_last,
):
    window = with_halo(image.astype(jnp.bfloat16), ((("slab", "coil"), 0),), 2)
    score_field = score_net(window, w_first, b_first, w_second, b_second, w_third, b_third, w_last)
    groups = lax.axis_size("coil")
    depth, parts, rows, lines = image.shape
    by_row = jnp.transpose(image, (2, 0, 1, 3))[:, None]
    copies = jnp.broadcast_to(by_row, (rows, groups, depth, parts, lines))
    copies = copies.reshape(rows * groups, depth, parts, lines)
    planes_in = lax.all_to_all(copies, ("slab", "coil"), split_axis=0, concat_axis=1, tiled=True)
    planes = jnp.transpose(planes_in, (2, 0, 3, 1))
    partial_sum = coil_adjoint(planes, sens, measured, mask)
    by_depth = jnp.transpose(partial_sum, (3, 0, 1, 2)).astype(jnp.bfloat16)
    by_device = lax.all_to_all(by_depth, ("slab", "coil"), split_axis=0, concat_axis=2, tiled=True)
    by_device = by_device.astype(jnp.float32).reshape(depth, parts, rows, groups, lines)
    gradient = jnp.sum(by_device, axis=3)
    return image + STEP_SIZE * (score_field - gradient) + noise


def solution(mesh):
    in_specs = (
        P(("slab", "coil"), None, None, None),
        P(("slab", "coil"), None, None, None),
        P("coil", None, "slab", None, None),
        P("coil", None, "slab", None, None),
        P(),
        P(),
        P(),
        P(),
        P(),
        P(),
        P(),
        P(),
    )
    out_specs = P(("slab", "coil"), None, None, None)
    return jax.shard_map(
        on_device, mesh=mesh, in_specs=in_specs, out_specs=out_specs, check_vma=False
    )
```

```python
import ml_dtypes
import numpy as np
import jax
import jax.numpy as jnp
from jax import lax
from jax.sharding import PartitionSpec as P
from jax.experimental import pallas as pl
from jax.experimental.pallas import tpu as pltpu

STEP_SIZE = 0.5


def with_halo(shard, sides, width):
    for axis, dim in sides:
        devices, length = (lax.axis_size(axis), shard.shape[dim])
        up = [(i, (i + 1) % devices) for i in range(devices - 1)]
        down = [(j, i) for i, j in up]
        last = lax.slice_in_dim(shard, length - width, length, axis=dim)
        first = lax.slice_in_dim(shard, 0, width, axis=dim)
        before = lax.ppermute(last, axis, up)
        after = lax.ppermute(first, axis, down)
        shard = jnp.concatenate([before, shard, after], axis=dim)
    return shard


def dft_tables(length):
    line_index = np.arange(length, dtype=np.int64)
    phase_turns = line_index[:, None] * line_index[None, :] % length
    phase_angle = phase_turns.astype(np.float32) * np.float32(2.0 * np.pi / length)
    norm_scale = np.float32(1.0) / np.sqrt(np.float32(length))
    return (
        (np.cos(phase_angle) * norm_scale).astype(ml_dtypes.bfloat16),
        (np.sin(phase_angle) * norm_scale).astype(ml_dtypes.bfloat16),
    )


def along_y(values, table):
    return jnp.einsum("...yz,yk->...kz", values, table, preferred_element_type=jnp.float32)


def along_z(values, table):
    return jnp.einsum("...z,zk->...k", values, table, preferred_element_type=jnp.float32)


def spectrum(real_part, imag_part, cos_y, sin_y, cos_z, sin_z, forward):
    sign = 1.0 if forward else -1.0
    out_real = (along_y(real_part, cos_y) + sign * along_y(imag_part, sin_y)).astype(jnp.bfloat16)
    out_imag = (along_y(imag_part, cos_y) - sign * along_y(real_part, sin_y)).astype(jnp.bfloat16)
    last_real = along_z(out_real, cos_z) + sign * along_z(out_imag, sin_z)
    last_imag = along_z(out_imag, cos_z) - sign * along_z(out_real, sin_z)
    return (last_real, last_imag)


def adjoint_kernel(planes_ref, sens_ref, meas_ref, mask_ref, ty_ref, tz_ref, out_ref):
    ny = planes_ref.shape[1]
    nz = planes_ref.shape[2]

    @pl.when(pl.program_id(0) == 0)
    def _():
        out_ref[...] = jnp.zeros_like(out_ref)

    ty = ty_ref[...]
    tz = tz_ref[...]
    sens_real = sens_ref[0].astype(jnp.float32)
    sens_imag = sens_ref[1].astype(jnp.float32)
    image_real = planes_ref[0]
    image_imag = planes_ref[1]
    coil_real = (sens_real * image_real - sens_imag * image_imag).astype(jnp.bfloat16)
    coil_imag = (sens_real * image_imag + sens_imag * image_real).astype(jnp.bfloat16)
    half = jnp.dot(ty, jnp.concatenate([coil_real, coil_imag], axis=1), preferred_element_type=jnp.float32)
    half_real = (half[:ny, :nz] + half[ny:, nz:]).astype(jnp.bfloat16)
    half_imag = (half[:ny, nz:] - half[ny:, :nz]).astype(jnp.bfloat16)
    full = jnp.dot(jnp.concatenate([half_real, half_imag], axis=0), tz, preferred_element_type=jnp.float32)
    spec_real = full[:ny, :nz] + full[ny:, nz:]
    spec_imag = full[ny:, :nz] - full[:ny, nz:]
    sampled = mask_ref[...].astype(jnp.float32)
    miss_real = (sampled * (spec_real - meas_ref[0].astype(jnp.float32))).astype(jnp.bfloat16)
    miss_imag = (sampled * (spec_imag - meas_ref[1].astype(jnp.float32))).astype(jnp.bfloat16)
    half = jnp.dot(ty, jnp.concatenate([miss_real, miss_imag], axis=1), preferred_element_type=jnp.float32)
    back_real = (half[:ny, :nz] - half[ny:, nz:]).astype(jnp.bfloat16)
    back_imag = (half[:ny, nz:] + half[ny:, :nz]).astype(jnp.bfloat16)
    full = jnp.dot(jnp.concatenate([back_real, back_imag], axis=0), tz, preferred_element_type=jnp.float32)
    grad_real = full[:ny, :nz] - full[ny:, nz:]
    grad_imag = full[ny:, :nz] + full[:ny, nz:]
    out_ref[0] += sens_real * grad_real + sens_imag * grad_imag
    out_ref[1] += sens_real * grad_imag - sens_imag * grad_real


def coil_adjoint(planes, sens, measured, mask):
    ny = planes.shape[2]
    nz = planes.shape[3]
    cos_y, sin_y = dft_tables(ny)
    cos_z, sin_z = dft_tables(nz)
    ty = jnp.asarray(np.concatenate([cos_y, sin_y], axis=0))
    tz = jnp.asarray(np.concatenate([cos_z, sin_z], axis=1))
    coils = sens.shape[0]
    return pl.pallas_call(
        adjoint_kernel,
        grid=(coils,),
        in_specs=[
            pl.BlockSpec((2, None, ny, nz), lambda c: (0, 0, 0, 0)),
            pl.BlockSpec((None, 2, None, ny, nz), lambda c: (c, 0, 0, 0, 0)),
            pl.BlockSpec((None, 2, None, ny, nz), lambda c: (c, 0, 0, 0, 0)),
            pl.BlockSpec((ny, nz), lambda c: (0, 0)),
            pl.BlockSpec((2 * ny, ny), lambda c: (0, 0)),
            pl.BlockSpec((nz, 2 * nz), lambda c: (0, 0)),
        ],
        out_specs=pl.BlockSpec((2, None, ny, nz), lambda c: (0, 0, 0, 0)),
        out_shape=jax.ShapeDtypeStruct(planes.shape, jnp.float32),
    )(planes, sens, measured, mask, ty, tz)


def net_kernel(x_ref, p_ref, q_ref):
    width = p_ref.shape[0] - 24
    taps_in = x_ref.shape[1]
    row_count = q_ref.shape[2]
    cols = q_ref.shape[3]
    outs = q_ref.shape[1]
    rows = 16
    w1 = [p_ref[:width, a * width : a * width + taps_in].astype(jnp.bfloat16) for a in range(3)]
    w2 = p_ref[:width, 3 * width : 4 * width].astype(jnp.bfloat16)
    w3 = p_ref[:width, 4 * width : 5 * width].astype(jnp.bfloat16)
    wl = p_ref[width : width + outs, 0:width].astype(jnp.bfloat16)
    b1 = p_ref[:width, 5 * width : 5 * width + 1]
    b2 = p_ref[:width, 5 * width + 1 : 5 * width + 2]
    b3 = p_ref[:width, 5 * width + 2 : 5 * width + 3]
    for chunk in range(row_count // rows):
        first = chunk * rows
        h = b1
        for a in range(3):
            x = jnp.concatenate([x_ref[0, :, first + row + a, :] for row in range(rows)], axis=1)
            h = h + jnp.dot(w1[a], x, preferred_element_type=jnp.float32)
        h = jax.nn.silu(h).astype(jnp.bfloat16)
        h = jnp.dot(w2, h, preferred_element_type=jnp.float32) + b2
        h = jax.nn.silu(h).astype(jnp.bfloat16)
        h = jnp.dot(w3, h, preferred_element_type=jnp.float32) + b3
        h = jax.nn.silu(h).astype(jnp.bfloat16)
        q = jnp.dot(wl, h, preferred_element_type=jnp.float32)
        for row in range(rows):
            q_ref[0, :, first + row, :] = q[:, row * cols : (row + 1) * cols]


def score_net(window, w_first, b_first, w_second, b_second, w_third, b_third, w_last, tie):
    slice_count = window.shape[0] - 4
    row_count = window.shape[2]
    col_count = window.shape[3]
    width = w_first.shape[-1]
    stacked = jnp.concatenate(
        [window[offset : offset + slice_count] for offset in range(5)], axis=1
    )
    framed = jnp.pad(stacked, ((0, 0), (0, 0), (1, 1), (1, 1)))
    shifted = jnp.concatenate(
        [framed[:, :, :, shift_y : shift_y + col_count] for shift_y in range(3)], axis=1
    )
    taps_in = shifted.shape[1]
    wl = w_last.reshape(-1, width)
    outs = wl.shape[0]
    pad_to = lambda m: jnp.pad(m.astype(jnp.float32), ((0, 0), (0, width - m.shape[1])))
    top = jnp.concatenate(
        [pad_to(w_first[shift_x].reshape(taps_in, width).T) for shift_x in range(3)]
        + [
            pad_to(w_second.T),
            pad_to(w_third.T),
            pad_to(jnp.stack([b_first, b_second, b_third], axis=1)),
        ],
        axis=1,
    )
    bottom = jnp.pad(wl.astype(jnp.float32), ((0, 24 - outs), (0, 5 * width)))
    packed = jnp.concatenate([top, bottom], axis=0)
    shifted, packed, tie = lax.optimization_barrier((shifted, packed, tie))
    q = pl.pallas_call(
        net_kernel,
        grid=(slice_count,),
        in_specs=[
            pl.BlockSpec((1,) + shifted.shape[1:], lambda z: (z, 0, 0, 0)),
            pl.BlockSpec(packed.shape, lambda z: (0, 0)),
        ],
        out_specs=pl.BlockSpec((1, outs, row_count, col_count), lambda z: (z, 0, 0, 0)),
        out_shape=jax.ShapeDtypeStruct((slice_count, outs, row_count, col_count), jnp.float32),
    )(shifted, packed)
    q = jnp.pad(q, ((0, 0), (0, 0), (1, 1), (1, 1)))
    score_field = jnp.zeros((slice_count, 2, row_count, col_count), jnp.float32)
    for shift_x in range(3):
        for shift_y in range(3):
            tap = (shift_x * 3 + shift_y) * 2
            score_field = score_field + q[
                :, tap : tap + 2, shift_x : shift_x + row_count, shift_y : shift_y + col_count
            ]
    return score_field, tie


def slab_slices(image):
    return lax.all_gather(image, "coil", axis=0, tiled=True)


def on_device(
    image,
    noise,
    sens,
    measured,
    mask,
    w_first,
    b_first,
    w_second,
    b_second,
    w_third,
    b_third,
    w_last,
):
    window = with_halo(image.astype(jnp.bfloat16), ((("slab", "coil"), 0),), 2)
    groups = lax.axis_size("coil")
    depth, parts, rows, lines = image.shape
    copies = jnp.broadcast_to(image[:, :, :, None], (depth, parts, rows, groups, lines))
    copies = copies.reshape(depth, parts, rows * groups, lines)
    planes_in = lax.all_to_all(copies, ("slab", "coil"), split_axis=2, concat_axis=0, tiled=True)
    score_field, planes_in = score_net(
        window, w_first, b_first, w_second, b_second, w_third, b_third, w_last, planes_in
    )
    planes = jnp.transpose(planes_in, (1, 2, 3, 0))
    partial_sum = coil_adjoint(planes, sens, measured, mask)
    by_depth = jnp.transpose(partial_sum, (3, 0, 1, 2)).astype(jnp.bfloat16)
    by_device = lax.all_to_all(by_depth, ("slab", "coil"), split_axis=0, concat_axis=2, tiled=True)
    by_device = by_device.astype(jnp.float32).reshape(depth, parts, rows, groups, lines)
    gradient = jnp.sum(by_device, axis=3)
    return image + STEP_SIZE * (score_field - gradient) + noise


def solution(mesh):
    in_specs = (
        P(("slab", "coil"), None, None, None),
        P(("slab", "coil"), None, None, None),
        P("coil", None, "slab", None, None),
        P("coil", None, "slab", None, None),
        P(),
        P(),
        P(),
        P(),
        P(),
        P(),
        P(),
        P(),
    )
    out_specs = P(("slab", "coil"), None, None, None)
    return jax.shard_map(
        on_device, mesh=mesh, in_specs=in_specs, out_specs=out_specs, check_vma=False
    )
```

```python
import ml_dtypes
import numpy as np
import jax
import jax.numpy as jnp
from jax import lax
from jax.sharding import PartitionSpec as P
from jax.experimental import pallas as pl
from jax.experimental.pallas import tpu as pltpu

STEP_SIZE = 0.5


def with_halo(shard, sides, width):
    for axis, dim in sides:
        devices, length = (lax.axis_size(axis), shard.shape[dim])
        up = [(i, (i + 1) % devices) for i in range(devices - 1)]
        down = [(j, i) for i, j in up]
        last = lax.slice_in_dim(shard, length - width, length, axis=dim)
        first = lax.slice_in_dim(shard, 0, width, axis=dim)
        before = lax.ppermute(last, axis, up)
        after = lax.ppermute(first, axis, down)
        shard = jnp.concatenate([before, shard, after], axis=dim)
    return shard


def dft_tables(length):
    line_index = np.arange(length, dtype=np.int64)
    phase_turns = line_index[:, None] * line_index[None, :] % length
    phase_angle = phase_turns.astype(np.float32) * np.float32(2.0 * np.pi / length)
    norm_scale = np.float32(1.0) / np.sqrt(np.float32(length))
    return (
        (np.cos(phase_angle) * norm_scale).astype(ml_dtypes.bfloat16),
        (np.sin(phase_angle) * norm_scale).astype(ml_dtypes.bfloat16),
    )


def along_y(values, table):
    return jnp.einsum("...yz,yk->...kz", values, table, preferred_element_type=jnp.float32)


def along_z(values, table):
    return jnp.einsum("...z,zk->...k", values, table, preferred_element_type=jnp.float32)


def spectrum(real_part, imag_part, cos_y, sin_y, cos_z, sin_z, forward):
    sign = 1.0 if forward else -1.0
    out_real = (along_y(real_part, cos_y) + sign * along_y(imag_part, sin_y)).astype(jnp.bfloat16)
    out_imag = (along_y(imag_part, cos_y) - sign * along_y(real_part, sin_y)).astype(jnp.bfloat16)
    last_real = along_z(out_real, cos_z) + sign * along_z(out_imag, sin_z)
    last_imag = along_z(out_imag, cos_z) - sign * along_z(out_real, sin_z)
    return (last_real, last_imag)


def adjoint_kernel(planes_ref, sens_ref, meas_ref, mask_ref, ty_ref, tz_ref, out_ref, acc_ref):
    ny = planes_ref.shape[1]
    nz = planes_ref.shape[2]

    @pl.when(pl.program_id(0) == 0)
    def _():
        acc_ref[...] = jnp.zeros_like(acc_ref)

    ty = ty_ref[...]
    tz = tz_ref[...]
    sens_real = sens_ref[0].astype(jnp.float32)
    sens_imag = sens_ref[1].astype(jnp.float32)
    image_real = planes_ref[0]
    image_imag = planes_ref[1]
    coil_real = (sens_real * image_real - sens_imag * image_imag).astype(jnp.bfloat16)
    coil_imag = (sens_real * image_imag + sens_imag * image_real).astype(jnp.bfloat16)
    half = jnp.dot(ty, jnp.concatenate([coil_real, coil_imag], axis=1), preferred_element_type=jnp.float32)
    half_real = (half[:ny, :nz] + half[ny:, nz:]).astype(jnp.bfloat16)
    half_imag = (half[:ny, nz:] - half[ny:, :nz]).astype(jnp.bfloat16)
    full = jnp.dot(jnp.concatenate([half_real, half_imag], axis=0), tz, preferred_element_type=jnp.float32)
    spec_real = full[:ny, :nz] + full[ny:, nz:]
    spec_imag = full[ny:, :nz] - full[:ny, nz:]
    sampled = mask_ref[...].astype(jnp.float32)
    miss_real = (sampled * (spec_real - meas_ref[0].astype(jnp.float32))).astype(jnp.bfloat16)
    miss_imag = (sampled * (spec_imag - meas_ref[1].astype(jnp.float32))).astype(jnp.bfloat16)
    half = jnp.dot(ty, jnp.concatenate([miss_real, miss_imag], axis=1), preferred_element_type=jnp.float32)
    back_real = (half[:ny, :nz] - half[ny:, nz:]).astype(jnp.bfloat16)
    back_imag = (half[:ny, nz:] + half[ny:, :nz]).astype(jnp.bfloat16)
    full = jnp.dot(jnp.concatenate([back_real, back_imag], axis=0), tz, preferred_element_type=jnp.float32)
    grad_real = full[:ny, :nz] - full[ny:, nz:]
    grad_imag = full[ny:, :nz] + full[:ny, nz:]
    acc_ref[0] += sens_real * grad_real + sens_imag * grad_imag
    acc_ref[1] += sens_real * grad_imag - sens_imag * grad_real

    @pl.when(pl.program_id(0) == pl.num_programs(0) - 1)
    def _():
        out_ref[...] = acc_ref[...].astype(out_ref.dtype)


def coil_adjoint(planes, sens, measured, mask):
    ny = planes.shape[2]
    nz = planes.shape[3]
    cos_y, sin_y = dft_tables(ny)
    cos_z, sin_z = dft_tables(nz)
    ty = jnp.asarray(np.concatenate([cos_y, sin_y], axis=0))
    tz = jnp.asarray(np.concatenate([cos_z, sin_z], axis=1))
    coils = sens.shape[0]
    return pl.pallas_call(
        adjoint_kernel,
        grid=(coils,),
        in_specs=[
            pl.BlockSpec((2, None, ny, nz), lambda c: (0, 0, 0, 0)),
            pl.BlockSpec((None, 2, None, ny, nz), lambda c: (c, 0, 0, 0, 0)),
            pl.BlockSpec((None, 2, None, ny, nz), lambda c: (c, 0, 0, 0, 0)),
            pl.BlockSpec((ny, nz), lambda c: (0, 0)),
            pl.BlockSpec((2 * ny, ny), lambda c: (0, 0)),
            pl.BlockSpec((nz, 2 * nz), lambda c: (0, 0)),
        ],
        out_specs=pl.BlockSpec((2, None, ny, nz), lambda c: (0, 0, 0, 0)),
        out_shape=jax.ShapeDtypeStruct(planes.shape, jnp.bfloat16),
        scratch_shapes=[pltpu.VMEM((2, ny, nz), jnp.float32)],
    )(planes, sens, measured, mask, ty, tz)


def net_kernel(x_ref, p_ref, q_ref):
    width = p_ref.shape[0] - 24
    taps_in = x_ref.shape[1]
    row_count = q_ref.shape[2]
    cols = q_ref.shape[3]
    outs = q_ref.shape[1]
    rows = 16
    w1 = [p_ref[:width, a * width : a * width + taps_in].astype(jnp.bfloat16) for a in range(3)]
    w2 = p_ref[:width, 3 * width : 4 * width].astype(jnp.bfloat16)
    w3 = p_ref[:width, 4 * width : 5 * width].astype(jnp.bfloat16)
    wl = p_ref[width : width + outs, 0:width].astype(jnp.bfloat16)
    b1 = p_ref[:width, 5 * width : 5 * width + 1]
    b2 = p_ref[:width, 5 * width + 1 : 5 * width + 2]
    b3 = p_ref[:width, 5 * width + 2 : 5 * width + 3]
    for chunk in range(row_count // rows):
        first = chunk * rows
        h = b1
        for a in range(3):
            x = jnp.concatenate([x_ref[0, :, first + row + a, :] for row in range(rows)], axis=1)
            h = h + jnp.dot(w1[a], x, preferred_element_type=jnp.float32)
        h = jax.nn.silu(h).astype(jnp.bfloat16)
        h = jnp.dot(w2, h, preferred_element_type=jnp.float32) + b2
        h = jax.nn.silu(h).astype(jnp.bfloat16)
        h = jnp.dot(w3, h, preferred_element_type=jnp.float32) + b3
        h = jax.nn.silu(h).astype(jnp.bfloat16)
        q = jnp.dot(wl, h, preferred_element_type=jnp.float32)
        for row in range(rows):
            q_ref[0, :, first + row, :] = q[:, row * cols : (row + 1) * cols]


def score_net(window, w_first, b_first, w_second, b_second, w_third, b_third, w_last, tie):
    slice_count = window.shape[0] - 4
    row_count = window.shape[2]
    col_count = window.shape[3]
    width = w_first.shape[-1]
    stacked = jnp.concatenate(
        [window[offset : offset + slice_count] for offset in range(5)], axis=1
    )
    framed = jnp.pad(stacked, ((0, 0), (0, 0), (1, 1), (1, 1)))
    shifted = jnp.concatenate(
        [framed[:, :, :, shift_y : shift_y + col_count] for shift_y in range(3)], axis=1
    )
    taps_in = shifted.shape[1]
    wl = w_last.reshape(-1, width)
    outs = wl.shape[0]
    pad_to = lambda m: jnp.pad(m.astype(jnp.float32), ((0, 0), (0, width - m.shape[1])))
    top = jnp.concatenate(
        [pad_to(w_first[shift_x].reshape(taps_in, width).T) for shift_x in range(3)]
        + [
            pad_to(w_second.T),
            pad_to(w_third.T),
            pad_to(jnp.stack([b_first, b_second, b_third], axis=1)),
        ],
        axis=1,
    )
    bottom = jnp.pad(wl.astype(jnp.float32), ((0, 24 - outs), (0, 5 * width)))
    packed = jnp.concatenate([top, bottom], axis=0)
    shifted, packed, tie = lax.optimization_barrier((shifted, packed, tie))
    q = pl.pallas_call(
        net_kernel,
        grid=(slice_count,),
        in_specs=[
            pl.BlockSpec((1,) + shifted.shape[1:], lambda z: (z, 0, 0, 0)),
            pl.BlockSpec(packed.shape, lambda z: (0, 0)),
        ],
        out_specs=pl.BlockSpec((1, outs, row_count, col_count), lambda z: (z, 0, 0, 0)),
        out_shape=jax.ShapeDtypeStruct((slice_count, outs, row_count, col_count), jnp.float32),
    )(shifted, packed)
    q = jnp.pad(q, ((0, 0), (0, 0), (1, 1), (1, 1)))
    score_field = jnp.zeros((slice_count, 2, row_count, col_count), jnp.float32)
    for shift_x in range(3):
        for shift_y in range(3):
            tap = (shift_x * 3 + shift_y) * 2
            score_field = score_field + q[
                :, tap : tap + 2, shift_x : shift_x + row_count, shift_y : shift_y + col_count
            ]
    return score_field, tie


def slab_slices(image):
    return lax.all_gather(image, "coil", axis=0, tiled=True)


def on_device(
    image,
    noise,
    sens,
    measured,
    mask,
    w_first,
    b_first,
    w_second,
    b_second,
    w_third,
    b_third,
    w_last,
):
    window = with_halo(image.astype(jnp.bfloat16), ((("slab", "coil"), 0),), 2)
    groups = lax.axis_size("coil")
    depth, parts, rows, lines = image.shape
    copies = jnp.broadcast_to(image[:, :, :, None], (depth, parts, rows, groups, lines))
    copies = copies.reshape(depth, parts, rows * groups, lines)
    planes_in = lax.all_to_all(copies, ("slab", "coil"), split_axis=2, concat_axis=0, tiled=True)
    score_field, planes_in = score_net(
        window, w_first, b_first, w_second, b_second, w_third, b_third, w_last, planes_in
    )
    planes = jnp.transpose(planes_in, (1, 2, 3, 0))
    partial_sum = coil_adjoint(planes, sens, measured, mask)
    by_depth = jnp.transpose(partial_sum, (3, 0, 1, 2))
    by_device = lax.all_to_all(by_depth, ("slab", "coil"), split_axis=0, concat_axis=2, tiled=True)
    by_device = by_device.astype(jnp.float32).reshape(depth, parts, rows, groups, lines)
    gradient = jnp.sum(by_device, axis=3)
    return image + STEP_SIZE * (score_field - gradient) + noise


def solution(mesh):
    in_specs = (
        P(("slab", "coil"), None, None, None),
        P(("slab", "coil"), None, None, None),
        P("coil", None, "slab", None, None),
        P("coil", None, "slab", None, None),
        P(),
        P(),
        P(),
        P(),
        P(),
        P(),
        P(),
        P(),
    )
    out_specs = P(("slab", "coil"), None, None, None)
    return jax.shard_map(
        on_device, mesh=mesh, in_specs=in_specs, out_specs=out_specs, check_vma=False
    )
```

```python
import ml_dtypes
import numpy as np
import jax
import jax.numpy as jnp
from jax import lax
from jax.sharding import PartitionSpec as P
from jax.experimental import pallas as pl
from jax.experimental.pallas import tpu as pltpu

STEP_SIZE = 0.5


def with_halo(shard, sides, width):
    for axis, dim in sides:
        devices, length = (lax.axis_size(axis), shard.shape[dim])
        up = [(i, (i + 1) % devices) for i in range(devices - 1)]
        down = [(j, i) for i, j in up]
        last = lax.slice_in_dim(shard, length - width, length, axis=dim)
        first = lax.slice_in_dim(shard, 0, width, axis=dim)
        before = lax.ppermute(last, axis, up)
        after = lax.ppermute(first, axis, down)
        shard = jnp.concatenate([before, shard, after], axis=dim)
    return shard


def dft_tables(length):
    line_index = np.arange(length, dtype=np.int64)
    phase_turns = line_index[:, None] * line_index[None, :] % length
    phase_angle = phase_turns.astype(np.float32) * np.float32(2.0 * np.pi / length)
    norm_scale = np.float32(1.0) / np.sqrt(np.float32(length))
    return (
        (np.cos(phase_angle) * norm_scale).astype(ml_dtypes.bfloat16),
        (np.sin(phase_angle) * norm_scale).astype(ml_dtypes.bfloat16),
    )


def along_y(values, table):
    return jnp.einsum("...yz,yk->...kz", values, table, preferred_element_type=jnp.float32)


def along_z(values, table):
    return jnp.einsum("...z,zk->...k", values, table, preferred_element_type=jnp.float32)


def spectrum(real_part, imag_part, cos_y, sin_y, cos_z, sin_z, forward):
    sign = 1.0 if forward else -1.0
    out_real = (along_y(real_part, cos_y) + sign * along_y(imag_part, sin_y)).astype(jnp.bfloat16)
    out_imag = (along_y(imag_part, cos_y) - sign * along_y(real_part, sin_y)).astype(jnp.bfloat16)
    last_real = along_z(out_real, cos_z) + sign * along_z(out_imag, sin_z)
    last_imag = along_z(out_imag, cos_z) - sign * along_z(out_real, sin_z)
    return (last_real, last_imag)


def adjoint_kernel(planes_ref, sens_ref, meas_ref, mask_ref, ty_ref, tz_ref, out_ref, acc_ref):
    ny = planes_ref.shape[1]
    nz = planes_ref.shape[2]

    @pl.when(pl.program_id(0) == 0)
    def _():
        acc_ref[...] = jnp.zeros_like(acc_ref)

    ty = ty_ref[...]
    tz = tz_ref[...]
    sens_real = sens_ref[0].astype(jnp.float32)
    sens_imag = sens_ref[1].astype(jnp.float32)
    image_real = planes_ref[0]
    image_imag = planes_ref[1]
    coil_real = (sens_real * image_real - sens_imag * image_imag).astype(jnp.bfloat16)
    coil_imag = (sens_real * image_imag + sens_imag * image_real).astype(jnp.bfloat16)
    half = jnp.dot(ty, jnp.concatenate([coil_real, coil_imag], axis=1), preferred_element_type=jnp.float32)
    half_real = (half[:ny, :nz] + half[ny:, nz:]).astype(jnp.bfloat16)
    half_imag = (half[:ny, nz:] - half[ny:, :nz]).astype(jnp.bfloat16)
    full = jnp.dot(jnp.concatenate([half_real, half_imag], axis=0), tz, preferred_element_type=jnp.float32)
    spec_real = full[:ny, :nz] + full[ny:, nz:]
    spec_imag = full[ny:, :nz] - full[:ny, nz:]
    sampled = mask_ref[...].astype(jnp.float32)
    miss_real = (sampled * (spec_real - meas_ref[0].astype(jnp.float32))).astype(jnp.bfloat16)
    miss_imag = (sampled * (spec_imag - meas_ref[1].astype(jnp.float32))).astype(jnp.bfloat16)
    half = jnp.dot(ty, jnp.concatenate([miss_real, miss_imag], axis=1), preferred_element_type=jnp.float32)
    back_real = (half[:ny, :nz] - half[ny:, nz:]).astype(jnp.bfloat16)
    back_imag = (half[:ny, nz:] + half[ny:, :nz]).astype(jnp.bfloat16)
    full = jnp.dot(jnp.concatenate([back_real, back_imag], axis=0), tz, preferred_element_type=jnp.float32)
    grad_real = full[:ny, :nz] - full[ny:, nz:]
    grad_imag = full[ny:, :nz] + full[:ny, nz:]
    acc_ref[0] += sens_real * grad_real + sens_imag * grad_imag
    acc_ref[1] += sens_real * grad_imag - sens_imag * grad_real

    @pl.when(pl.program_id(0) == pl.num_programs(0) - 1)
    def _():
        out_ref[...] = acc_ref[...].astype(out_ref.dtype)


def coil_adjoint(planes, sens, measured, mask):
    ny = planes.shape[2]
    nz = planes.shape[3]
    cos_y, sin_y = dft_tables(ny)
    cos_z, sin_z = dft_tables(nz)
    ty = jnp.asarray(np.concatenate([cos_y, sin_y], axis=0))
    tz = jnp.asarray(np.concatenate([cos_z, sin_z], axis=1))
    coils = sens.shape[0]
    return pl.pallas_call(
        adjoint_kernel,
        grid=(coils,),
        in_specs=[
            pl.BlockSpec((2, None, ny, nz), lambda c: (0, 0, 0, 0)),
            pl.BlockSpec((None, 2, None, ny, nz), lambda c: (c, 0, 0, 0, 0)),
            pl.BlockSpec((None, 2, None, ny, nz), lambda c: (c, 0, 0, 0, 0)),
            pl.BlockSpec((ny, nz), lambda c: (0, 0)),
            pl.BlockSpec((2 * ny, ny), lambda c: (0, 0)),
            pl.BlockSpec((nz, 2 * nz), lambda c: (0, 0)),
        ],
        out_specs=pl.BlockSpec((2, None, ny, nz), lambda c: (0, 0, 0, 0)),
        out_shape=jax.ShapeDtypeStruct(planes.shape, jnp.bfloat16),
        scratch_shapes=[pltpu.VMEM((2, ny, nz), jnp.float32)],
    )(planes, sens, measured, mask, ty, tz)


def net_kernel(x_ref, p_ref, q_ref):
    width = p_ref.shape[0] - 24
    taps_in = x_ref.shape[1]
    row_count = q_ref.shape[2]
    cols = q_ref.shape[3]
    outs = q_ref.shape[1]
    rows = 8
    w1 = [p_ref[:width, a * width : a * width + taps_in].astype(jnp.bfloat16) for a in range(3)]
    w2 = p_ref[:width, 3 * width : 4 * width].astype(jnp.bfloat16)
    w3 = p_ref[:width, 4 * width : 5 * width].astype(jnp.bfloat16)
    wl = p_ref[width : width + outs, 0:width].astype(jnp.bfloat16)
    b1 = p_ref[:width, 5 * width : 5 * width + 1]
    b2 = p_ref[:width, 5 * width + 1 : 5 * width + 2]
    b3 = p_ref[:width, 5 * width + 2 : 5 * width + 3]
    for chunk in range(row_count // rows):
        first = chunk * rows
        h = b1
        for a in range(3):
            x = jnp.concatenate([x_ref[0, :, first + row + a, :] for row in range(rows)], axis=1)
            h = h + jnp.dot(w1[a], x, preferred_element_type=jnp.float32)
        h = jax.nn.silu(h).astype(jnp.bfloat16)
        h = jnp.dot(w2, h, preferred_element_type=jnp.float32) + b2
        h = jax.nn.silu(h).astype(jnp.bfloat16)
        h = jnp.dot(w3, h, preferred_element_type=jnp.float32) + b3
        h = jax.nn.silu(h).astype(jnp.bfloat16)
        q = jnp.dot(wl, h, preferred_element_type=jnp.float32)
        for row in range(rows):
            q_ref[0, :, first + row, :] = q[:, row * cols : (row + 1) * cols]


def score_net(window, w_first, b_first, w_second, b_second, w_third, b_third, w_last, tie):
    slice_count = window.shape[0] - 4
    row_count = window.shape[2]
    col_count = window.shape[3]
    width = w_first.shape[-1]
    stacked = jnp.concatenate(
        [window[offset : offset + slice_count] for offset in range(5)], axis=1
    )
    framed = jnp.pad(stacked, ((0, 0), (0, 0), (1, 1), (1, 1)))
    shifted = jnp.concatenate(
        [framed[:, :, :, shift_y : shift_y + col_count] for shift_y in range(3)], axis=1
    )
    taps_in = shifted.shape[1]
    wl = w_last.reshape(-1, width)
    outs = wl.shape[0]
    pad_to = lambda m: jnp.pad(m.astype(jnp.float32), ((0, 0), (0, width - m.shape[1])))
    top = jnp.concatenate(
        [pad_to(w_first[shift_x].reshape(taps_in, width).T) for shift_x in range(3)]
        + [
            pad_to(w_second.T),
            pad_to(w_third.T),
            pad_to(jnp.stack([b_first, b_second, b_third], axis=1)),
        ],
        axis=1,
    )
    bottom = jnp.pad(wl.astype(jnp.float32), ((0, 24 - outs), (0, 5 * width)))
    packed = jnp.concatenate([top, bottom], axis=0)
    shifted, packed, tie = lax.optimization_barrier((shifted, packed, tie))
    q = pl.pallas_call(
        net_kernel,
        grid=(slice_count,),
        in_specs=[
            pl.BlockSpec((1,) + shifted.shape[1:], lambda z: (z, 0, 0, 0)),
            pl.BlockSpec(packed.shape, lambda z: (0, 0)),
        ],
        out_specs=pl.BlockSpec((1, outs, row_count, col_count), lambda z: (z, 0, 0, 0)),
        out_shape=jax.ShapeDtypeStruct((slice_count, outs, row_count, col_count), jnp.float32),
    )(shifted, packed)
    q = jnp.pad(q, ((0, 0), (0, 0), (1, 1), (1, 1)))
    score_field = jnp.zeros((slice_count, 2, row_count, col_count), jnp.float32)
    for shift_x in range(3):
        for shift_y in range(3):
            tap = (shift_x * 3 + shift_y) * 2
            score_field = score_field + q[
                :, tap : tap + 2, shift_x : shift_x + row_count, shift_y : shift_y + col_count
            ]
    return score_field, tie


def slab_slices(image):
    return lax.all_gather(image, "coil", axis=0, tiled=True)


def on_device(
    image,
    noise,
    sens,
    measured,
    mask,
    w_first,
    b_first,
    w_second,
    b_second,
    w_third,
    b_third,
    w_last,
):
    window = with_halo(image.astype(jnp.bfloat16), ((("slab", "coil"), 0),), 2)
    groups = lax.axis_size("coil")
    depth, parts, rows, lines = image.shape
    copies = jnp.broadcast_to(image[:, :, :, None], (depth, parts, rows, groups, lines))
    copies = copies.reshape(depth, parts, rows * groups, lines)
    planes_in = lax.all_to_all(copies, ("slab", "coil"), split_axis=2, concat_axis=0, tiled=True)
    score_field, planes_in = score_net(
        window, w_first, b_first, w_second, b_second, w_third, b_third, w_last, planes_in
    )
    planes = jnp.transpose(planes_in, (1, 2, 3, 0))
    partial_sum = coil_adjoint(planes, sens, measured, mask)
    by_depth = jnp.transpose(partial_sum, (3, 0, 1, 2))
    by_device = lax.all_to_all(by_depth, ("slab", "coil"), split_axis=0, concat_axis=2, tiled=True)
    by_device = by_device.astype(jnp.float32).reshape(depth, parts, rows, groups, lines)
    gradient = jnp.sum(by_device, axis=3)
    return image + STEP_SIZE * (score_field - gradient) + noise


def solution(mesh):
    in_specs = (
        P(("slab", "coil"), None, None, None),
        P(("slab", "coil"), None, None, None),
        P("coil", None, "slab", None, None),
        P("coil", None, "slab", None, None),
        P(),
        P(),
        P(),
        P(),
        P(),
        P(),
        P(),
        P(),
    )
    out_specs = P(("slab", "coil"), None, None, None)
    return jax.shard_map(
        on_device, mesh=mesh, in_specs=in_specs, out_specs=out_specs, check_vma=False
    )
```

```python
import ml_dtypes
import numpy as np
import jax
import jax.numpy as jnp
from jax import lax
from jax.sharding import PartitionSpec as P
from jax.experimental import pallas as pl
from jax.experimental.pallas import tpu as pltpu

STEP_SIZE = 0.5


def with_halo(shard, sides, width):
    for axis, dim in sides:
        devices, length = (lax.axis_size(axis), shard.shape[dim])
        up = [(i, (i + 1) % devices) for i in range(devices - 1)]
        down = [(j, i) for i, j in up]
        last = lax.slice_in_dim(shard, length - width, length, axis=dim)
        first = lax.slice_in_dim(shard, 0, width, axis=dim)
        before = lax.ppermute(last, axis, up)
        after = lax.ppermute(first, axis, down)
        shard = jnp.concatenate([before, shard, after], axis=dim)
    return shard


def dft_tables(length):
    line_index = np.arange(length, dtype=np.int64)
    phase_turns = line_index[:, None] * line_index[None, :] % length
    phase_angle = phase_turns.astype(np.float32) * np.float32(2.0 * np.pi / length)
    norm_scale = np.float32(1.0) / np.sqrt(np.float32(length))
    return (
        (np.cos(phase_angle) * norm_scale).astype(ml_dtypes.bfloat16),
        (np.sin(phase_angle) * norm_scale).astype(ml_dtypes.bfloat16),
    )


def along_y(values, table):
    return jnp.einsum("...yz,yk->...kz", values, table, preferred_element_type=jnp.float32)


def along_z(values, table):
    return jnp.einsum("...z,zk->...k", values, table, preferred_element_type=jnp.float32)


def spectrum(real_part, imag_part, cos_y, sin_y, cos_z, sin_z, forward):
    sign = 1.0 if forward else -1.0
    out_real = (along_y(real_part, cos_y) + sign * along_y(imag_part, sin_y)).astype(jnp.bfloat16)
    out_imag = (along_y(imag_part, cos_y) - sign * along_y(real_part, sin_y)).astype(jnp.bfloat16)
    last_real = along_z(out_real, cos_z) + sign * along_z(out_imag, sin_z)
    last_imag = along_z(out_imag, cos_z) - sign * along_z(out_real, sin_z)
    return (last_real, last_imag)


def adjoint_kernel(planes_ref, sens_ref, meas_ref, mask_ref, ty_ref, tz_ref, out_ref, acc_ref):
    ny = planes_ref.shape[1]
    nz = planes_ref.shape[2]

    @pl.when(pl.program_id(0) == 0)
    def _():
        acc_ref[...] = jnp.zeros_like(acc_ref)

    ty = ty_ref[...]
    tz = tz_ref[...]
    sens_real = sens_ref[0].astype(jnp.float32)
    sens_imag = sens_ref[1].astype(jnp.float32)
    image_real = planes_ref[0]
    image_imag = planes_ref[1]
    coil_real = (sens_real * image_real - sens_imag * image_imag).astype(jnp.bfloat16)
    coil_imag = (sens_real * image_imag + sens_imag * image_real).astype(jnp.bfloat16)
    half = jnp.dot(ty, jnp.concatenate([coil_real, coil_imag], axis=1), preferred_element_type=jnp.float32)
    half_real = (half[:ny, :nz] + half[ny:, nz:]).astype(jnp.bfloat16)
    half_imag = (half[:ny, nz:] - half[ny:, :nz]).astype(jnp.bfloat16)
    full = jnp.dot(jnp.concatenate([half_real, half_imag], axis=0), tz, preferred_element_type=jnp.float32)
    spec_real = full[:ny, :nz] + full[ny:, nz:]
    spec_imag = full[ny:, :nz] - full[:ny, nz:]
    sampled = mask_ref[...].astype(jnp.float32)
    miss_real = (sampled * (spec_real - meas_ref[0].astype(jnp.float32))).astype(jnp.bfloat16)
    miss_imag = (sampled * (spec_imag - meas_ref[1].astype(jnp.float32))).astype(jnp.bfloat16)
    half = jnp.dot(ty, jnp.concatenate([miss_real, miss_imag], axis=1), preferred_element_type=jnp.float32)
    back_real = (half[:ny, :nz] - half[ny:, nz:]).astype(jnp.bfloat16)
    back_imag = (half[:ny, nz:] + half[ny:, :nz]).astype(jnp.bfloat16)
    full = jnp.dot(jnp.concatenate([back_real, back_imag], axis=0), tz, preferred_element_type=jnp.float32)
    grad_real = full[:ny, :nz] - full[ny:, nz:]
    grad_imag = full[ny:, :nz] + full[:ny, nz:]
    acc_ref[0] += sens_real * grad_real + sens_imag * grad_imag
    acc_ref[1] += sens_real * grad_imag - sens_imag * grad_real

    @pl.when(pl.program_id(0) == pl.num_programs(0) - 1)
    def _():
        out_ref[...] = acc_ref[...].astype(out_ref.dtype)


def coil_adjoint(planes, sens, measured, mask):
    ny = planes.shape[2]
    nz = planes.shape[3]
    cos_y, sin_y = dft_tables(ny)
    cos_z, sin_z = dft_tables(nz)
    ty = jnp.asarray(np.concatenate([cos_y, sin_y], axis=0))
    tz = jnp.asarray(np.concatenate([cos_z, sin_z], axis=1))
    coils = sens.shape[0]
    return pl.pallas_call(
        adjoint_kernel,
        grid=(coils,),
        in_specs=[
            pl.BlockSpec((2, None, ny, nz), lambda c: (0, 0, 0, 0)),
            pl.BlockSpec((None, 2, None, ny, nz), lambda c: (c, 0, 0, 0, 0)),
            pl.BlockSpec((None, 2, None, ny, nz), lambda c: (c, 0, 0, 0, 0)),
            pl.BlockSpec((ny, nz), lambda c: (0, 0)),
            pl.BlockSpec((2 * ny, ny), lambda c: (0, 0)),
            pl.BlockSpec((nz, 2 * nz), lambda c: (0, 0)),
        ],
        out_specs=pl.BlockSpec((2, None, ny, nz), lambda c: (0, 0, 0, 0)),
        out_shape=jax.ShapeDtypeStruct(planes.shape, jnp.bfloat16),
        scratch_shapes=[pltpu.VMEM((2, ny, nz), jnp.float32)],
    )(planes, sens, measured, mask, ty, tz)


def net_kernel(x_ref, p_ref, q_ref):
    width = p_ref.shape[0] - 24
    taps_in = x_ref.shape[1]
    row_count = q_ref.shape[2]
    cols = q_ref.shape[3]
    outs = q_ref.shape[1]
    rows = 4
    w1 = [p_ref[:width, a * width : a * width + taps_in].astype(jnp.bfloat16) for a in range(3)]
    w2 = p_ref[:width, 3 * width : 4 * width].astype(jnp.bfloat16)
    w3 = p_ref[:width, 4 * width : 5 * width].astype(jnp.bfloat16)
    wl = p_ref[width : width + outs, 0:width].astype(jnp.bfloat16)
    b1 = p_ref[:width, 5 * width : 5 * width + 1]
    b2 = p_ref[:width, 5 * width + 1 : 5 * width + 2]
    b3 = p_ref[:width, 5 * width + 2 : 5 * width + 3]
    for chunk in range(row_count // rows):
        first = chunk * rows
        h = b1
        for a in range(3):
            x = jnp.concatenate([x_ref[0, :, first + row + a, :] for row in range(rows)], axis=1)
            h = h + jnp.dot(w1[a], x, preferred_element_type=jnp.float32)
        h = jax.nn.silu(h).astype(jnp.bfloat16)
        h = jnp.dot(w2, h, preferred_element_type=jnp.float32) + b2
        h = jax.nn.silu(h).astype(jnp.bfloat16)
        h = jnp.dot(w3, h, preferred_element_type=jnp.float32) + b3
        h = jax.nn.silu(h).astype(jnp.bfloat16)
        q = jnp.dot(wl, h, preferred_element_type=jnp.float32)
        for row in range(rows):
            q_ref[0, :, first + row, :] = q[:, row * cols : (row + 1) * cols]


def score_net(window, w_first, b_first, w_second, b_second, w_third, b_third, w_last, tie):
    slice_count = window.shape[0] - 4
    row_count = window.shape[2]
    col_count = window.shape[3]
    width = w_first.shape[-1]
    stacked = jnp.concatenate(
        [window[offset : offset + slice_count] for offset in range(5)], axis=1
    )
    framed = jnp.pad(stacked, ((0, 0), (0, 0), (1, 1), (1, 1)))
    shifted = jnp.concatenate(
        [framed[:, :, :, shift_y : shift_y + col_count] for shift_y in range(3)], axis=1
    )
    taps_in = shifted.shape[1]
    wl = w_last.reshape(-1, width)
    outs = wl.shape[0]
    pad_to = lambda m: jnp.pad(m.astype(jnp.float32), ((0, 0), (0, width - m.shape[1])))
    top = jnp.concatenate(
        [pad_to(w_first[shift_x].reshape(taps_in, width).T) for shift_x in range(3)]
        + [
            pad_to(w_second.T),
            pad_to(w_third.T),
            pad_to(jnp.stack([b_first, b_second, b_third], axis=1)),
        ],
        axis=1,
    )
    bottom = jnp.pad(wl.astype(jnp.float32), ((0, 24 - outs), (0, 5 * width)))
    packed = jnp.concatenate([top, bottom], axis=0)
    shifted, packed, tie = lax.optimization_barrier((shifted, packed, tie))
    q = pl.pallas_call(
        net_kernel,
        grid=(slice_count,),
        in_specs=[
            pl.BlockSpec((1,) + shifted.shape[1:], lambda z: (z, 0, 0, 0)),
            pl.BlockSpec(packed.shape, lambda z: (0, 0)),
        ],
        out_specs=pl.BlockSpec((1, outs, row_count, col_count), lambda z: (z, 0, 0, 0)),
        out_shape=jax.ShapeDtypeStruct((slice_count, outs, row_count, col_count), jnp.float32),
    )(shifted, packed)
    q = jnp.pad(q, ((0, 0), (0, 0), (1, 1), (1, 1)))
    score_field = jnp.zeros((slice_count, 2, row_count, col_count), jnp.float32)
    for shift_x in range(3):
        for shift_y in range(3):
            tap = (shift_x * 3 + shift_y) * 2
            score_field = score_field + q[
                :, tap : tap + 2, shift_x : shift_x + row_count, shift_y : shift_y + col_count
            ]
    return score_field, tie


def slab_slices(image):
    return lax.all_gather(image, "coil", axis=0, tiled=True)


def on_device(
    image,
    noise,
    sens,
    measured,
    mask,
    w_first,
    b_first,
    w_second,
    b_second,
    w_third,
    b_third,
    w_last,
):
    window = with_halo(image.astype(jnp.bfloat16), ((("slab", "coil"), 0),), 2)
    groups = lax.axis_size("coil")
    depth, parts, rows, lines = image.shape
    copies = jnp.broadcast_to(image[:, :, :, None], (depth, parts, rows, groups, lines))
    copies = copies.reshape(depth, parts, rows * groups, lines)
    planes_in = lax.all_to_all(copies, ("slab", "coil"), split_axis=2, concat_axis=0, tiled=True)
    score_field, planes_in = score_net(
        window, w_first, b_first, w_second, b_second, w_third, b_third, w_last, planes_in
    )
    planes = jnp.transpose(planes_in, (1, 2, 3, 0))
    partial_sum = coil_adjoint(planes, sens, measured, mask)
    by_depth = jnp.transpose(partial_sum, (3, 0, 1, 2))
    by_device = lax.all_to_all(by_depth, ("slab", "coil"), split_axis=0, concat_axis=2, tiled=True)
    by_device = by_device.astype(jnp.float32).reshape(depth, parts, rows, groups, lines)
    gradient = jnp.sum(by_device, axis=3)
    return image + STEP_SIZE * (score_field - gradient) + noise


def solution(mesh):
    in_specs = (
        P(("slab", "coil"), None, None, None),
        P(("slab", "coil"), None, None, None),
        P("coil", None, "slab", None, None),
        P("coil", None, "slab", None, None),
        P(),
        P(),
        P(),
        P(),
        P(),
        P(),
        P(),
        P(),
    )
    out_specs = P(("slab", "coil"), None, None, None)
    return jax.shard_map(
        on_device, mesh=mesh, in_specs=in_specs, out_specs=out_specs, check_vma=False
    )
```

```python
import ml_dtypes
import numpy as np
import jax
import jax.numpy as jnp
from jax import lax
from jax.sharding import PartitionSpec as P
from jax.experimental import pallas as pl
from jax.experimental.pallas import tpu as pltpu

STEP_SIZE = 0.5


def with_halo(shard, sides, width):
    for axis, dim in sides:
        devices, length = (lax.axis_size(axis), shard.shape[dim])
        up = [(i, (i + 1) % devices) for i in range(devices - 1)]
        down = [(j, i) for i, j in up]
        last = lax.slice_in_dim(shard, length - width, length, axis=dim)
        first = lax.slice_in_dim(shard, 0, width, axis=dim)
        before = lax.ppermute(last, axis, up)
        after = lax.ppermute(first, axis, down)
        shard = jnp.concatenate([before, shard, after], axis=dim)
    return shard


def dft_tables(length):
    line_index = np.arange(length, dtype=np.int64)
    phase_turns = line_index[:, None] * line_index[None, :] % length
    phase_angle = phase_turns.astype(np.float32) * np.float32(2.0 * np.pi / length)
    norm_scale = np.float32(1.0) / np.sqrt(np.float32(length))
    return (
        (np.cos(phase_angle) * norm_scale).astype(ml_dtypes.bfloat16),
        (np.sin(phase_angle) * norm_scale).astype(ml_dtypes.bfloat16),
    )


def along_y(values, table):
    return jnp.einsum("...yz,yk->...kz", values, table, preferred_element_type=jnp.float32)


def along_z(values, table):
    return jnp.einsum("...z,zk->...k", values, table, preferred_element_type=jnp.float32)


def spectrum(real_part, imag_part, cos_y, sin_y, cos_z, sin_z, forward):
    sign = 1.0 if forward else -1.0
    out_real = (along_y(real_part, cos_y) + sign * along_y(imag_part, sin_y)).astype(jnp.bfloat16)
    out_imag = (along_y(imag_part, cos_y) - sign * along_y(real_part, sin_y)).astype(jnp.bfloat16)
    last_real = along_z(out_real, cos_z) + sign * along_z(out_imag, sin_z)
    last_imag = along_z(out_imag, cos_z) - sign * along_z(out_real, sin_z)
    return (last_real, last_imag)


def adjoint_kernel(planes_ref, sens_ref, meas_ref, mask_ref, ty_ref, tz_ref, out_ref, acc_ref):
    ny = planes_ref.shape[1]
    nz = planes_ref.shape[2]

    @pl.when(pl.program_id(0) == 0)
    def _():
        acc_ref[...] = jnp.zeros_like(acc_ref)

    ty = ty_ref[...]
    tz = tz_ref[...]
    sens_real = sens_ref[0].astype(jnp.float32)
    sens_imag = sens_ref[1].astype(jnp.float32)
    image_real = planes_ref[0]
    image_imag = planes_ref[1]
    coil_real = (sens_real * image_real - sens_imag * image_imag).astype(jnp.bfloat16)
    coil_imag = (sens_real * image_imag + sens_imag * image_real).astype(jnp.bfloat16)
    of_real = jnp.dot(ty, coil_real, preferred_element_type=jnp.float32)
    of_imag = jnp.dot(ty, coil_imag, preferred_element_type=jnp.float32)
    half_real = (of_real[:ny] + of_imag[ny:]).astype(jnp.bfloat16)
    half_imag = (of_imag[:ny] - of_real[ny:]).astype(jnp.bfloat16)
    of_real = jnp.dot(half_real, tz, preferred_element_type=jnp.float32)
    of_imag = jnp.dot(half_imag, tz, preferred_element_type=jnp.float32)
    spec_real = of_real[:, :nz] + of_imag[:, nz:]
    spec_imag = of_imag[:, :nz] - of_real[:, nz:]
    sampled = mask_ref[...].astype(jnp.float32)
    miss_real = (sampled * (spec_real - meas_ref[0].astype(jnp.float32))).astype(jnp.bfloat16)
    miss_imag = (sampled * (spec_imag - meas_ref[1].astype(jnp.float32))).astype(jnp.bfloat16)
    of_real = jnp.dot(ty, miss_real, preferred_element_type=jnp.float32)
    of_imag = jnp.dot(ty, miss_imag, preferred_element_type=jnp.float32)
    back_real = (of_real[:ny] - of_imag[ny:]).astype(jnp.bfloat16)
    back_imag = (of_imag[:ny] + of_real[ny:]).astype(jnp.bfloat16)
    of_real = jnp.dot(back_real, tz, preferred_element_type=jnp.float32)
    of_imag = jnp.dot(back_imag, tz, preferred_element_type=jnp.float32)
    grad_real = of_real[:, :nz] - of_imag[:, nz:]
    grad_imag = of_imag[:, :nz] + of_real[:, nz:]
    acc_ref[0] += sens_real * grad_real + sens_imag * grad_imag
    acc_ref[1] += sens_real * grad_imag - sens_imag * grad_real

    @pl.when(pl.program_id(0) == pl.num_programs(0) - 1)
    def _():
        out_ref[...] = acc_ref[...].astype(out_ref.dtype)


def coil_adjoint(planes, sens, measured, mask):
    ny = planes.shape[2]
    nz = planes.shape[3]
    cos_y, sin_y = dft_tables(ny)
    cos_z, sin_z = dft_tables(nz)
    ty = jnp.asarray(np.concatenate([cos_y, sin_y], axis=0))
    tz = jnp.asarray(np.concatenate([cos_z, sin_z], axis=1))
    coils = sens.shape[0]
    return pl.pallas_call(
        adjoint_kernel,
        grid=(coils,),
        in_specs=[
            pl.BlockSpec((2, None, ny, nz), lambda c: (0, 0, 0, 0)),
            pl.BlockSpec((None, 2, None, ny, nz), lambda c: (c, 0, 0, 0, 0)),
            pl.BlockSpec((None, 2, None, ny, nz), lambda c: (c, 0, 0, 0, 0)),
            pl.BlockSpec((ny, nz), lambda c: (0, 0)),
            pl.BlockSpec((2 * ny, ny), lambda c: (0, 0)),
            pl.BlockSpec((nz, 2 * nz), lambda c: (0, 0)),
        ],
        out_specs=pl.BlockSpec((2, None, ny, nz), lambda c: (0, 0, 0, 0)),
        out_shape=jax.ShapeDtypeStruct(planes.shape, jnp.bfloat16),
        scratch_shapes=[pltpu.VMEM((2, ny, nz), jnp.float32)],
    )(planes, sens, measured, mask, ty, tz)


def net_kernel(x_ref, p_ref, q_ref):
    width = p_ref.shape[0] - 24
    taps_in = x_ref.shape[1]
    row_count = q_ref.shape[2]
    cols = q_ref.shape[3]
    outs = q_ref.shape[1]
    rows = 8
    w1 = [p_ref[:width, a * width : a * width + taps_in].astype(jnp.bfloat16) for a in range(3)]
    w2 = p_ref[:width, 3 * width : 4 * width].astype(jnp.bfloat16)
    w3 = p_ref[:width, 4 * width : 5 * width].astype(jnp.bfloat16)
    wl = p_ref[width : width + outs, 0:width].astype(jnp.bfloat16)
    b1 = p_ref[:width, 5 * width : 5 * width + 1]
    b2 = p_ref[:width, 5 * width + 1 : 5 * width + 2]
    b3 = p_ref[:width, 5 * width + 2 : 5 * width + 3]
    for chunk in range(row_count // rows):
        first = chunk * rows
        h = b1
        for a in range(3):
            x = jnp.concatenate([x_ref[0, :, first + row + a, :] for row in range(rows)], axis=1)
            h = h + jnp.dot(w1[a], x, preferred_element_type=jnp.float32)
        h = jax.nn.silu(h).astype(jnp.bfloat16)
        h = jnp.dot(w2, h, preferred_element_type=jnp.float32) + b2
        h = jax.nn.silu(h).astype(jnp.bfloat16)
        h = jnp.dot(w3, h, preferred_element_type=jnp.float32) + b3
        h = jax.nn.silu(h).astype(jnp.bfloat16)
        q = jnp.dot(wl, h, preferred_element_type=jnp.float32)
        for row in range(rows):
            q_ref[0, :, first + row, :] = q[:, row * cols : (row + 1) * cols]


def score_net(window, w_first, b_first, w_second, b_second, w_third, b_third, w_last, tie):
    slice_count = window.shape[0] - 4
    row_count = window.shape[2]
    col_count = window.shape[3]
    width = w_first.shape[-1]
    stacked = jnp.concatenate(
        [window[offset : offset + slice_count] for offset in range(5)], axis=1
    )
    framed = jnp.pad(stacked, ((0, 0), (0, 0), (1, 1), (1, 1)))
    shifted = jnp.concatenate(
        [framed[:, :, :, shift_y : shift_y + col_count] for shift_y in range(3)], axis=1
    )
    taps_in = shifted.shape[1]
    wl = w_last.reshape(-1, width)
    outs = wl.shape[0]
    pad_to = lambda m: jnp.pad(m.astype(jnp.float32), ((0, 0), (0, width - m.shape[1])))
    top = jnp.concatenate(
        [pad_to(w_first[shift_x].reshape(taps_in, width).T) for shift_x in range(3)]
        + [
            pad_to(w_second.T),
            pad_to(w_third.T),
            pad_to(jnp.stack([b_first, b_second, b_third], axis=1)),
        ],
        axis=1,
    )
    bottom = jnp.pad(wl.astype(jnp.float32), ((0, 24 - outs), (0, 5 * width)))
    packed = jnp.concatenate([top, bottom], axis=0)
    shifted, packed, tie = lax.optimization_barrier((shifted, packed, tie))
    q = pl.pallas_call(
        net_kernel,
        grid=(slice_count,),
        in_specs=[
            pl.BlockSpec((1,) + shifted.shape[1:], lambda z: (z, 0, 0, 0)),
            pl.BlockSpec(packed.shape, lambda z: (0, 0)),
        ],
        out_specs=pl.BlockSpec((1, outs, row_count, col_count), lambda z: (z, 0, 0, 0)),
        out_shape=jax.ShapeDtypeStruct((slice_count, outs, row_count, col_count), jnp.float32),
    )(shifted, packed)
    q = jnp.pad(q, ((0, 0), (0, 0), (1, 1), (1, 1)))
    score_field = jnp.zeros((slice_count, 2, row_count, col_count), jnp.float32)
    for shift_x in range(3):
        for shift_y in range(3):
            tap = (shift_x * 3 + shift_y) * 2
            score_field = score_field + q[
                :, tap : tap + 2, shift_x : shift_x + row_count, shift_y : shift_y + col_count
            ]
    return score_field, tie


def slab_slices(image):
    return lax.all_gather(image, "coil", axis=0, tiled=True)


def on_device(
    image,
    noise,
    sens,
    measured,
    mask,
    w_first,
    b_first,
    w_second,
    b_second,
    w_third,
    b_third,
    w_last,
):
    window = with_halo(image.astype(jnp.bfloat16), ((("slab", "coil"), 0),), 2)
    groups = lax.axis_size("coil")
    depth, parts, rows, lines = image.shape
    copies = jnp.broadcast_to(image[:, :, :, None], (depth, parts, rows, groups, lines))
    copies = copies.reshape(depth, parts, rows * groups, lines)
    planes_in = lax.all_to_all(copies, ("slab", "coil"), split_axis=2, concat_axis=0, tiled=True)
    score_field, planes_in = score_net(
        window, w_first, b_first, w_second, b_second, w_third, b_third, w_last, planes_in
    )
    planes = jnp.transpose(planes_in, (1, 2, 3, 0))
    partial_sum = coil_adjoint(planes, sens, measured, mask)
    by_depth = jnp.transpose(partial_sum, (3, 0, 1, 2))
    by_device = lax.all_to_all(by_depth, ("slab", "coil"), split_axis=0, concat_axis=2, tiled=True)
    by_device = by_device.astype(jnp.float32).reshape(depth, parts, rows, groups, lines)
    gradient = jnp.sum(by_device, axis=3)
    return image + STEP_SIZE * (score_field - gradient) + noise


def solution(mesh):
    in_specs = (
        P(("slab", "coil"), None, None, None),
        P(("slab", "coil"), None, None, None),
        P("coil", None, "slab", None, None),
        P("coil", None, "slab", None, None),
        P(),
        P(),
        P(),
        P(),
        P(),
        P(),
        P(),
        P(),
    )
    out_specs = P(("slab", "coil"), None, None, None)
    return jax.shard_map(
        on_device, mesh=mesh, in_specs=in_specs, out_specs=out_specs, check_vma=False
    )
```
